128 devices in a mesh: section: 2 (over core), dp: 16 (over z, x), mp: 4 (over y).
Axes of the slice: x: 4, y: 4, z: 4, core: 2. Of those that a mesh axis runs over, the one named last changes fastest.
Arguments:
- states: bfloat16 [2, 2048, 4096], P('section', 'dp'), may hold values from -6 to 6
- gains: float32 [2, 4096], P('section'), may hold values from 0.25 to 1.75
- proj_a: bfloat16 [2, 4096, 4096], P('section', None, 'mp'), may hold values from -0.03125 to 0.03125
- proj_b: bfloat16 [2, 4096, 4096], P('section', None, 'mp'), may hold values from -0.09375 to 0.09375
- cotangent: bfloat16 [2048, 4096], P('dp'), may hold values from -12 to 12
- src_len: int32 [16, 16], replicated, may hold values from 1 to 16, 128 in all within a row
- tgt_len: int32 [16, 16], replicated, may hold values from 1 to 16, 128 in all within a row
- dest: int32 [16, 16], replicated, may hold values from 0 to 255, as said below
Outputs:
- grad_states: bfloat16 [2, 2048, 4096], P('section', 'dp')
- grad_a: float32 [2, 4096, 4096], P('section', 'dp', 'mp')
- grad_b: float32 [2, 4096, 4096], P('section', 'dp', 'mp')
The draws below stay inside these ranges and needn't reach their ends.
Inputs may be any that keep to these rules, and one draw needn't show every extreme that they name: `src_len`: each row sums to 128. `tgt_len`: each row sums to 128. `dest`: every value from 0 to 255 appears once; each row holds exactly 1 values in each range d * 16 to (d + 1) * 16 - 1.
All inputs are finite; a program needn't handle non-finite values.
Results may differ from the reference program's by a relative error of at most 0.014.
Values may be sent and summed in bfloat16 or wider, within the bound.
No kernel may reach another device: no remote copies, remote signals or barrier semaphores. Data moves between devices by JAX's collectives and lax.ppermute only.
A program may use at most 128 MiB of HBM per device.

```python
import math
import jax
import jax.numpy as jnp
import numpy as np
from jax import lax

D = 4096
HEAD_DIM = 64
TOK_DEV = 128
SEQ_DEV = 16
INNER = 4096
MAXLEN = 16
ROWS = 2048
N_DP = 16


def draw_dest(key, part):
    group = SEQ_DEV // N_DP
    send_key, slot_key = jax.random.split(jax.random.fold_in(key, 17))
    send_perm = jax.vmap(lambda one: jax.random.permutation(one, SEQ_DEV))(jax.random.split(send_key, N_DP)).astype(jnp.int32)
    slot_perm = jax.vmap(lambda one: jax.random.permutation(one, SEQ_DEV))(jax.random.split(slot_key, N_DP)).astype(jnp.int32)
    source = jnp.arange(N_DP, dtype=jnp.int32)[:, None]
    place = jnp.arange(SEQ_DEV, dtype=jnp.int32)[None, :]
    target = place // group
    slot = slot_perm[target, source * group + place % group]
    value = (target * SEQ_DEV + slot).astype(jnp.int32)
    sources = jnp.broadcast_to(source, (N_DP, SEQ_DEV))
    return jnp.zeros((N_DP, SEQ_DEV), jnp.int32).at[sources, send_perm].set(value)


def strengthened(drawn, own_key, source, target, blocks, factor):
    def block_of(position):
        return (jnp.arange(drawn.shape[position]) // (drawn.shape[position] // blocks)).reshape((-1,) + (1,) * (drawn.ndim - 1 - position))

    near = jax.random.permutation(own_key, blocks)[block_of(target)]
    second = (block_of(target) + blocks // 2) % blocks
    return jnp.where((block_of(source) == near) | (block_of(source) == second), factor * drawn, drawn)


def shard_levels(key, extent, cuts, least, high):
    loudness, own = 1.0, jax.random.fold_in(key, 6)
    for axis_at, shards_of in cuts:
        draws = jnp.exp(jax.random.uniform(jax.random.fold_in(own, axis_at), (shards_of,), jnp.float32, least / len(cuts), high / len(cuts)))
        loudness = loudness * jnp.repeat(draws, extent[axis_at] // shards_of).reshape([-1 if axis == axis_at else 1 for axis in range(len(extent))])
    return loudness


def split_up(number_of, total, limit, slope):
    weights = [(1 << 20) // math.isqrt(grade ** slope) + 1 for grade in range(2, number_of + 1)]
    spare, given = total - limit - (number_of - 1), [1] * (number_of - 1)
    while spare > 0:
        free = [i for i in range(number_of - 1) if given[i] < limit]
        pool, budget = sum([weights[i] for i in free]), spare
        for i in free:
            more = min(limit - given[i], max(1, budget * weights[i] // pool), spare)
            given[i] = given[i] + more
            spare = spare - more
    return np.array([limit] + given)


def uneven_parts(key, count, total, reach, lean):
    if count == 2:
        one = jax.random.randint(key, (), max(1, total - reach), min(reach, total - 1) + 1)
        return jnp.stack([one, total - one])
    sizes = jnp.asarray(split_up(count, total, reach, lean), jnp.int32)
    pairs = (count - 1) // 2
    donor, taker = sizes[1:1 + 2 * pairs:2], sizes[2:2 + 2 * pairs:2]
    room = jnp.minimum(donor - 1, reach - taker)
    passed = jax.random.randint(jax.random.fold_in(key, 1), (pairs,), 0, 1 << 20) % (room + 1)
    sizes = sizes.at[1:1 + 2 * pairs:2].set(donor - passed).at[2:2 + 2 * pairs:2].set(taker + passed)
    return sizes[jax.random.permutation(jax.random.fold_in(key, 2), count)]


def gaussian(stream_key, extent, spread, reach, shards=(), held_as=jnp.bfloat16):
    array = jax.random.normal(stream_key, extent, jnp.float32) * spread
    if len(shards) > 0:
        array = shard_levels(stream_key, extent, shards, -0.22, 0.18) * array
    return jnp.clip(array, min=-reach, max=reach).astype(held_as)


def heavy_noise(key, shape, deviation, limit, shards, heavy, kind=jnp.bfloat16):
    drawn = deviation * jax.random.normal(key, shape, jnp.float32)
    if shards:
        drawn = drawn * shard_levels(key, shape, shards, -0.22, 0.18)
    return jnp.clip(strengthened(drawn, jax.random.fold_in(key, 3), *heavy), -limit, limit).astype(kind)


def setup_inputs(seed: int = 0) -> dict:
    key_of = jax.random.split(jax.random.key(seed), 9)
    states = heavy_noise(key_of[0], (2, ROWS, D), 1.0, 6.0, ((0, 2), (1, 16)), (1, 2, 16, 2.0))
    gains = jnp.clip(1.0 + 0.15 * jax.random.normal(key_of[1], (2, D), jnp.float32), 0.25, 1.75)
    proj_a = gaussian(key_of[2], (2, D, INNER), (8 * D) ** -0.5, 0.03125, ((0, 2), (2, 4)))
    proj_b = gaussian(key_of[3], (2, D, INNER), D ** -0.5, 0.09375, ((0, 2), (2, 4)))
    cotangent = gaussian(key_of[4], (ROWS, D), 2.0, 12.0, ((0, 16),))
    src_len = jax.vmap(lambda own: uneven_parts(own, SEQ_DEV, TOK_DEV, MAXLEN, 2))(jax.random.split(key_of[5], N_DP)).reshape((N_DP, SEQ_DEV)).astype(jnp.int32)
    tgt_len = jax.vmap(lambda own: uneven_parts(own, SEQ_DEV, TOK_DEV, MAXLEN, 2))(jax.random.split(key_of[6], N_DP)).reshape((N_DP, SEQ_DEV)).astype(jnp.int32)
    dest = draw_dest(jax.random.fold_in(key_of[8], 71), 0)
    return {"states": states, "gains": gains, "proj_a": proj_a, "proj_b": proj_b, "cotangent": cotangent, "src_len": src_len, "tgt_len": tgt_len, "dest": dest}


EPS = 1e-06

def rms_forward(states_row, gain):
    xf = states_row.astype(jnp.float32)
    scale = lax.rsqrt(lax.optimization_barrier(jnp.mean(xf * xf, axis=-1, keepdims=True)) + EPS)
    return (xf, scale, (xf * scale * gain).astype(jnp.bfloat16))

def rms_backward(xf, scale, gain, dnorm):
    upper = gain * dnorm
    inner = lax.optimization_barrier(jnp.mean(xf * upper, axis=-1, keepdims=True))
    return (scale * upper - xf * scale * scale * scale * inner).astype(jnp.bfloat16)

def starts_of(lengths):
    count = lengths.shape[0]
    local = (jnp.cumsum(lengths, axis=1) - lengths).astype(jnp.int32)
    base = (jnp.arange(count, dtype=jnp.int32) * TOK_DEV)[:, None]
    return ((base + local).reshape(-1).astype(jnp.int32), lengths.reshape(-1).astype(jnp.int32))

def pack(rows, starts, lengths):
    steps = jnp.arange(MAXLEN, dtype=jnp.int32)
    index = starts[:, None] + steps[None, :]
    valid = steps[None, :] < lengths[:, None]
    picked = rows[jnp.minimum(index, rows.shape[0] - 1)]
    return jnp.where(valid[:, :, None], picked, jnp.zeros((), rows.dtype))

def unpack(padded, lengths):
    count, per = lengths.shape
    local = (jnp.cumsum(lengths, axis=1) - lengths).astype(jnp.int32)
    ends = local + lengths
    place = jnp.arange(TOK_DEV, dtype=jnp.int32)
    which = lax.optimization_barrier(jnp.sum((place[None, :, None] >= ends[:, None, :]).astype(jnp.int32), axis=-1)).astype(jnp.int32)
    offset = jnp.take_along_axis(local, which, axis=1)
    device = jnp.arange(count, dtype=jnp.int32)[:, None]
    flat = ((device * per + which) * MAXLEN + place[None, :] - offset).reshape(-1)
    return padded.reshape(-1, padded.shape[-1])[flat]

def attend(own, remote, key_len):
    seqs, length, width = own.shape
    cols = width // 2
    heads = cols // HEAD_DIM
    query = own[..., :cols].reshape(seqs, length, heads, HEAD_DIM)
    dout = own[..., cols:].reshape(seqs, length, heads, HEAD_DIM)
    keys = remote[..., :cols].reshape(seqs, length, heads, HEAD_DIM)
    values = remote[..., cols:].reshape(seqs, length, heads, HEAD_DIM)
    qf, df = (query.astype(jnp.float32), dout.astype(jnp.float32))
    kf, vf = (keys.astype(jnp.float32), values.astype(jnp.float32))
    scores = jnp.einsum('sqhd,skhd->shqk', qf, kf)
    live = jnp.arange(length, dtype=jnp.int32)[None, None, None, :] < key_len[:, None, None, None]
    expo = jnp.where(live, jnp.exp(scores), jnp.float32(0.0))
    weight = expo / lax.optimization_barrier(jnp.sum(expo, axis=-1, keepdims=True))
    weight_b = weight.astype(jnp.bfloat16)
    wbf = weight_b.astype(jnp.float32)
    attended = jnp.einsum('shqk,skhd->sqhd', wbf, vf).astype(jnp.bfloat16)
    dweight = jnp.einsum('sqhd,skhd->shqk', df, vf)
    total = lax.optimization_barrier(jnp.sum(weight * dweight, axis=-1, keepdims=True))
    dscore = (weight * (dweight - total)).astype(jnp.bfloat16).astype(jnp.float32)
    dquery = jnp.einsum('shqk,skhd->sqhd', dscore, kf).astype(jnp.bfloat16)
    dkeys = jnp.einsum('shqk,sqhd->skhd', dscore, qf).astype(jnp.bfloat16)
    dvalues = jnp.einsum('shqk,sqhd->skhd', wbf, df).astype(jnp.bfloat16)
    front = jnp.concatenate([dquery.reshape(seqs, length, cols), attended.reshape(seqs, length, cols)], axis=-1)
    back = jnp.concatenate([dkeys.reshape(seqs, length, cols), dvalues.reshape(seqs, length, cols)], axis=-1)
    return (front, back)

def left_product(left, right):
    return lax.dot_general(left, right, (((0,), (0,)), ((), ())), preferred_element_type=jnp.float32)

def right_product(rows, weight):
    return lax.dot_general(rows, weight, (((1,), (1,)), ((), ())), preferred_element_type=jnp.float32)

def reference(states, gains, proj_a, proj_b, cotangent, src_len, tgt_len, dest):
    enc_x, enc_scale, enc_norm = rms_forward(states[0], gains[0])
    dec_x, dec_scale, dec_norm = rms_forward(states[1], gains[1])
    keys = jnp.dot(enc_norm, proj_a[0], preferred_element_type=jnp.float32).astype(jnp.bfloat16)
    values = jnp.dot(enc_norm, proj_b[0], preferred_element_type=jnp.float32).astype(jnp.bfloat16)
    query = jnp.dot(dec_norm, proj_a[1], preferred_element_type=jnp.float32).astype(jnp.bfloat16)
    dout = jnp.dot(cotangent, proj_b[1], preferred_element_type=jnp.float32).astype(jnp.bfloat16)
    flat_dest = dest.reshape(-1).astype(jnp.int32)
    total = flat_dest.shape[0]
    inverse = jnp.zeros((total,), jnp.int32).at[flat_dest].set(jnp.arange(total, dtype=jnp.int32))
    src_start, src_flat = starts_of(src_len)
    tgt_start, tgt_flat = starts_of(tgt_len)
    remote = pack(jnp.concatenate([keys, values], axis=1), src_start[inverse], src_flat[inverse])
    own = pack(jnp.concatenate([query, dout], axis=1), tgt_start, tgt_flat)
    front, back = attend(own, remote, src_flat[inverse])
    dec_rows = unpack(front, tgt_len)
    enc_rows = unpack(back[flat_dest], src_len)
    cols = proj_a.shape[2]
    dquery, attended = (dec_rows[:, :cols], dec_rows[:, cols:])
    dkeys, dvalues = (enc_rows[:, :cols], enc_rows[:, cols:])
    enc_dnorm = right_product(dkeys, proj_a[0]) + right_product(dvalues, proj_b[0])
    dec_dnorm = right_product(dquery, proj_a[1])
    grad_states = jnp.stack([rms_backward(enc_x, enc_scale, gains[0], enc_dnorm), rms_backward(dec_x, dec_scale, gains[1], dec_dnorm)])
    grad_a = jnp.stack([left_product(enc_norm, dkeys), left_product(dec_norm, dquery)])
    grad_b = jnp.stack([left_product(enc_norm, dvalues), left_product(cotangent, attended)])
    return (grad_states, grad_a, grad_b)
```

```python
import functools

import jax
import jax.numpy as jnp
from jax import lax
from jax.experimental import pallas as pl
from jax.experimental.pallas import tpu as pltpu
from jax.sharding import PartitionSpec as P

HEAD_DIM = 64
SEQ_DEV = 16
MAXLEN = 16
TOK = 128
SLOTS = 256
RING = 4
EPS = 1e-06
F32 = jnp.float32
BF16 = jnp.bfloat16
VMEM = pl.BlockSpec(memory_space=pltpu.VMEM)
SMEM = pl.BlockSpec(memory_space=pltpu.SMEM)


def iota(shape, dim):
    return lax.broadcasted_iota(jnp.int32, shape, dim)


def total(value, axis):
    return jnp.sum(value.astype(F32), axis=axis, keepdims=True)


def cost(flops, nbytes):
    return pl.CostEstimate(flops=flops, bytes_accessed=nbytes, transcendentals=0)


def params(mib=32, **more):
    return pltpu.CompilerParams(vmem_limit_bytes=mib << 20, **more)


def column_of(row):
    square = jnp.broadcast_to(row, (SEQ_DEV, SEQ_DEV))
    same = iota((SEQ_DEV, SEQ_DEV), 0) == iota((SEQ_DEV, SEQ_DEV), 1)
    return total(jnp.where(same, square, 0), 1)


def slot_onehot(member, src_len, dest):
    i, j = iota((SEQ_DEV, SEQ_DEV), 0), iota((SEQ_DEV, SEQ_DEV), 1)
    lengths = src_len[pl.ds(member, 1), :]
    ends = total(jnp.where(j <= i, jnp.broadcast_to(lengths, (SEQ_DEV, SEQ_DEV)), 0), 1)
    begins = ends - column_of(lengths)
    place = column_of(dest[pl.ds(member, 1), :] >> 4) * MAXLEN
    row = iota((SEQ_DEV, TOK), 1).astype(F32)
    inside = (row >= begins) & (row < ends)
    target = total(jnp.where(inside, place + row - begins, 0.0), 0)
    hit = iota((SLOTS, TOK), 0).astype(F32) == target
    return jnp.where(hit, 1.0, 0.0).astype(BF16)


def pair_mask(member, src_len, tgt_len, dest):
    i, j = iota((SEQ_DEV, SEQ_DEV), 0), iota((SEQ_DEV, SEQ_DEV), 1)
    column = column_of(tgt_len[pl.ds(member, 1), :])
    ends = total(jnp.where(i <= j, jnp.broadcast_to(column, (SEQ_DEV, SEQ_DEV)), 0.0), 0)
    row = iota((TOK, SEQ_DEV), 0).astype(F32)
    mine = total(jnp.where(row >= ends, 1.0, 0.0), 1)
    codes = dest[...]
    to_me = (codes >> 4) == member
    target = total(jnp.where(to_me, codes & 15, 0), 1)
    length = total(jnp.where(to_me, src_len[...], 0), 1)
    lane = iota((SEQ_DEV, SLOTS), 1)
    own = (lane >> 4) == iota((SEQ_DEV, SLOTS), 0)
    target = total(jnp.where(own, target, 0.0), 0)
    length = total(jnp.where(own, length, 0.0), 0)
    step = (iota((1, SLOTS), 1) & 15).astype(F32)
    target = jnp.where(step < length, target, -1.0)
    return mine == target


def norm_kernel(where_ref, x_ref, gain_ref, cot_ref, normed_ref, left_ref, by_x_ref, by_z_ref):
    xf = x_ref[...].astype(F32)
    scale = lax.rsqrt(jnp.mean(xf * xf, axis=-1, keepdims=True) + EPS)
    normed = (xf * scale * gain_ref[...]).astype(BF16)
    normed_ref[...] = normed
    block = normed.shape[1] // (RING * RING)
    for xd in range(RING):
        for zd in range(RING):
            at = (zd * RING + xd) * block
            by_x_ref[xd, :, zd * block : (zd + 1) * block] = normed[:, at : at + block]

    @pl.when(where_ref[0] == 0)
    def _():
        left_ref[...] = normed_ref[...]

    @pl.when(where_ref[0] != 0)
    def _():
        left_ref[...] = cot_ref[...]

    span = RING * block
    for zd in range(RING):
        by_z_ref[zd] = left_ref[:, zd * span : (zd + 1) * span]


def normalise(where, x, gain, cot):
    rows, width = x.shape
    return pl.pallas_call(
        norm_kernel,
        in_specs=[SMEM, VMEM, VMEM, VMEM],
        out_specs=[VMEM] * 4,
        out_shape=[
            jax.ShapeDtypeStruct((rows, width), BF16),
            jax.ShapeDtypeStruct((rows, width), BF16),
            jax.ShapeDtypeStruct((RING, rows, width // RING), BF16),
            jax.ShapeDtypeStruct((RING, rows, width // RING), BF16),
        ],
        compiler_params=params(),
        cost_estimate=cost(5 * rows * width, 12 * rows * width),
        name="norm",
    )(where, x, gain, cot)


def project_kernel(where_ref, n_ref, l_ref, a_ref, b_ref, keep_ref, send_ref, acc_a, acc_b):
    k = pl.program_id(0)

    @pl.when(k == 0)
    def _():
        acc_a[...] = jnp.zeros_like(acc_a)
        acc_b[...] = jnp.zeros_like(acc_b)

    acc_a[...] += jnp.dot(n_ref[...], a_ref[...], preferred_element_type=F32)
    acc_b[...] += jnp.dot(l_ref[...], b_ref[...], preferred_element_type=F32)

    @pl.when(k == pl.num_programs(0) - 1)
    def _():
        half = acc_a.shape[1] // 2
        mine = pl.multiple_of(where_ref[0] * half, half)
        other = pl.multiple_of((1 - where_ref[0]) * half, half)
        keep_ref[:, :half] = acc_a[:, pl.ds(mine, half)].astype(BF16)
        keep_ref[:, half:] = acc_b[:, pl.ds(mine, half)].astype(BF16)
        send_ref[:, :half] = acc_a[:, pl.ds(other, half)].astype(BF16)
        send_ref[:, half:] = acc_b[:, pl.ds(other, half)].astype(BF16)


def project(where, normed, left, weight_a, weight_b):
    rows, width = normed.shape
    cols = weight_a.shape[1]
    step = 512
    half = jax.ShapeDtypeStruct((rows, cols), BF16)
    return pl.pallas_call(
        project_kernel,
        grid=(width // step,),
        in_specs=[
            SMEM,
            pl.BlockSpec((rows, step), lambda k: (0, k)),
            pl.BlockSpec((rows, step), lambda k: (0, k)),
            pl.BlockSpec((step, cols), lambda k: (k, 0)),
            pl.BlockSpec((step, cols), lambda k: (k, 0)),
        ],
        out_specs=[pl.BlockSpec((rows, cols), lambda k: (0, 0))] * 2,
        out_shape=[half, half],
        scratch_shapes=[pltpu.VMEM((rows, cols), F32)] * 2,
        compiler_params=params(dimension_semantics=("arbitrary",)),
        cost_estimate=cost(4 * rows * width * cols, 4 * width * cols),
        name="project",
    )(where, normed, left, weight_a, weight_b)


def pack_kernel(where_ref, keep_ref, got_ref, src_ref, dest_ref, out_ref):
    spread = slot_onehot(where_ref[1], src_ref, dest_ref)

    @pl.when(where_ref[0] == 0)
    def _():
        out_ref[...] = jnp.dot(spread, keep_ref[...], preferred_element_type=F32).astype(BF16)

    @pl.when(where_ref[0] != 0)
    def _():
        out_ref[...] = jnp.dot(spread, got_ref[...], preferred_element_type=F32).astype(BF16)


def pack(where, keep, got, src_len, dest):
    width = keep.shape[1]
    return pl.pallas_call(
        pack_kernel,
        in_specs=[SMEM] + [VMEM] * 4,
        out_specs=VMEM,
        out_shape=jax.ShapeDtypeStruct((SLOTS, width), BF16),
        compiler_params=params(),
        cost_estimate=cost(2 * SLOTS * TOK * width, 2 * SLOTS * width),
        name="pack",
    )(where, keep, got, src_len, dest)


def attend_kernel(
    where_ref, keep_ref, got_ref, slots_ref, src_ref, tgt_ref, dest_ref, front_ref, back_ref, own_ref
):
    mask = pair_mask(where_ref[1], src_ref, tgt_ref, dest_ref)

    @pl.when(where_ref[0] == 0)
    def _():
        own_ref[...] = got_ref[...]

    @pl.when(where_ref[0] != 0)
    def _():
        own_ref[...] = keep_ref[...]

    half = own_ref.shape[1] // 2
    pair = 2 * HEAD_DIM
    low = iota((1, pair), 1) < HEAD_DIM
    nothing = jnp.zeros((), BF16)

    def both(value):
        return jnp.concatenate(
            [jnp.where(low, value, nothing), jnp.where(low, nothing, value)], axis=0
        )

    def nt(left, right):
        return lax.dot_general(left, right, (((1,), (1,)), ((), ())), preferred_element_type=F32)

    def tn(left, right):
        return lax.dot_general(left, right, (((0,), (0,)), ((), ())), preferred_element_type=F32)

    def one(score, dweight):
        expo = jnp.where(mask, jnp.exp(score), 0.0)
        weight = expo * (1.0 / jnp.sum(expo, axis=-1, keepdims=True))
        mean = jnp.sum(weight * dweight, axis=-1, keepdims=True)
        return weight.astype(BF16), (weight * (dweight - mean)).astype(BF16)

    def fold(value):
        return jnp.where(low, value[:SLOTS], value[SLOTS:]).astype(BF16)

    for p in range(half // pair):
        first = slice(p * pair, (p + 1) * pair)
        second = slice(half + p * pair, half + (p + 1) * pair)
        query, dout = own_ref[:, first], own_ref[:, second]
        keys, values = both(slots_ref[:, first]), both(slots_ref[:, second])
        score, dweight = nt(query, keys), nt(dout, values)
        weight_0, dscore_0 = one(score[:, :SLOTS], dweight[:, :SLOTS])
        weight_1, dscore_1 = one(score[:, SLOTS:], dweight[:, SLOTS:])
        weight = jnp.concatenate([weight_0, weight_1], axis=1)
        dscore = jnp.concatenate([dscore_0, dscore_1], axis=1)
        front_ref[:, first] = jnp.dot(dscore, keys, preferred_element_type=F32).astype(BF16)
        front_ref[:, second] = jnp.dot(weight, values, preferred_element_type=F32).astype(BF16)
        back_ref[:, first] = fold(tn(dscore, query))
        back_ref[:, second] = fold(tn(weight, dout))


def attend(where, keep, got, slots, src_len, tgt_len, dest):
    rows, width = keep.shape
    return pl.pallas_call(
        attend_kernel,
        in_specs=[SMEM] + [VMEM] * 6,
        out_specs=[VMEM] * 2,
        out_shape=[
            jax.ShapeDtypeStruct((rows, width), BF16),
            jax.ShapeDtypeStruct((SLOTS, width), BF16),
        ],
        scratch_shapes=[pltpu.VMEM((rows, width), BF16)],
        compiler_params=params(),
        cost_estimate=cost(24 * rows * SLOTS * width, 8 * SLOTS * width),
        name="attend",
    )(where, keep, got, slots, src_len, tgt_len, dest)


def unpack_kernel(where_ref, back_ref, front_ref, src_ref, dest_ref, keep_ref, send_ref):
    spread = slot_onehot(where_ref[1], src_ref, dest_ref)
    rows = lax.dot_general(
        spread, back_ref[...], (((0,), (0,)), ((), ())), preferred_element_type=F32
    ).astype(BF16)

    @pl.when(where_ref[0] == 0)
    def _():
        keep_ref[...] = rows
        send_ref[...] = front_ref[...]

    @pl.when(where_ref[0] != 0)
    def _():
        keep_ref[...] = front_ref[...]
        send_ref[...] = rows


def unpack(where, back, front, src_len, dest):
    width = front.shape[1]
    half = jax.ShapeDtypeStruct((TOK, width), BF16)
    return pl.pallas_call(
        unpack_kernel,
        in_specs=[SMEM] + [VMEM] * 4,
        out_specs=[VMEM] * 2,
        out_shape=[half, half],
        compiler_params=params(),
        cost_estimate=cost(2 * SLOTS * TOK * width, 4 * SLOTS * width),
        name="unpack",
    )(where, back, front, src_len, dest)


def join_kernel(where_ref, keep_ref, got_ref, first_ref, second_ref):
    half = keep_ref.shape[1] // 2
    mine = pl.multiple_of(where_ref[0] * half, half)
    other = pl.multiple_of((1 - where_ref[0]) * half, half)
    first_ref[:, pl.ds(mine, half)] = keep_ref[:, :half]
    first_ref[:, pl.ds(other, half)] = got_ref[:, :half]
    second_ref[:, pl.ds(mine, half)] = keep_ref[:, half:]
    second_ref[:, pl.ds(other, half)] = got_ref[:, half:]


def join(where, keep, got):
    shape = jax.ShapeDtypeStruct(keep.shape, BF16)
    return pl.pallas_call(
        join_kernel,
        in_specs=[SMEM, VMEM, VMEM],
        out_specs=[VMEM] * 2,
        out_shape=[shape, shape],
        compiler_params=params(),
        cost_estimate=cost(0, 8 * keep.size),
        name="join",
    )(where, keep, got)


def dnorm_kernel(where_ref, first_ref, second_ref, a_ref, b_ref, out_ref):
    def nt(left, right):
        return lax.dot_general(left, right, (((1,), (1,)), ((), ())), preferred_element_type=F32)

    @pl.when(where_ref[0] == 0)
    def _():
        out_ref[...] = (
            nt(first_ref[...], a_ref[...]) + nt(second_ref[...], b_ref[...])
        ).astype(BF16)

    @pl.when(where_ref[0] != 0)
    def _():
        out_ref[...] = nt(first_ref[...], a_ref[...]).astype(BF16)


def dnorm_partial(where, first, second, weight_a, weight_b):
    rows, cols = first.shape
    width = weight_a.shape[0]
    step = 512
    return pl.pallas_call(
        dnorm_kernel,
        grid=(width // step,),
        in_specs=[
            SMEM,
            pl.BlockSpec((rows, cols), lambda k: (0, 0)),
            pl.BlockSpec((rows, cols), lambda k: (0, 0)),
            pl.BlockSpec((step, cols), lambda k: (k, 0)),
            pl.BlockSpec((step, cols), lambda k: (k, 0)),
        ],
        out_specs=pl.BlockSpec((rows, step), lambda k: (0, k)),
        out_shape=jax.ShapeDtypeStruct((rows, width), BF16),
        compiler_params=params(dimension_semantics=("arbitrary",)),
        cost_estimate=cost(4 * rows * width * cols, 4 * width * cols),
        name="dnorm",
    )(where, first, second, weight_a, weight_b)


def rms_back_kernel(where_ref, x_ref, gain_ref, parts_ref, out_ref):
    rows = out_ref.shape[0]
    mine = pl.multiple_of(where_ref[2] * rows, rows)
    xf = x_ref[pl.ds(mine, rows), :].astype(F32)
    scale = lax.rsqrt(jnp.mean(xf * xf, axis=-1, keepdims=True) + EPS)
    dnorm = parts_ref[0].astype(F32)
    for i in range(1, RING):
        dnorm += parts_ref[i].astype(F32)
    upper = gain_ref[...] * dnorm
    inner = jnp.mean(xf * upper, axis=-1, keepdims=True)
    out_ref[...] = (scale * upper - xf * (scale * scale * scale * inner)).astype(BF16)


def rms_back(where, x, gain, parts):
    rows, width = parts.shape[1:]
    return pl.pallas_call(
        rms_back_kernel,
        in_specs=[SMEM] + [VMEM] * 3,
        out_specs=VMEM,
        out_shape=jax.ShapeDtypeStruct((rows, width), BF16),
        compiler_params=params(),
        cost_estimate=cost(10 * rows * width, 12 * rows * width),
        name="rms_back",
    )(where, x, gain, parts)


def place_kernel(where_ref, own_ref, left_ref, right_ref, far_a_ref, far_b_ref, out_ref):
    rows = own_ref.shape[0]
    half = rows // 2

    def at(k):
        return pl.multiple_of(((where_ref[2] + k) % RING) * rows, rows)

    out_ref[pl.ds(at(0), rows), :] = own_ref[...]
    out_ref[pl.ds(at(3), rows), :] = left_ref[...]
    out_ref[pl.ds(at(1), rows), :] = right_ref[...]
    out_ref[pl.ds(at(2), half), :] = far_a_ref[...]
    out_ref[pl.ds(pl.multiple_of(at(2) + half, half), half), :] = far_b_ref[...]


def place(where, pieces):
    rows, width = pieces[0].shape
    return pl.pallas_call(
        place_kernel,
        in_specs=[SMEM] + [VMEM] * 5,
        out_specs=VMEM,
        out_shape=jax.ShapeDtypeStruct((RING * rows, width), BF16),
        compiler_params=params(),
        cost_estimate=cost(0, 4 * RING * rows * width),
        name="place",
    )(where, *pieces)


def shift(value, axis, k):
    return lax.ppermute(value, axis, [(i, (i + k) % RING) for i in range(RING)])


def gathered(block, axis):
    half = block.shape[0] // 2
    left, right = shift(block, axis, 1), shift(block, axis, 3)
    far_a, far_b = shift(left[:half], axis, 1), shift(right[half:], axis, 3)
    return [block, left, right, far_a, far_b]


def exchanged(slices, axis):
    me = lax.axis_index(axis)

    def take(k):
        return lax.dynamic_index_in_dim(slices, (me + k) % RING, 0, keepdims=False)

    return [take(0), shift(take(1), axis, 1), shift(take(3), axis, 3), shift(take(2), axis, 2)]


def outer_kernel(ks, slot, where_ref, *refs):
    lefts, rights = refs[:4], refs[4:9]
    outs, left, right = refs[9:-2], refs[-2], refs[-1]
    at = 0
    for ref in lefts:
        left[at : at + ref.shape[0], :] = ref[...]
        at += ref.shape[0]
    at = 0
    for ref in rights:
        right[at : at + ref.shape[0], :] = ref[...]
        at += ref.shape[0]
    block = left.shape[1] // RING
    for k, out in zip(ks, outs, strict=True):
        column = pl.multiple_of(((where_ref[slot] + k) % RING) * block, block)
        out[...] = lax.dot_general(
            left[:, pl.ds(column, block)],
            right[...],
            (((0,), (0,)), ((), ())),
            preferred_element_type=F32,
        ).astype(out.dtype)


def outer(where, slot, lefts, rights, ks, kinds):
    rows = sum(piece.shape[0] for piece in lefts)
    width, cols = lefts[0].shape[1], rights[0].shape[1]
    block = width // RING
    return pl.pallas_call(
        functools.partial(outer_kernel, ks, slot),
        in_specs=[SMEM] + [VMEM] * 9,
        out_specs=[VMEM] * len(ks),
        out_shape=[jax.ShapeDtypeStruct((block, cols), kind) for kind in kinds],
        scratch_shapes=[pltpu.VMEM((rows, width), BF16), pltpu.VMEM((rows, cols), BF16)],
        compiler_params=params(),
        cost_estimate=cost(2 * rows * block * cols * len(ks), 4 * rows * cols),
        name="outer",
    )(where, *lefts, *rights)


def reduced(where, slot, lefts, rights, axis):
    (far,) = outer(where, slot, lefts, rights, (2,), (BF16,))
    half = far.shape[0] // 2
    from_left, from_right = shift(far[:half], axis, 1), shift(far[half:], axis, 3)
    right, left, own = outer(where, slot, lefts, rights, (1, 3, 0), (BF16, BF16, F32))
    right = jnp.concatenate([right[:half] + from_left, right[half:]], axis=0)
    left = jnp.concatenate([left[:half], left[half:] + from_right], axis=0)
    a, b = shift(right, axis, 1), shift(left, axis, 3)
    return own + a.astype(F32) + b.astype(F32)


def per_device(states, gains, proj_a, proj_b, cotangent, src_len, tgt_len, dest):
    z, x = lax.axis_index("z"), lax.axis_index("x")
    member = z * RING + x
    where = jnp.stack([lax.axis_index("section"), member, lax.axis_index("mp"), z, x]).astype(jnp.int32)
    weight_a, weight_b = proj_a[0], proj_b[0]
    rows = states[0]
    normed, left, by_x, by_z = normalise(where, rows, gains, cotangent)
    keep, send = project(where, normed, left, weight_a, weight_b)
    swap = [(0, 1), (1, 0)]
    got = lax.ppermute(send, "section", swap)
    slots = pack(where, keep, got, src_len, dest)
    width = slots.shape[1]
    slots = slots.reshape(SEQ_DEV, MAXLEN, width)
    slots = lax.all_to_all(slots, ("z", "x"), split_axis=0, concat_axis=0, tiled=True)
    slots = slots.reshape(SLOTS, width)
    lefts_a, lefts_b = exchanged(by_x, "x"), exchanged(by_z, "z")
    front, back = attend(where, keep, got, slots, src_len, tgt_len, dest)
    back = back.reshape(SEQ_DEV, MAXLEN, width)
    back = lax.all_to_all(back, ("z", "x"), split_axis=0, concat_axis=0, tiled=True)
    keep, send = unpack(where, back.reshape(SLOTS, width), front, src_len, dest)
    got = lax.ppermute(send, "section", swap)
    first, second = join(where, keep, got)

    rights_a, rights_b = gathered(first, "x"), gathered(second, "z")
    partial = dnorm_partial(where, first, second, weight_a, weight_b)
    parts = lax.all_to_all(
        partial.reshape(RING, TOK // RING, -1), "mp", split_axis=0, concat_axis=0, tiled=True
    )
    quarter = rms_back(where, rows, gains, parts)
    grad_states = place(where, gathered(quarter, "mp"))

    grad_a = reduced(where, 3, lefts_a, rights_a, "z")
    grad_b = reduced(where, 4, lefts_b, rights_b, "x")
    return (grad_states[None], grad_a[None], grad_b[None])


def solution(mesh):
    split = jax.sharding.Mesh(mesh.devices.reshape(2, RING, RING, RING), ("section", "z", "x", "mp"))
    dp = ("z", "x")
    return jax.shard_map(
        per_device,
        mesh=split,
        in_specs=(
            P("section", dp, None),
            P("section", None),
            P("section", None, "mp"),
            P("section", None, "mp"),
            P(dp, None),
            P(),
            P(),
            P(),
        ),
        out_specs=(P("section", dp, None), P("section", dp, "mp"), P("section", dp, "mp")),
        check_vma=False,
    )
```

```python
import jax
import jax.numpy as jnp
from jax import lax
from jax.experimental import pallas as pl
from jax.experimental.pallas import tpu as pltpu
from jax.sharding import PartitionSpec as P

HEAD_DIM = 64
SEQ_DEV = 16
MAXLEN = 16
TOK = 128
SLOTS = 256
RING = 4
EPS = 1e-06
F32 = jnp.float32
BF16 = jnp.bfloat16
VMEM = pl.BlockSpec(memory_space=pltpu.VMEM)
HBM = pl.BlockSpec(memory_space=pltpu.HBM)


def iota(shape, dim):
    return lax.broadcasted_iota(jnp.int32, shape, dim)


def total(value, axis):
    return jnp.sum(value.astype(F32), axis=axis, keepdims=True)


def cost(flops, nbytes):
    return pl.CostEstimate(flops=flops, bytes_accessed=nbytes, transcendentals=0)


def params(mib=12, **more):
    return pltpu.CompilerParams(vmem_limit_bytes=mib << 20, **more)


def column_of(row):
    square = jnp.broadcast_to(row, (SEQ_DEV, SEQ_DEV))
    same = iota((SEQ_DEV, SEQ_DEV), 0) == iota((SEQ_DEV, SEQ_DEV), 1)
    return total(jnp.where(same, square, 0), 1)


def member_index():
    return lax.axis_index("z") * RING + lax.axis_index("x")


def slot_onehot(member, src_len, dest):
    i, j = iota((SEQ_DEV, SEQ_DEV), 0), iota((SEQ_DEV, SEQ_DEV), 1)
    lengths = src_len[pl.ds(member, 1), :]
    ends = total(jnp.where(j <= i, jnp.broadcast_to(lengths, (SEQ_DEV, SEQ_DEV)), 0), 1)
    begins = ends - column_of(lengths)
    place = column_of(dest[pl.ds(member, 1), :] >> 4) * MAXLEN
    row = iota((SEQ_DEV, TOK), 1).astype(F32)
    inside = (row >= begins) & (row < ends)
    target = total(jnp.where(inside, place + row - begins, 0.0), 0)
    hit = iota((SLOTS, TOK), 0).astype(F32) == target
    return jnp.where(hit, 1.0, 0.0).astype(BF16)


def pair_mask(member, src_len, tgt_len, dest):
    i, j = iota((SEQ_DEV, SEQ_DEV), 0), iota((SEQ_DEV, SEQ_DEV), 1)
    column = column_of(tgt_len[pl.ds(member, 1), :])
    ends = total(jnp.where(i <= j, jnp.broadcast_to(column, (SEQ_DEV, SEQ_DEV)), 0.0), 0)
    row = iota((TOK, SEQ_DEV), 0).astype(F32)
    mine = total(jnp.where(row >= ends, 1.0, 0.0), 1)
    codes = dest[...]
    to_me = (codes >> 4) == member
    target = total(jnp.where(to_me, codes & 15, 0), 1)
    length = total(jnp.where(to_me, src_len[...], 0), 1)
    lane = iota((SEQ_DEV, SLOTS), 1)
    own = (lane >> 4) == iota((SEQ_DEV, SLOTS), 0)
    target = total(jnp.where(own, target, 0.0), 0)
    length = total(jnp.where(own, length, 0.0), 0)
    step = (iota((1, SLOTS), 1) & 15).astype(F32)
    target = jnp.where(step < length, target, -1.0)
    return mine == target


def forward_kernel(
    x_ref, gain_ref, cot_ref, a_hbm, b_hbm, keep_ref, send_ref, *rest
):
    by_x, by_z = rest[:RING], rest[RING : 2 * RING]
    a_buf, b_buf, normed_ref, left_ref, a_sem, b_sem = rest[2 * RING :]
    count, step, cols = a_buf.shape

    def fetch(k):
        rows = pl.ds(k * step, step)
        return (
            pltpu.make_async_copy(a_hbm.at[rows, :], a_buf.at[k], a_sem.at[k]),
            pltpu.make_async_copy(b_hbm.at[rows, :], b_buf.at[k], b_sem.at[k]),
        )

    for k in range(count):
        for copy in fetch(k):
            copy.start()
    xf = x_ref[...].astype(F32)
    scale = lax.rsqrt(jnp.mean(xf * xf, axis=-1, keepdims=True) + EPS)
    normed_ref[...] = (xf * scale * gain_ref[...]).astype(BF16)
    core = lax.axis_index("section")

    @pl.when(core == 0)
    def _():
        left_ref[...] = normed_ref[...]

    @pl.when(core != 0)
    def _():
        left_ref[...] = cot_ref[...]

    acc_a = acc_b = None
    for k in range(count):
        for copy in fetch(k):
            copy.wait()
        at = slice(k * step, (k + 1) * step)
        part_a = jnp.dot(normed_ref[:, at], a_buf[k], preferred_element_type=F32)
        part_b = jnp.dot(left_ref[:, at], b_buf[k], preferred_element_type=F32)
        acc_a = part_a if acc_a is None else acc_a + part_a
        acc_b = part_b if acc_b is None else acc_b + part_b
    half = cols // 2
    parts = [[acc[:, i * half : (i + 1) * half].astype(BF16) for acc in (acc_a, acc_b)] for i in range(2)]

    def put(ref, pieces):
        ref[:, :half] = pieces[0]
        ref[:, half:] = pieces[1]

    @pl.when(core == 0)
    def _():
        put(keep_ref, parts[0])
        put(send_ref, parts[1])

    @pl.when(core != 0)
    def _():
        put(keep_ref, parts[1])
        put(send_ref, parts[0])

    z, x = lax.axis_index("z"), lax.axis_index("x")
    block = cols // RING
    for k in range(RING):
        for j in range(RING):
            to = slice(j * block, (j + 1) * block)
            at = ((z + j) % RING * RING + (x + k) % RING) * block
            by_x[k][:, to] = normed_ref[:, pl.ds(pl.multiple_of(at, block), block)]
            at = ((z + k) % RING * RING + (x + j) % RING) * block
            by_z[k][:, to] = left_ref[:, pl.ds(pl.multiple_of(at, block), block)]


def forward(x, gain, cot, weight_a, weight_b):
    rows, width = x.shape
    cols = weight_a.shape[1]
    step = 512
    count = width // step
    half = jax.ShapeDtypeStruct((rows, cols), BF16)
    outs = pl.pallas_call(
        forward_kernel,
        in_specs=[VMEM] * 3 + [HBM] * 2,
        out_specs=[VMEM] * (2 + 2 * RING),
        out_shape=[half] * (2 + 2 * RING),
        scratch_shapes=[pltpu.VMEM((count, step, cols), BF16)] * 2
        + [pltpu.VMEM((rows, width), BF16)] * 2
        + [pltpu.SemaphoreType.DMA((count,))] * 2,
        compiler_params=params(32),
        cost_estimate=cost(4 * rows * width * cols, 4 * width * cols),
        name="forward",
    )(x, gain, cot, weight_a, weight_b)
    return outs[0], outs[1], outs[2 : 2 + RING], outs[2 + RING :]


def pack_kernel(keep_ref, got_ref, src_ref, dest_ref, out_ref):
    spread = slot_onehot(member_index(), src_ref, dest_ref)

    @pl.when(lax.axis_index("section") == 0)
    def _():
        out_ref[...] = jnp.dot(spread, keep_ref[...], preferred_element_type=F32).astype(BF16)

    @pl.when(lax.axis_index("section") != 0)
    def _():
        out_ref[...] = jnp.dot(spread, got_ref[...], preferred_element_type=F32).astype(BF16)


def pack(keep, got, src_len, dest):
    width = keep.shape[1]
    return pl.pallas_call(
        pack_kernel,
        in_specs=[VMEM] * 4,
        out_specs=VMEM,
        out_shape=jax.ShapeDtypeStruct((SLOTS, width), BF16),
        compiler_params=params(),
        cost_estimate=cost(2 * SLOTS * TOK * width, 2 * SLOTS * width),
        name="pack",
    )(keep, got, src_len, dest)


def attend_kernel(
    keep_ref, got_ref, slots_ref, src_ref, tgt_ref, dest_ref, front_ref, back_ref, own_ref
):
    mask = pair_mask(member_index(), src_ref, tgt_ref, dest_ref)

    @pl.when(lax.axis_index("section") == 0)
    def _():
        own_ref[...] = got_ref[...]

    @pl.when(lax.axis_index("section") != 0)
    def _():
        own_ref[...] = keep_ref[...]

    half = own_ref.shape[1] // 2
    pair = 2 * HEAD_DIM
    low = iota((1, pair), 1) < HEAD_DIM
    nothing = jnp.zeros((), BF16)

    def both(value):
        return jnp.concatenate(
            [jnp.where(low, value, nothing), jnp.where(low, nothing, value)], axis=0
        )

    def nt(left, right):
        return lax.dot_general(left, right, (((1,), (1,)), ((), ())), preferred_element_type=F32)

    def tn(left, right):
        return lax.dot_general(left, right, (((0,), (0,)), ((), ())), preferred_element_type=F32)

    def one(score, dweight):
        expo = jnp.where(mask, jnp.exp(score), 0.0)
        weight = expo * (1.0 / jnp.sum(expo, axis=-1, keepdims=True))
        mean = jnp.sum(weight * dweight, axis=-1, keepdims=True)
        return weight.astype(BF16), (weight * (dweight - mean)).astype(BF16)

    def fold(value):
        return jnp.where(low, value[:SLOTS], value[SLOTS:]).astype(BF16)

    for p in range(half // pair):
        first = slice(p * pair, (p + 1) * pair)
        second = slice(half + p * pair, half + (p + 1) * pair)
        query, dout = own_ref[:, first], own_ref[:, second]
        keys, values = both(slots_ref[:, first]), both(slots_ref[:, second])
        score, dweight = nt(query, keys), nt(dout, values)
        weight_0, dscore_0 = one(score[:, :SLOTS], dweight[:, :SLOTS])
        weight_1, dscore_1 = one(score[:, SLOTS:], dweight[:, SLOTS:])
        weight = jnp.concatenate([weight_0, weight_1], axis=1)
        dscore = jnp.concatenate([dscore_0, dscore_1], axis=1)
        front_ref[:, first] = jnp.dot(dscore, keys, preferred_element_type=F32).astype(BF16)
        front_ref[:, second] = jnp.dot(weight, values, preferred_element_type=F32).astype(BF16)
        back_ref[:, first] = fold(tn(dscore, query))
        back_ref[:, second] = fold(tn(weight, dout))


def attend(keep, got, slots, src_len, tgt_len, dest):
    rows, width = keep.shape
    return pl.pallas_call(
        attend_kernel,
        in_specs=[VMEM] * 6,
        out_specs=[VMEM] * 2,
        out_shape=[
            jax.ShapeDtypeStruct((rows, width), BF16),
            jax.ShapeDtypeStruct((SLOTS, width), BF16),
        ],
        scratch_shapes=[pltpu.VMEM((rows, width), BF16)],
        compiler_params=params(),
        cost_estimate=cost(24 * rows * SLOTS * width, 8 * SLOTS * width),
        name="attend",
    )(keep, got, slots, src_len, tgt_len, dest)


def unpack_kernel(back_ref, front_ref, src_ref, dest_ref, keep_ref, send_ref):
    spread = slot_onehot(member_index(), src_ref, dest_ref)
    rows = lax.dot_general(
        spread, back_ref[...], (((0,), (0,)), ((), ())), preferred_element_type=F32
    ).astype(BF16)

    @pl.when(lax.axis_index("section") == 0)
    def _():
        keep_ref[...] = rows
        send_ref[...] = front_ref[...]

    @pl.when(lax.axis_index("section") != 0)
    def _():
        keep_ref[...] = front_ref[...]
        send_ref[...] = rows


def unpack(back, front, src_len, dest):
    width = front.shape[1]
    half = jax.ShapeDtypeStruct((TOK, width), BF16)
    return pl.pallas_call(
        unpack_kernel,
        in_specs=[VMEM] * 4,
        out_specs=[VMEM] * 2,
        out_shape=[half, half],
        compiler_params=params(),
        cost_estimate=cost(2 * SLOTS * TOK * width, 4 * SLOTS * width),
        name="unpack",
    )(back, front, src_len, dest)


def join_kernel(keep_ref, got_ref, first_ref, second_ref):
    half = keep_ref.shape[1] // 2
    mine = pl.multiple_of(lax.axis_index("section") * half, half)
    other = pl.multiple_of((1 - lax.axis_index("section")) * half, half)
    first_ref[:, pl.ds(mine, half)] = keep_ref[:, :half]
    first_ref[:, pl.ds(other, half)] = got_ref[:, :half]
    second_ref[:, pl.ds(mine, half)] = keep_ref[:, half:]
    second_ref[:, pl.ds(other, half)] = got_ref[:, half:]


def join(keep, got):
    shape = jax.ShapeDtypeStruct(keep.shape, BF16)
    return pl.pallas_call(
        join_kernel,
        in_specs=[VMEM, VMEM],
        out_specs=[VMEM] * 2,
        out_shape=[shape, shape],
        compiler_params=params(),
        cost_estimate=cost(0, 8 * keep.size),
        name="join",
    )(keep, got)


def dnorm_kernel(first_ref, second_ref, a_hbm, b_hbm, out_ref, a_buf, b_buf, a_sem, b_sem):
    count, step, _ = a_buf.shape
    source = lax.axis_index("section") == 0

    def nt(left, right):
        return lax.dot_general(left, right, (((1,), (1,)), ((), ())), preferred_element_type=F32)

    def fetch(k):
        rows = pl.ds(k * step, step)
        return (
            pltpu.make_async_copy(a_hbm.at[rows, :], a_buf.at[k], a_sem.at[k]),
            pltpu.make_async_copy(b_hbm.at[rows, :], b_buf.at[k], b_sem.at[k]),
        )

    for k in range(count):
        for copy in fetch(k):
            copy.start()
    for k in range(count):
        at = slice(k * step, (k + 1) * step)
        for copy in fetch(k):
            copy.wait()

        @pl.when(source)
        def _(k=k, at=at):
            out_ref[:, at] = (
                nt(first_ref[...], a_buf[k]) + nt(second_ref[...], b_buf[k])
            ).astype(BF16)

        @pl.when(jnp.logical_not(source))
        def _(k=k, at=at):
            out_ref[:, at] = nt(first_ref[...], a_buf[k]).astype(BF16)


def dnorm_partial(first, second, weight_a, weight_b):
    rows, cols = first.shape
    width = weight_a.shape[0]
    step = 512
    count = width // step
    return pl.pallas_call(
        dnorm_kernel,
        in_specs=[VMEM] * 2 + [HBM] * 2,
        out_specs=VMEM,
        out_shape=jax.ShapeDtypeStruct((rows, width), BF16),
        scratch_shapes=[pltpu.VMEM((count, step, cols), BF16)] * 2
        + [pltpu.SemaphoreType.DMA((count,))] * 2,
        compiler_params=params(24),
        cost_estimate=cost(4 * rows * width * cols, 4 * width * cols),
        name="dnorm",
    )(first, second, weight_a, weight_b)


def rms_back_kernel(x_ref, gain_ref, parts_ref, out_ref):
    rows = out_ref.shape[0]
    mine = pl.multiple_of(lax.axis_index("mp") * rows, rows)
    xf = x_ref[pl.ds(mine, rows), :].astype(F32)
    scale = lax.rsqrt(jnp.mean(xf * xf, axis=-1, keepdims=True) + EPS)
    dnorm = parts_ref[0].astype(F32)
    for i in range(1, RING):
        dnorm += parts_ref[i].astype(F32)
    upper = gain_ref[...] * dnorm
    inner = jnp.mean(xf * upper, axis=-1, keepdims=True)
    out_ref[...] = (scale * upper - xf * (scale * scale * scale * inner)).astype(BF16)


def rms_back(x, gain, parts):
    rows, width = parts.shape[1:]
    return pl.pallas_call(
        rms_back_kernel,
        in_specs=[VMEM] * 3,
        out_specs=VMEM,
        out_shape=jax.ShapeDtypeStruct((rows, width), BF16),
        compiler_params=params(),
        cost_estimate=cost(10 * rows * width, 12 * rows * width),
        name="rms_back",
    )(x, gain, parts)


def place_kernel(own_ref, left_ref, right_ref, far_a_ref, far_b_ref, out_ref):
    rows = own_ref.shape[0]
    half = rows // 2

    def at(k):
        return pl.multiple_of(((lax.axis_index("mp") + k) % RING) * rows, rows)

    out_ref[pl.ds(at(0), rows), :] = own_ref[...]
    out_ref[pl.ds(at(3), rows), :] = left_ref[...]
    out_ref[pl.ds(at(1), rows), :] = right_ref[...]
    out_ref[pl.ds(at(2), half), :] = far_a_ref[...]
    out_ref[pl.ds(pl.multiple_of(at(2) + half, half), half), :] = far_b_ref[...]


def place(pieces):
    rows, width = pieces[0].shape
    return pl.pallas_call(
        place_kernel,
        in_specs=[VMEM] * 5,
        out_specs=VMEM,
        out_shape=jax.ShapeDtypeStruct((RING * rows, width), BF16),
        compiler_params=params(),
        cost_estimate=cost(0, 4 * RING * rows * width),
        name="place",
    )(*pieces)


def shift(value, axis, k):
    return lax.ppermute(value, axis, [(i, (i + k) % RING) for i in range(RING)])


def gathered(block, axis):
    half = block.shape[0] // 2
    left, right = shift(block, axis, 1), shift(block, axis, 3)
    far_a, far_b = shift(left[:half], axis, 1), shift(right[half:], axis, 3)
    return [block, left, right, far_a, far_b]


def spread(block, axis):
    far = shift(block, axis, 2)
    return [block, shift(block, axis, 1), shift(block, axis, 3), far]


def exchanged(slices, axis):
    far = shift(slices[2], axis, 2)
    return [slices[0], shift(slices[1], axis, 1), shift(slices[3], axis, 3), far]


def turn_kernel(*refs):
    pieces, out_ref = refs[:-1], refs[-1]
    block, rows = out_ref.shape[1], pieces[0].shape[0]
    for k in range(RING):
        for p, piece in enumerate(pieces):
            out_ref[k, :, p * rows : (p + 1) * rows] = piece[:, k * block : (k + 1) * block].T


def turned(pieces):
    rows, width = pieces[0].shape
    return pl.pallas_call(
        turn_kernel,
        in_specs=[VMEM] * RING,
        out_specs=VMEM,
        out_shape=jax.ShapeDtypeStruct((RING, width // RING, RING * rows), BF16),
        compiler_params=params(),
        cost_estimate=cost(0, 4 * RING * rows * width),
        name="turn",
    )(*pieces)


def far_kernel(left_ref, own_ref, near_ref, next_ref, far_ref, top_ref, low_ref, rows_ref):
    rows = own_ref.shape[0]
    for p, piece in enumerate((own_ref, near_ref, next_ref, far_ref)):
        rows_ref[p * rows : (p + 1) * rows, :] = piece[...]
    half = top_ref.shape[0]
    for i, out in enumerate((top_ref, low_ref)):
        out[...] = jnp.dot(
            left_ref[2, i * half : (i + 1) * half, :], rows_ref[...], preferred_element_type=F32
        ).astype(BF16)


def far_block(left, pieces):
    rows, cols = pieces[0].shape
    block = left.shape[1]
    half = jax.ShapeDtypeStruct((block // 2, cols), BF16)
    return pl.pallas_call(
        far_kernel,
        in_specs=[VMEM] * (1 + RING),
        out_specs=[VMEM] * 3,
        out_shape=[half, half, jax.ShapeDtypeStruct((RING * rows, cols), BF16)],
        compiler_params=params(),
        cost_estimate=cost(2 * RING * rows * block * cols, 8 * RING * rows * cols),
        name="far",
    )(left, *pieces)


def side_kernel(left_ref, rows_ref, from_left_ref, from_right_ref, right_out, left_out):
    half = from_left_ref.shape[0]

    def product(k):
        return jnp.dot(left_ref[k], rows_ref[...], preferred_element_type=F32)

    block = product(1)
    right_out[:half, :] = (block[:half] + from_left_ref[...].astype(F32)).astype(BF16)
    right_out[half:, :] = block[half:].astype(BF16)
    block = product(3)
    left_out[:half, :] = block[:half].astype(BF16)
    left_out[half:, :] = (block[half:] + from_right_ref[...].astype(F32)).astype(BF16)


def side_blocks(left, rows, from_left, from_right):
    block, cols = left.shape[1], rows.shape[1]
    shape = jax.ShapeDtypeStruct((block, cols), BF16)
    return pl.pallas_call(
        side_kernel,
        in_specs=[VMEM] * 4,
        out_specs=[VMEM] * 2,
        out_shape=[shape, shape],
        compiler_params=params(),
        cost_estimate=cost(4 * rows.shape[0] * block * cols, 4 * rows.size),
        name="side",
    )(left, rows, from_left, from_right)


def own_kernel(left_ref, rows_ref, a_ref, b_ref, out_ref):
    block = jnp.dot(left_ref[0], rows_ref[...], preferred_element_type=F32)
    out_ref[...] = block + a_ref[...].astype(F32) + b_ref[...].astype(F32)


def own_block(left, rows, a, b):
    block, cols = left.shape[1], rows.shape[1]
    return pl.pallas_call(
        own_kernel,
        in_specs=[VMEM] * 4,
        out_specs=VMEM,
        out_shape=jax.ShapeDtypeStruct((block, cols), F32),
        compiler_params=params(),
        cost_estimate=cost(2 * rows.shape[0] * block * cols, 8 * rows.size),
        name="own",
    )(left, rows, a, b)


def reduced(left, pieces, axis):
    top, low, rows = far_block(left, pieces)
    from_left, from_right = shift(top, axis, 1), shift(low, axis, 3)
    to_right, to_left = side_blocks(left, rows, from_left, from_right)
    return own_block(left, rows, shift(to_right, axis, 1), shift(to_left, axis, 3))


def per_device(states, gains, proj_a, proj_b, cotangent, src_len, tgt_len, dest):
    weight_a, weight_b = proj_a[0], proj_b[0]
    rows = states[0]
    keep, send, by_x, by_z = forward(rows, gains, cotangent, weight_a, weight_b)
    swap = [(0, 1), (1, 0)]
    got = lax.ppermute(send, "section", swap)
    slots = pack(keep, got, src_len, dest)
    width = slots.shape[1]
    slots = slots.reshape(SEQ_DEV, MAXLEN, width)
    slots = lax.all_to_all(slots, ("z", "x"), split_axis=0, concat_axis=0, tiled=True)
    slots = slots.reshape(SLOTS, width)
    lefts_a, lefts_b = exchanged(by_x, "x"), exchanged(by_z, "z")
    slots, lefts_a = lax.optimization_barrier((slots, lefts_a))
    front, back = attend(keep, got, slots, src_len, tgt_len, dest)
    back = back.reshape(SEQ_DEV, MAXLEN, width)
    back = lax.all_to_all(back, ("z", "x"), split_axis=0, concat_axis=0, tiled=True)
    left_a, left_b = turned(lefts_a), turned(lefts_b)
    back, left_a, left_b = lax.optimization_barrier((back, left_a, left_b))
    keep, send = unpack(back.reshape(SLOTS, width), front, src_len, dest)
    got = lax.ppermute(send, "section", swap)
    first, second = join(keep, got)

    rights_a, rights_b = spread(first, "x"), spread(second, "z")
    partial = dnorm_partial(first, second, weight_a, weight_b)
    parts = lax.all_to_all(
        partial.reshape(RING, TOK // RING, -1), "mp", split_axis=0, concat_axis=0, tiled=True
    )
    quarter = rms_back(rows, gains, parts)
    grad_states = place(gathered(quarter, "mp"))

    grad_a = reduced(left_a, rights_a, "z")
    grad_b = reduced(left_b, rights_b, "x")
    return (grad_states[None], grad_a[None], grad_b[None])


def solution(mesh):
    split = jax.sharding.Mesh(mesh.devices.reshape(2, RING, RING, RING), ("section", "z", "x", "mp"))
    dp = ("z", "x")
    return jax.shard_map(
        per_device,
        mesh=split,
        in_specs=(
            P("section", dp, None),
            P("section", None),
            P("section", None, "mp"),
            P("section", None, "mp"),
            P(dp, None),
            P(),
            P(),
            P(),
        ),
        out_specs=(P("section", dp, None), P("section", dp, "mp"), P("section", dp, "mp")),
        check_vma=False,
    )
```

```python
import jax
import jax.numpy as jnp
from jax import lax
from jax.experimental import pallas as pl
from jax.experimental.pallas import tpu as pltpu
from jax.sharding import PartitionSpec as P

HEAD_DIM = 64
SEQ_DEV = 16
MAXLEN = 16
TOK = 128
SLOTS = 256
RING = 4
EPS = 1e-06
F32 = jnp.float32
BF16 = jnp.bfloat16
VMEM = pl.BlockSpec(memory_space=pltpu.VMEM)
HBM = pl.BlockSpec(memory_space=pltpu.HBM)


def iota(shape, dim):
    return lax.broadcasted_iota(jnp.int32, shape, dim)


def total(value, axis):
    return jnp.sum(value.astype(F32), axis=axis, keepdims=True)


def in_hbm(value):
    return pltpu.with_memory_space_constraint(value, pltpu.HBM)


def cost(flops, nbytes):
    return pl.CostEstimate(flops=flops, bytes_accessed=nbytes, transcendentals=0)


def params(mib=12, **more):
    return pltpu.CompilerParams(vmem_limit_bytes=mib << 20, **more)


def column_of(row):
    square = jnp.broadcast_to(row, (SEQ_DEV, SEQ_DEV))
    same = iota((SEQ_DEV, SEQ_DEV), 0) == iota((SEQ_DEV, SEQ_DEV), 1)
    return total(jnp.where(same, square, 0), 1)


def member_index():
    return lax.axis_index("z") * RING + lax.axis_index("x")


def slot_onehot(member, src_len, dest):
    i, j = iota((SEQ_DEV, SEQ_DEV), 0), iota((SEQ_DEV, SEQ_DEV), 1)
    lengths = src_len[pl.ds(member, 1), :]
    ends = total(jnp.where(j <= i, jnp.broadcast_to(lengths, (SEQ_DEV, SEQ_DEV)), 0), 1)
    begins = ends - column_of(lengths)
    place = column_of(dest[pl.ds(member, 1), :] >> 4) * MAXLEN
    row = iota((SEQ_DEV, TOK), 1).astype(F32)
    inside = (row >= begins) & (row < ends)
    target = total(jnp.where(inside, place + row - begins, 0.0), 0)
    hit = iota((SLOTS, TOK), 0).astype(F32) == target
    return jnp.where(hit, 1.0, 0.0).astype(BF16)


def pair_mask(member, src_len, tgt_len, dest):
    i, j = iota((SEQ_DEV, SEQ_DEV), 0), iota((SEQ_DEV, SEQ_DEV), 1)
    column = column_of(tgt_len[pl.ds(member, 1), :])
    ends = total(jnp.where(i <= j, jnp.broadcast_to(column, (SEQ_DEV, SEQ_DEV)), 0.0), 0)
    row = iota((TOK, SEQ_DEV), 0).astype(F32)
    mine = total(jnp.where(row >= ends, 1.0, 0.0), 1)
    codes = dest[...]
    to_me = (codes >> 4) == member
    target = total(jnp.where(to_me, codes & 15, 0), 1)
    length = total(jnp.where(to_me, src_len[...], 0), 1)
    lane = iota((SEQ_DEV, SLOTS), 1)
    own = (lane >> 4) == iota((SEQ_DEV, SLOTS), 0)
    target = total(jnp.where(own, target, 0.0), 0)
    length = total(jnp.where(own, length, 0.0), 0)
    step = (iota((1, SLOTS), 1) & 15).astype(F32)
    target = jnp.where(step < length, target, -1.0)
    return mine == target


def forward_kernel(
    x_hbm, gain_hbm, cot_hbm, a_hbm, b_hbm, keep_ref, send_ref, *rest
):
    by_x, by_z = rest[:RING], rest[RING : 2 * RING]
    x_ref, gain_ref, a_buf, b_buf, normed_ref, left_ref, in_sem, a_sem, b_sem, out_sem = rest[2 * RING :]
    count, step, cols = a_buf.shape
    core = lax.axis_index("section")
    get_x = pltpu.make_async_copy(x_hbm, x_ref, in_sem.at[0])
    get_gain = pltpu.make_async_copy(gain_hbm, gain_ref, in_sem.at[1])
    get_left = pltpu.make_async_copy(cot_hbm, left_ref, in_sem.at[2])
    get_x.start()
    get_gain.start()

    @pl.when(core != 0)
    def _():
        get_left.start()

    def fetch(k):
        rows = pl.ds(k * step, step)
        return (
            pltpu.make_async_copy(a_hbm.at[rows, :], a_buf.at[k], a_sem.at[k]),
            pltpu.make_async_copy(b_hbm.at[rows, :], b_buf.at[k], b_sem.at[k]),
        )

    for k in range(count):
        for copy in fetch(k):
            copy.start()
    get_x.wait()
    get_gain.wait()
    xf = x_ref[...].astype(F32)
    scale = lax.rsqrt(jnp.mean(xf * xf, axis=-1, keepdims=True) + EPS)
    normed_ref[...] = (xf * scale * gain_ref[...]).astype(BF16)

    @pl.when(core == 0)
    def _():
        left_ref[...] = normed_ref[...]

    @pl.when(core != 0)
    def _():
        get_left.wait()

    z, x = lax.axis_index("z"), lax.axis_index("x")
    block = cols // RING
    copies = []
    for k in range(RING):
        for j in range(RING):
            to = slice(j * block, (j + 1) * block)
            at_x = ((z + j) % RING * RING + (x + k) % RING) * block
            at_z = ((z + k) % RING * RING + (x + j) % RING) * block
            for source, at, out in ((normed_ref, at_x, by_x[k]), (left_ref, at_z, by_z[k])):
                copies.append(
                    pltpu.make_async_copy(
                        source.at[:, pl.ds(pl.multiple_of(at, block), block)],
                        out.at[:, to],
                        out_sem.at[len(copies)],
                    )
                )
                copies[-1].start()

    acc_a = acc_b = None
    for k in range(count):
        for copy in fetch(k):
            copy.wait()
        at = slice(k * step, (k + 1) * step)
        part_a = jnp.dot(normed_ref[:, at], a_buf[k], preferred_element_type=F32)
        part_b = jnp.dot(left_ref[:, at], b_buf[k], preferred_element_type=F32)
        acc_a = part_a if acc_a is None else acc_a + part_a
        acc_b = part_b if acc_b is None else acc_b + part_b
    half = cols // 2
    parts = [[acc[:, i * half : (i + 1) * half].astype(BF16) for acc in (acc_a, acc_b)] for i in range(2)]

    def put(ref, pieces):
        ref[:, :half] = pieces[0]
        ref[:, half:] = pieces[1]

    @pl.when(core == 0)
    def _():
        put(keep_ref, parts[0])
        put(send_ref, parts[1])

    @pl.when(core != 0)
    def _():
        put(keep_ref, parts[1])
        put(send_ref, parts[0])

    for copy in copies:
        copy.wait()


def forward(x, gain, cot, weight_a, weight_b):
    rows, width = x.shape
    cols = weight_a.shape[1]
    step = 512
    count = width // step
    half = jax.ShapeDtypeStruct((rows, cols), BF16)
    outs = pl.pallas_call(
        forward_kernel,
        in_specs=[HBM] * 5,
        out_specs=[VMEM] * 2 + [HBM] * (2 * RING),
        out_shape=[half] * 2 + [pltpu.HBM((rows, cols), BF16)] * (2 * RING),
        scratch_shapes=[pltpu.VMEM((rows, width), BF16), pltpu.VMEM((1, width), F32)]
        + [pltpu.VMEM((count, step, cols), BF16)] * 2
        + [pltpu.VMEM((rows, width), BF16)] * 2
        + [pltpu.SemaphoreType.DMA((3,))]
        + [pltpu.SemaphoreType.DMA((count,))] * 2
        + [pltpu.SemaphoreType.DMA((2 * RING * RING,))],
        compiler_params=params(32),
        cost_estimate=cost(4 * rows * width * cols, 4 * width * cols),
        name="forward",
    )(in_hbm(x), in_hbm(gain), in_hbm(cot), in_hbm(weight_a), in_hbm(weight_b))
    return outs[0], outs[1], outs[2 : 2 + RING], outs[2 + RING :]


def pack_kernel(keep_ref, got_ref, src_ref, dest_ref, out_ref):
    spread = slot_onehot(member_index(), src_ref, dest_ref)

    @pl.when(lax.axis_index("section") == 0)
    def _():
        out_ref[...] = jnp.dot(spread, keep_ref[...], preferred_element_type=F32).astype(BF16)

    @pl.when(lax.axis_index("section") != 0)
    def _():
        out_ref[...] = jnp.dot(spread, got_ref[...], preferred_element_type=F32).astype(BF16)


def pack(keep, got, src_len, dest):
    width = keep.shape[1]
    return pl.pallas_call(
        pack_kernel,
        in_specs=[VMEM] * 4,
        out_specs=VMEM,
        out_shape=jax.ShapeDtypeStruct((SLOTS, width), BF16),
        compiler_params=params(),
        cost_estimate=cost(2 * SLOTS * TOK * width, 2 * SLOTS * width),
        name="pack",
    )(keep, got, src_len, dest)


def attend_kernel(
    keep_ref, got_ref, slots_ref, src_ref, tgt_ref, dest_ref, front_ref, back_ref, own_ref
):
    mask = pair_mask(member_index(), src_ref, tgt_ref, dest_ref)

    @pl.when(lax.axis_index("section") == 0)
    def _():
        own_ref[...] = got_ref[...]

    @pl.when(lax.axis_index("section") != 0)
    def _():
        own_ref[...] = keep_ref[...]

    half = own_ref.shape[1] // 2
    pair = 2 * HEAD_DIM
    low = iota((1, pair), 1) < HEAD_DIM
    nothing = jnp.zeros((), BF16)

    def both(value):
        return jnp.concatenate(
            [jnp.where(low, value, nothing), jnp.where(low, nothing, value)], axis=0
        )

    def nt(left, right):
        return lax.dot_general(left, right, (((1,), (1,)), ((), ())), preferred_element_type=F32)

    def tn(left, right):
        return lax.dot_general(left, right, (((0,), (0,)), ((), ())), preferred_element_type=F32)

    def one(score, dweight):
        expo = jnp.where(mask, jnp.exp(score), 0.0)
        weight = expo * (1.0 / jnp.sum(expo, axis=-1, keepdims=True))
        mean = jnp.sum(weight * dweight, axis=-1, keepdims=True)
        return weight.astype(BF16), (weight * (dweight - mean)).astype(BF16)

    def fold(value):
        return jnp.where(low, value[:SLOTS], value[SLOTS:]).astype(BF16)

    for p in range(half // pair):
        first = slice(p * pair, (p + 1) * pair)
        second = slice(half + p * pair, half + (p + 1) * pair)
        query, dout = own_ref[:, first], own_ref[:, second]
        keys, values = both(slots_ref[:, first]), both(slots_ref[:, second])
        score, dweight = nt(query, keys), nt(dout, values)
        weight_0, dscore_0 = one(score[:, :SLOTS], dweight[:, :SLOTS])
        weight_1, dscore_1 = one(score[:, SLOTS:], dweight[:, SLOTS:])
        weight = jnp.concatenate([weight_0, weight_1], axis=1)
        dscore = jnp.concatenate([dscore_0, dscore_1], axis=1)
        front_ref[:, first] = jnp.dot(dscore, keys, preferred_element_type=F32).astype(BF16)
        front_ref[:, second] = jnp.dot(weight, values, preferred_element_type=F32).astype(BF16)
        back_ref[:, first] = fold(tn(dscore, query))
        back_ref[:, second] = fold(tn(weight, dout))


def attend(keep, got, slots, src_len, tgt_len, dest):
    rows, width = keep.shape
    return pl.pallas_call(
        attend_kernel,
        in_specs=[VMEM] * 6,
        out_specs=[VMEM] * 2,
        out_shape=[
            jax.ShapeDtypeStruct((rows, width), BF16),
            jax.ShapeDtypeStruct((SLOTS, width), BF16),
        ],
        scratch_shapes=[pltpu.VMEM((rows, width), BF16)],
        compiler_params=params(),
        cost_estimate=cost(24 * rows * SLOTS * width, 8 * SLOTS * width),
        name="attend",
    )(keep, got, slots, src_len, tgt_len, dest)


def unpack_kernel(back_ref, front_ref, src_ref, dest_ref, keep_ref, send_ref):
    spread = slot_onehot(member_index(), src_ref, dest_ref)
    rows = lax.dot_general(
        spread, back_ref[...], (((0,), (0,)), ((), ())), preferred_element_type=F32
    ).astype(BF16)

    @pl.when(lax.axis_index("section") == 0)
    def _():
        keep_ref[...] = rows
        send_ref[...] = front_ref[...]

    @pl.when(lax.axis_index("section") != 0)
    def _():
        keep_ref[...] = front_ref[...]
        send_ref[...] = rows


def unpack(back, front, src_len, dest):
    width = front.shape[1]
    half = jax.ShapeDtypeStruct((TOK, width), BF16)
    return pl.pallas_call(
        unpack_kernel,
        in_specs=[VMEM] * 4,
        out_specs=[VMEM] * 2,
        out_shape=[half, half],
        compiler_params=params(),
        cost_estimate=cost(2 * SLOTS * TOK * width, 4 * SLOTS * width),
        name="unpack",
    )(back, front, src_len, dest)


def join_kernel(keep_ref, got_ref, first_ref, second_ref):
    half = keep_ref.shape[1] // 2
    mine = pl.multiple_of(lax.axis_index("section") * half, half)
    other = pl.multiple_of((1 - lax.axis_index("section")) * half, half)
    first_ref[:, pl.ds(mine, half)] = keep_ref[:, :half]
    first_ref[:, pl.ds(other, half)] = got_ref[:, :half]
    second_ref[:, pl.ds(mine, half)] = keep_ref[:, half:]
    second_ref[:, pl.ds(other, half)] = got_ref[:, half:]


def join(keep, got):
    shape = jax.ShapeDtypeStruct(keep.shape, BF16)
    return pl.pallas_call(
        join_kernel,
        in_specs=[VMEM, VMEM],
        out_specs=[VMEM] * 2,
        out_shape=[shape, shape],
        compiler_params=params(),
        cost_estimate=cost(0, 8 * keep.size),
        name="join",
    )(keep, got)


def dnorm_kernel(first_ref, second_ref, a_hbm, b_hbm, out_ref, a_buf, b_buf, a_sem, b_sem):
    count, step, _ = a_buf.shape
    source = lax.axis_index("section") == 0

    def nt(left, right):
        return lax.dot_general(left, right, (((1,), (1,)), ((), ())), preferred_element_type=F32)

    def fetch(k):
        rows = pl.ds(k * step, step)
        return (
            pltpu.make_async_copy(a_hbm.at[rows, :], a_buf.at[k], a_sem.at[k]),
            pltpu.make_async_copy(b_hbm.at[rows, :], b_buf.at[k], b_sem.at[k]),
        )

    for k in range(count):
        for copy in fetch(k):
            copy.start()
    for k in range(count):
        at = slice(k * step, (k + 1) * step)
        for copy in fetch(k):
            copy.wait()

        @pl.when(source)
        def _(k=k, at=at):
            out_ref[:, at] = (
                nt(first_ref[...], a_buf[k]) + nt(second_ref[...], b_buf[k])
            ).astype(BF16)

        @pl.when(jnp.logical_not(source))
        def _(k=k, at=at):
            out_ref[:, at] = nt(first_ref[...], a_buf[k]).astype(BF16)


def dnorm_partial(first, second, weight_a, weight_b):
    rows, cols = first.shape
    width = weight_a.shape[0]
    step = 512
    count = width // step
    return pl.pallas_call(
        dnorm_kernel,
        in_specs=[VMEM] * 2 + [HBM] * 2,
        out_specs=VMEM,
        out_shape=jax.ShapeDtypeStruct((rows, width), BF16),
        scratch_shapes=[pltpu.VMEM((count, step, cols), BF16)] * 2
        + [pltpu.SemaphoreType.DMA((count,))] * 2,
        compiler_params=params(24),
        cost_estimate=cost(4 * rows * width * cols, 4 * width * cols),
        name="dnorm",
    )(first, second, in_hbm(weight_a), in_hbm(weight_b))


def rms_back_kernel(x_hbm, gain_ref, parts_ref, out_ref, x_ref, sem):
    rows = out_ref.shape[0]
    mine = pl.multiple_of(lax.axis_index("mp") * rows, rows)
    get_x = pltpu.make_async_copy(x_hbm.at[pl.ds(mine, rows), :], x_ref, sem)
    get_x.start()
    dnorm = parts_ref[0].astype(F32)
    for i in range(1, RING):
        dnorm += parts_ref[i].astype(F32)
    get_x.wait()
    xf = x_ref[...].astype(F32)
    scale = lax.rsqrt(jnp.mean(xf * xf, axis=-1, keepdims=True) + EPS)
    upper = gain_ref[...] * dnorm
    inner = jnp.mean(xf * upper, axis=-1, keepdims=True)
    out_ref[...] = (scale * upper - xf * (scale * scale * scale * inner)).astype(BF16)


def rms_back(x, gain, parts):
    rows, width = parts.shape[1:]
    return pl.pallas_call(
        rms_back_kernel,
        in_specs=[HBM] + [VMEM] * 2,
        out_specs=VMEM,
        out_shape=jax.ShapeDtypeStruct((rows, width), BF16),
        scratch_shapes=[pltpu.VMEM((rows, width), BF16), pltpu.SemaphoreType.DMA],
        compiler_params=params(),
        cost_estimate=cost(10 * rows * width, 12 * rows * width),
        name="rms_back",
    )(in_hbm(x), gain, parts)


def place_kernel(own_ref, left_ref, right_ref, far_ref, out_ref):
    rows = own_ref.shape[0]
    for k, ref in ((0, own_ref), (3, left_ref), (1, right_ref), (2, far_ref)):
        at = (lax.axis_index("mp") + k) % RING * rows
        out_ref[pl.ds(pl.multiple_of(at, rows), rows), :] = ref[...]


def place(pieces):
    rows, width = pieces[0].shape
    return pl.pallas_call(
        place_kernel,
        in_specs=[VMEM] * 4,
        out_specs=VMEM,
        out_shape=jax.ShapeDtypeStruct((RING * rows, width), BF16),
        compiler_params=params(),
        cost_estimate=cost(0, 4 * RING * rows * width),
        name="place",
    )(*pieces)


def shift(value, axis, k):
    return lax.ppermute(value, axis, [(i, (i + k) % RING) for i in range(RING)])


def gathered(block, axis):
    left = shift(block, axis, 1)
    return [block, left, shift(block, axis, 3), shift(left, axis, 1)]


def spread(block, axis):
    far = shift(block, axis, 2)
    return [block, shift(block, axis, 1), shift(block, axis, 3), far]


def exchanged(slices, axis):
    return [shift(slices[1], axis, 1), shift(slices[3], axis, 3)], shift(slices[2], axis, 2)


def turn_kernel(*refs):
    pieces, (out_hbm, in_buf, out_buf, in_sem, out_sem) = refs[:RING], refs[RING:]
    block, rows = out_buf.shape[1], pieces[0].shape[0]
    loads = [pltpu.make_async_copy(pieces[p], in_buf.at[p], in_sem.at[p]) for p in range(RING)]
    for load in loads:
        load.start()
    for load in loads:
        load.wait()
    stores = []
    for k in range(RING):
        for p in range(RING):
            turned_block = in_buf[p, :, k * block : (k + 1) * block].T
            out_buf[k, :, p * rows : (p + 1) * rows] = turned_block
        stores.append(pltpu.make_async_copy(out_buf.at[k], out_hbm.at[k], out_sem.at[k]))
        stores[-1].start()
    for store in stores:
        store.wait()


def turned(pieces):
    rows, width = pieces[0].shape
    shape = (RING, width // RING, RING * rows)
    return pl.pallas_call(
        turn_kernel,
        in_specs=[HBM] * RING,
        out_specs=HBM,
        out_shape=pltpu.HBM(shape, BF16),
        scratch_shapes=[pltpu.VMEM((RING, rows, width), BF16), pltpu.VMEM(shape, BF16)]
        + [pltpu.SemaphoreType.DMA((RING,))] * 2,
        compiler_params=params(),
        cost_estimate=cost(0, 4 * RING * rows * width),
        name="turn",
    )(*[in_hbm(piece) for piece in pieces])


def far_kernel(left_hbm, own_ref, near_ref, next_ref, far_ref, top_ref, low_ref, rows_ref, left, sem):
    load = pltpu.make_async_copy(left_hbm.at[2], left, sem)
    load.start()
    rows = own_ref.shape[0]
    for p, piece in enumerate((own_ref, near_ref, next_ref, far_ref)):
        rows_ref[p * rows : (p + 1) * rows, :] = piece[...]
    load.wait()
    half = top_ref.shape[0]
    for i, out in enumerate((top_ref, low_ref)):
        out[...] = jnp.dot(
            left[i * half : (i + 1) * half, :], rows_ref[...], preferred_element_type=F32
        ).astype(BF16)


def far_block(left, pieces):
    rows, cols = pieces[0].shape
    _, block, depth = left.shape
    half = jax.ShapeDtypeStruct((block // 2, cols), BF16)
    return pl.pallas_call(
        far_kernel,
        in_specs=[HBM] + [VMEM] * RING,
        out_specs=[VMEM] * 3,
        out_shape=[half, half, jax.ShapeDtypeStruct((RING * rows, cols), BF16)],
        scratch_shapes=[pltpu.VMEM((block, depth), BF16), pltpu.SemaphoreType.DMA],
        compiler_params=params(),
        cost_estimate=cost(2 * RING * rows * block * cols, 8 * RING * rows * cols),
        name="far",
    )(in_hbm(left), *pieces)


def side_kernel(left_hbm, rows_ref, from_left_ref, from_right_ref, right_out, left_out, left, sems):
    loads = [pltpu.make_async_copy(left_hbm.at[k], left.at[i], sems.at[i]) for i, k in enumerate((1, 3))]
    for load in loads:
        load.start()
    half = from_left_ref.shape[0]

    def product(i):
        loads[i].wait()
        return jnp.dot(left[i], rows_ref[...], preferred_element_type=F32)

    block = product(0)
    right_out[:half, :] = (block[:half] + from_left_ref[...].astype(F32)).astype(BF16)
    right_out[half:, :] = block[half:].astype(BF16)
    block = product(1)
    left_out[:half, :] = block[:half].astype(BF16)
    left_out[half:, :] = (block[half:] + from_right_ref[...].astype(F32)).astype(BF16)


def side_blocks(left, rows, from_left, from_right):
    _, block, depth = left.shape
    cols = rows.shape[1]
    shape = jax.ShapeDtypeStruct((block, cols), BF16)
    return pl.pallas_call(
        side_kernel,
        in_specs=[HBM] + [VMEM] * 3,
        out_specs=[VMEM] * 2,
        out_shape=[shape, shape],
        scratch_shapes=[pltpu.VMEM((2, block, depth), BF16), pltpu.SemaphoreType.DMA((2,))],
        compiler_params=params(),
        cost_estimate=cost(4 * rows.shape[0] * block * cols, 4 * rows.size),
        name="side",
    )(in_hbm(left), rows, from_left, from_right)


def own_kernel(left_hbm, rows_ref, a_ref, b_ref, out_ref, left, sem):
    load = pltpu.make_async_copy(left_hbm.at[0], left, sem)
    load.start()
    load.wait()
    block = jnp.dot(left[...], rows_ref[...], preferred_element_type=F32)
    out_ref[...] = block + a_ref[...].astype(F32) + b_ref[...].astype(F32)


def own_block(left, rows, a, b):
    _, block, depth = left.shape
    cols = rows.shape[1]
    return pl.pallas_call(
        own_kernel,
        in_specs=[HBM] + [VMEM] * 3,
        out_specs=VMEM,
        out_shape=jax.ShapeDtypeStruct((block, cols), F32),
        scratch_shapes=[pltpu.VMEM((block, depth), BF16), pltpu.SemaphoreType.DMA],
        compiler_params=params(),
        cost_estimate=cost(2 * rows.shape[0] * block * cols, 8 * rows.size),
        name="own",
    )(in_hbm(left), rows, a, b)


def reduced(left, pieces, axis):
    top, low, rows = far_block(left, pieces)
    from_left, from_right = shift(top, axis, 1), shift(low, axis, 3)
    to_right, to_left = side_blocks(left, rows, from_left, from_right)
    return own_block(left, rows, shift(to_right, axis, 1), shift(to_left, axis, 3))


def per_device(states, gains, proj_a, proj_b, cotangent, src_len, tgt_len, dest):
    weight_a = proj_a[0]
    weight_b = proj_b[0]
    rows = states[0]
    keep, send, by_x, by_z = forward(rows, gains, cotangent, weight_a, weight_b)
    swap = [(0, 1), (1, 0)]
    got = lax.ppermute(send, "section", swap)
    slots = pack(keep, got, src_len, dest)
    width = slots.shape[1]
    slots = slots.reshape(SEQ_DEV, MAXLEN, width)
    slots = lax.all_to_all(slots, ("z", "x"), split_axis=0, concat_axis=0, tiled=True)
    slots = slots.reshape(SLOTS, width)
    (near_a, far_a), (near_b, far_b) = exchanged(by_x, "x"), exchanged(by_z, "z")
    slots, near_a, near_b = lax.optimization_barrier((slots, near_a, near_b))
    front, back = attend(keep, got, slots, src_len, tgt_len, dest)
    back = back.reshape(SEQ_DEV, MAXLEN, width)
    back = lax.all_to_all(back, ("z", "x"), split_axis=0, concat_axis=0, tiled=True)
    left_a, left_b = turned([by_x[0], *near_a, far_a]), turned([by_z[0], *near_b, far_b])
    back, left_a, left_b = lax.optimization_barrier((back, left_a, left_b))
    keep, send = unpack(back.reshape(SLOTS, width), front, src_len, dest)
    got = lax.ppermute(send, "section", swap)
    first, second = join(keep, got)

    rights_a, rights_b = spread(first, "x"), spread(second, "z")
    partial = dnorm_partial(first, second, weight_a, weight_b)
    parts = lax.all_to_all(
        partial.reshape(RING, TOK // RING, -1), "mp", split_axis=0, concat_axis=0, tiled=True
    )
    quarter = rms_back(rows, gains, parts)
    grad_states = place(gathered(quarter, "mp"))

    grad_a = reduced(left_a, rights_a, "z")
    grad_b = reduced(left_b, rights_b, "x")
    return (grad_states[None], grad_a[None], grad_b[None])


def solution(mesh):
    split = jax.sharding.Mesh(mesh.devices.reshape(2, RING, RING, RING), ("section", "z", "x", "mp"))
    dp = ("z", "x")
    return jax.shard_map(
        per_device,
        mesh=split,
        in_specs=(
            P("section", dp, None),
            P("section", None),
            P("section", None, "mp"),
            P("section", None, "mp"),
            P(dp, None),
            P(),
            P(),
            P(),
        ),
        out_specs=(P("section", dp, None), P("section", dp, "mp"), P("section", dp, "mp")),
        check_vma=False,
    )
```

```python
import jax
import jax.numpy as jnp
from jax import lax
from jax.experimental import pallas as pl
from jax.experimental.pallas import tpu as pltpu
from jax.sharding import PartitionSpec as P

HEAD_DIM = 64
SEQ_DEV = 16
MAXLEN = 16
TOK = 128
SLOTS = 256
RING = 4
QUARTER = TOK // RING
ORDER = (0, 3, 1, 2)
EPS = 1e-06
F32 = jnp.float32
BF16 = jnp.bfloat16
VMEM = pl.BlockSpec(memory_space=pltpu.VMEM)
ANY = pl.BlockSpec(memory_space=pl.ANY)
HBM = pl.BlockSpec(memory_space=pltpu.HBM)


def iota(shape, dim):
    return lax.broadcasted_iota(jnp.int32, shape, dim)


def total(value, axis):
    return jnp.sum(value.astype(F32), axis=axis, keepdims=True)


def in_hbm(value):
    return pltpu.with_memory_space_constraint(value, pltpu.HBM)


def cost(flops, nbytes):
    return pl.CostEstimate(flops=flops, bytes_accessed=nbytes, transcendentals=0)


def params(mib=12, **more):
    return pltpu.CompilerParams(vmem_limit_bytes=mib << 20, **more)


def column_of(row):
    square = jnp.broadcast_to(row, (SEQ_DEV, SEQ_DEV))
    same = iota((SEQ_DEV, SEQ_DEV), 0) == iota((SEQ_DEV, SEQ_DEV), 1)
    return total(jnp.where(same, square, 0), 1)


def member_index():
    return lax.axis_index("z") * RING + lax.axis_index("x")


def slot_onehot(member, src_len, dest):
    i, j = iota((SEQ_DEV, SEQ_DEV), 0), iota((SEQ_DEV, SEQ_DEV), 1)
    lengths = src_len[pl.ds(member, 1), :]
    ends = total(jnp.where(j <= i, jnp.broadcast_to(lengths, (SEQ_DEV, SEQ_DEV)), 0), 1)
    begins = ends - column_of(lengths)
    place = column_of(dest[pl.ds(member, 1), :] >> 4) * MAXLEN
    row = iota((SEQ_DEV, TOK), 1).astype(F32)
    inside = (row >= begins) & (row < ends)
    target = total(jnp.where(inside, place + row - begins, 0.0), 0)
    hit = iota((SLOTS, TOK), 0).astype(F32) == target
    return jnp.where(hit, 1.0, 0.0).astype(BF16)


def pair_mask(member, src_len, tgt_len, dest):
    i, j = iota((SEQ_DEV, SEQ_DEV), 0), iota((SEQ_DEV, SEQ_DEV), 1)
    column = column_of(tgt_len[pl.ds(member, 1), :])
    ends = total(jnp.where(i <= j, jnp.broadcast_to(column, (SEQ_DEV, SEQ_DEV)), 0.0), 0)
    row = iota((TOK, SEQ_DEV), 0).astype(F32)
    mine = total(jnp.where(row >= ends, 1.0, 0.0), 1)
    codes = dest[...]
    to_me = (codes >> 4) == member
    target = total(jnp.where(to_me, codes & 15, 0), 1)
    length = total(jnp.where(to_me, src_len[...], 0), 1)
    lane = iota((SEQ_DEV, SLOTS), 1)
    own = (lane >> 4) == iota((SEQ_DEV, SLOTS), 0)
    target = total(jnp.where(own, target, 0.0), 0)
    length = total(jnp.where(own, length, 0.0), 0)
    step = (iota((1, SLOTS), 1) & 15).astype(F32)
    target = jnp.where(step < length, target, -1.0)
    return mine == target


def forward_kernel(
    x_hbm, gain_hbm, cot_hbm, a_hbm, b_hbm, keep_ref, send_ref, *rest
):
    by_x, by_z = rest[:RING], rest[RING : 2 * RING]
    x_ref, gain_ref, a_buf, b_buf, normed_ref, left_ref, in_sem, a_sem, b_sem, out_sem = rest[2 * RING :]
    count, step, cols = a_buf.shape
    core = lax.axis_index("section")
    get_x = pltpu.make_async_copy(x_hbm, x_ref, in_sem.at[0])
    get_gain = pltpu.make_async_copy(gain_hbm, gain_ref, in_sem.at[1])
    get_left = pltpu.make_async_copy(cot_hbm, left_ref, in_sem.at[2])
    get_x.start()
    get_gain.start()

    @pl.when(core != 0)
    def _():
        get_left.start()

    def fetch(k):
        rows = pl.ds(k * step, step)
        return (
            pltpu.make_async_copy(a_hbm.at[rows, :], a_buf.at[k], a_sem.at[k]),
            pltpu.make_async_copy(b_hbm.at[rows, :], b_buf.at[k], b_sem.at[k]),
        )

    for k in range(count):
        for copy in fetch(k):
            copy.start()
    get_x.wait()
    get_gain.wait()
    xf = x_ref[...].astype(F32)
    scale = lax.rsqrt(jnp.mean(xf * xf, axis=-1, keepdims=True) + EPS)
    normed_ref[...] = (xf * scale * gain_ref[...]).astype(BF16)

    @pl.when(core == 0)
    def _():
        left_ref[...] = normed_ref[...]

    @pl.when(core != 0)
    def _():
        get_left.wait()

    z, x = lax.axis_index("z"), lax.axis_index("x")
    quarter = pl.ds(pl.multiple_of(lax.axis_index("mp") * QUARTER, QUARTER), QUARTER)
    block = cols // RING
    copies = []
    for k in range(RING):
        for j in range(RING):
            to = slice(j * block, (j + 1) * block)
            at_x = ((z + j) % RING * RING + (x + k) % RING) * block
            at_z = ((z + k) % RING * RING + (x + j) % RING) * block
            for source, at, out in ((normed_ref, at_x, by_x[k]), (left_ref, at_z, by_z[k])):
                copies.append(
                    pltpu.make_async_copy(
                        source.at[quarter, pl.ds(pl.multiple_of(at, block), block)],
                        out.at[:, to],
                        out_sem.at[len(copies)],
                    )
                )
                copies[-1].start()

    acc_a = acc_b = None
    for k in range(count):
        for copy in fetch(k):
            copy.wait()
        at = slice(k * step, (k + 1) * step)
        part_a = jnp.dot(normed_ref[:, at], a_buf[k], preferred_element_type=F32)
        part_b = jnp.dot(left_ref[:, at], b_buf[k], preferred_element_type=F32)
        acc_a = part_a if acc_a is None else acc_a + part_a
        acc_b = part_b if acc_b is None else acc_b + part_b
    half = cols // 2
    parts = [[acc[:, i * half : (i + 1) * half].astype(BF16) for acc in (acc_a, acc_b)] for i in range(2)]

    def put(ref, pieces):
        ref[:, :half] = pieces[0]
        ref[:, half:] = pieces[1]

    @pl.when(core == 0)
    def _():
        put(keep_ref, parts[0])
        put(send_ref, parts[1])

    @pl.when(core != 0)
    def _():
        put(keep_ref, parts[1])
        put(send_ref, parts[0])

    for copy in copies:
        copy.wait()


def forward(x, gain, cot, weight_a, weight_b):
    rows, width = x.shape
    cols = weight_a.shape[1]
    step = 512
    count = width // step
    half = jax.ShapeDtypeStruct((rows, cols), BF16)
    outs = pl.pallas_call(
        forward_kernel,
        in_specs=[HBM] * 5,
        out_specs=[VMEM] * 2 + [HBM] * (2 * RING),
        out_shape=[half] * 2 + [pltpu.HBM((QUARTER, cols), BF16)] * (2 * RING),
        scratch_shapes=[pltpu.VMEM((rows, width), BF16), pltpu.VMEM((1, width), F32)]
        + [pltpu.VMEM((count, step, cols), BF16)] * 2
        + [pltpu.VMEM((rows, width), BF16)] * 2
        + [pltpu.SemaphoreType.DMA((3,))]
        + [pltpu.SemaphoreType.DMA((count,))] * 2
        + [pltpu.SemaphoreType.DMA((2 * RING * RING,))],
        compiler_params=params(32),
        cost_estimate=cost(4 * rows * width * cols, 4 * width * cols),
        name="forward",
    )(in_hbm(x), in_hbm(gain), in_hbm(cot), in_hbm(weight_a), in_hbm(weight_b))
    return outs[0], outs[1], outs[2 : 2 + RING], outs[2 + RING :]


def pack_kernel(keep_ref, got_ref, src_ref, dest_ref, out_ref):
    spread = slot_onehot(member_index(), src_ref, dest_ref)

    @pl.when(lax.axis_index("section") == 0)
    def _():
        out_ref[...] = jnp.dot(spread, keep_ref[...], preferred_element_type=F32).astype(BF16)

    @pl.when(lax.axis_index("section") != 0)
    def _():
        out_ref[...] = jnp.dot(spread, got_ref[...], preferred_element_type=F32).astype(BF16)


def pack(keep, got, src_len, dest):
    width = keep.shape[1]
    return pl.pallas_call(
        pack_kernel,
        in_specs=[VMEM] * 4,
        out_specs=VMEM,
        out_shape=jax.ShapeDtypeStruct((SLOTS, width), BF16),
        compiler_params=params(),
        cost_estimate=cost(2 * SLOTS * TOK * width, 2 * SLOTS * width),
        name="pack",
    )(keep, got, src_len, dest)


def attend_kernel(
    keep_ref, got_ref, slots_ref, src_ref, tgt_ref, dest_ref, front_ref, back_ref, own_ref
):
    mask = pair_mask(member_index(), src_ref, tgt_ref, dest_ref)

    @pl.when(lax.axis_index("section") == 0)
    def _():
        own_ref[...] = got_ref[...]

    @pl.when(lax.axis_index("section") != 0)
    def _():
        own_ref[...] = keep_ref[...]

    half = own_ref.shape[1] // 2
    pair = 2 * HEAD_DIM
    low = iota((1, pair), 1) < HEAD_DIM
    nothing = jnp.zeros((), BF16)

    def both(value):
        return jnp.concatenate(
            [jnp.where(low, value, nothing), jnp.where(low, nothing, value)], axis=0
        )

    def nt(left, right):
        return lax.dot_general(left, right, (((1,), (1,)), ((), ())), preferred_element_type=F32)

    def tn(left, right):
        return lax.dot_general(left, right, (((0,), (0,)), ((), ())), preferred_element_type=F32)

    def one(score, dweight):
        expo = jnp.where(mask, jnp.exp(score), 0.0)
        weight = expo * (1.0 / jnp.sum(expo, axis=-1, keepdims=True))
        mean = jnp.sum(weight * dweight, axis=-1, keepdims=True)
        return weight.astype(BF16), (weight * (dweight - mean)).astype(BF16)

    def fold(value):
        return jnp.where(low, value[:SLOTS], value[SLOTS:]).astype(BF16)

    for p in range(half // pair):
        first = slice(p * pair, (p + 1) * pair)
        second = slice(half + p * pair, half + (p + 1) * pair)
        query, dout = own_ref[:, first], own_ref[:, second]
        keys, values = both(slots_ref[:, first]), both(slots_ref[:, second])
        score, dweight = nt(query, keys), nt(dout, values)
        weight_0, dscore_0 = one(score[:, :SLOTS], dweight[:, :SLOTS])
        weight_1, dscore_1 = one(score[:, SLOTS:], dweight[:, SLOTS:])
        weight = jnp.concatenate([weight_0, weight_1], axis=1)
        dscore = jnp.concatenate([dscore_0, dscore_1], axis=1)
        front_ref[:, first] = jnp.dot(dscore, keys, preferred_element_type=F32).astype(BF16)
        front_ref[:, second] = jnp.dot(weight, values, preferred_element_type=F32).astype(BF16)
        back_ref[:, first] = fold(tn(dscore, query))
        back_ref[:, second] = fold(tn(weight, dout))


def attend(keep, got, slots, src_len, tgt_len, dest):
    rows, width = keep.shape
    return pl.pallas_call(
        attend_kernel,
        in_specs=[VMEM] * 6,
        out_specs=[VMEM] * 2,
        out_shape=[
            jax.ShapeDtypeStruct((rows, width), BF16),
            jax.ShapeDtypeStruct((SLOTS, width), BF16),
        ],
        scratch_shapes=[pltpu.VMEM((rows, width), BF16)],
        compiler_params=params(),
        cost_estimate=cost(24 * rows * SLOTS * width, 8 * SLOTS * width),
        name="attend",
    )(keep, got, slots, src_len, tgt_len, dest)


def unpack_kernel(back_ref, front_ref, src_ref, dest_ref, keep_ref, send_ref):
    spread = slot_onehot(member_index(), src_ref, dest_ref)
    rows = lax.dot_general(
        spread, back_ref[...], (((0,), (0,)), ((), ())), preferred_element_type=F32
    ).astype(BF16)

    @pl.when(lax.axis_index("section") == 0)
    def _():
        keep_ref[...] = rows
        send_ref[...] = front_ref[...]

    @pl.when(lax.axis_index("section") != 0)
    def _():
        keep_ref[...] = front_ref[...]
        send_ref[...] = rows


def unpack(back, front, src_len, dest):
    width = front.shape[1]
    half = jax.ShapeDtypeStruct((TOK, width), BF16)
    return pl.pallas_call(
        unpack_kernel,
        in_specs=[VMEM] * 4,
        out_specs=[VMEM] * 2,
        out_shape=[half, half],
        compiler_params=params(),
        cost_estimate=cost(2 * SLOTS * TOK * width, 4 * SLOTS * width),
        name="unpack",
    )(back, front, src_len, dest)


def join_kernel(keep_ref, got_ref, first_ref, second_ref):
    half = keep_ref.shape[1] // 2
    mine = pl.multiple_of(lax.axis_index("section") * half, half)
    other = pl.multiple_of((1 - lax.axis_index("section")) * half, half)
    first_ref[:, pl.ds(mine, half)] = keep_ref[:, :half]
    first_ref[:, pl.ds(other, half)] = got_ref[:, :half]
    second_ref[:, pl.ds(mine, half)] = keep_ref[:, half:]
    second_ref[:, pl.ds(other, half)] = got_ref[:, half:]


def join(keep, got):
    shape = jax.ShapeDtypeStruct(keep.shape, BF16)
    return pl.pallas_call(
        join_kernel,
        in_specs=[VMEM, VMEM],
        out_specs=[VMEM] * 2,
        out_shape=[shape, shape],
        compiler_params=params(),
        cost_estimate=cost(0, 8 * keep.size),
        name="join",
    )(keep, got)


def dnorm_kernel(first_ref, second_ref, a_hbm, b_hbm, out_ref, a_buf, b_buf, a_sem, b_sem):
    count, step, _ = a_buf.shape
    source = lax.axis_index("section") == 0

    def nt(left, right):
        return lax.dot_general(left, right, (((1,), (1,)), ((), ())), preferred_element_type=F32)

    def fetch(k):
        rows = pl.ds(k * step, step)
        return (
            pltpu.make_async_copy(a_hbm.at[rows, :], a_buf.at[k], a_sem.at[k]),
            pltpu.make_async_copy(b_hbm.at[rows, :], b_buf.at[k], b_sem.at[k]),
        )

    for k in range(count):
        for copy in fetch(k):
            copy.start()
    for k in range(count):
        at = slice(k * step, (k + 1) * step)
        for copy in fetch(k):
            copy.wait()

        @pl.when(source)
        def _(k=k, at=at):
            out_ref[:, at] = (
                nt(first_ref[...], a_buf[k]) + nt(second_ref[...], b_buf[k])
            ).astype(BF16)

        @pl.when(jnp.logical_not(source))
        def _(k=k, at=at):
            out_ref[:, at] = nt(first_ref[...], a_buf[k]).astype(BF16)


def dnorm_partial(first, second, weight_a, weight_b):
    rows, cols = first.shape
    width = weight_a.shape[0]
    step = 512
    count = width // step
    return pl.pallas_call(
        dnorm_kernel,
        in_specs=[VMEM] * 2 + [HBM] * 2,
        out_specs=VMEM,
        out_shape=jax.ShapeDtypeStruct((rows, width), BF16),
        scratch_shapes=[pltpu.VMEM((count, step, cols), BF16)] * 2
        + [pltpu.SemaphoreType.DMA((count,))] * 2,
        compiler_params=params(24),
        cost_estimate=cost(4 * rows * width * cols, 4 * width * cols),
        name="dnorm",
    )(first, second, in_hbm(weight_a), in_hbm(weight_b))


def rms_back_kernel(x_hbm, gain_ref, parts_ref, out_ref, x_ref, sem):
    rows = out_ref.shape[0]
    mine = pl.multiple_of(lax.axis_index("mp") * rows, rows)
    get_x = pltpu.make_async_copy(x_hbm.at[pl.ds(mine, rows), :], x_ref, sem)
    get_x.start()
    dnorm = parts_ref[0].astype(F32)
    for i in range(1, RING):
        dnorm += parts_ref[i].astype(F32)
    get_x.wait()
    xf = x_ref[...].astype(F32)
    scale = lax.rsqrt(jnp.mean(xf * xf, axis=-1, keepdims=True) + EPS)
    upper = gain_ref[...] * dnorm
    inner = jnp.mean(xf * upper, axis=-1, keepdims=True)
    out_ref[...] = (scale * upper - xf * (scale * scale * scale * inner)).astype(BF16)


def rms_back(x, gain, parts):
    rows, width = parts.shape[1:]
    return pl.pallas_call(
        rms_back_kernel,
        in_specs=[HBM] + [VMEM] * 2,
        out_specs=VMEM,
        out_shape=jax.ShapeDtypeStruct((rows, width), BF16),
        scratch_shapes=[pltpu.VMEM((rows, width), BF16), pltpu.SemaphoreType.DMA],
        compiler_params=params(),
        cost_estimate=cost(10 * rows * width, 12 * rows * width),
        name="rms_back",
    )(in_hbm(x), gain, parts)


def place_kernel(*refs):
    pieces, (out_hbm, sems) = refs[:RING], refs[RING:]
    rows = pieces[0].shape[0]
    copies = []
    for i, k in enumerate(ORDER):
        at = pl.multiple_of((lax.axis_index("mp") + k) % RING * rows, rows)
        copies.append(pltpu.make_async_copy(pieces[i], out_hbm.at[pl.ds(at, rows), :], sems.at[i]))
        copies[-1].start()
    for copy in copies:
        copy.wait()


def place(pieces):
    rows, width = pieces[0].shape
    return pl.pallas_call(
        place_kernel,
        in_specs=[ANY] * RING,
        out_specs=HBM,
        out_shape=pltpu.HBM((RING * rows, width), BF16),
        scratch_shapes=[pltpu.SemaphoreType.DMA((RING,))],
        compiler_params=params(),
        cost_estimate=cost(0, 4 * RING * rows * width),
        name="place",
    )(*pieces)


def shift(value, axis, k):
    return lax.ppermute(value, axis, [(i, (i + k) % RING) for i in range(RING)])


def gathered(block, axis):
    left = shift(block, axis, 1)
    return [block, left, shift(block, axis, 3), shift(left, axis, 1)]


def spread(block, axis):
    far = shift(block, axis, 2)
    return [block, shift(block, axis, 1), shift(block, axis, 3), far]


def exchanged(slices, axis):
    far = shift(slices[2], axis, 2)
    return [slices[0], shift(slices[1], axis, 1), shift(slices[3], axis, 3), far]


def stack_kernel(*refs):
    pieces, (out_hbm, sems) = refs[:-2], refs[-2:]
    rows = pieces[0].shape[0]
    copies = [
        pltpu.make_async_copy(piece, out_hbm.at[pl.ds(i * rows, rows), :], sems.at[i])
        for i, piece in enumerate(pieces)
    ]
    for copy in copies:
        copy.start()
    for copy in copies:
        copy.wait()


def stacked(pieces):
    rows, cols = pieces[0].shape
    count = len(pieces)
    return pl.pallas_call(
        stack_kernel,
        in_specs=[ANY] * count,
        out_specs=HBM,
        out_shape=pltpu.HBM((count * rows, cols), BF16),
        scratch_shapes=[pltpu.SemaphoreType.DMA((count,))],
        compiler_params=params(),
        cost_estimate=cost(0, 4 * count * rows * cols),
        name="stack",
    )(*pieces)


def tn(left, right):
    return lax.dot_general(left, right, (((0,), (0,)), ((), ())), preferred_element_type=F32)


def left_loads(lefts, buf, sems, ks):
    block = buf.shape[-1]
    mine = lax.axis_index("mp")
    loads = [[[] for _ in ks] for _ in range(2)]
    for f in range(2):
        for i, k in enumerate(ks):
            for j, (left, distance) in enumerate(zip(lefts, ORDER, strict=True)):
                at = pl.multiple_of((mine + distance) % RING * QUARTER, QUARTER)
                loads[f][i].append(
                    pltpu.make_async_copy(
                        left.at[f, :, :, pl.ds(k * block, block)],
                        buf.at[f, i, :, pl.ds(at, QUARTER), :],
                        sems.at[f, i, j],
                    )
                )
                loads[f][i][-1].start()
    return loads


def left_scratch(block, count):
    return [
        pltpu.VMEM((2, count, RING, TOK, block), BF16),
        pltpu.SemaphoreType.DMA((2, count, RING)),
    ]


def flat(value):
    return value.reshape(RING * TOK, value.shape[-1])


def wait_all(copies):
    for copy in copies:
        copy.wait()


def far_kernel(*refs):
    lefts, pieces, outs = refs[:RING], refs[RING : 3 * RING], refs[3 * RING : 3 * RING + 4]
    rows_refs, (buf, sems, row_sems) = refs[3 * RING + 4 : 3 * RING + 6], refs[3 * RING + 6 :]
    gets = [
        pltpu.make_async_copy(
            piece, rows_refs[i // RING].at[pl.ds(i % RING * TOK, TOK), :], row_sems.at[i]
        )
        for i, piece in enumerate(pieces)
    ]
    for get in gets:
        get.start()
    loads = left_loads(lefts, buf, sems, (2,))
    half = outs[0].shape[0]
    for f in range(2):
        wait_all(gets[f * RING : (f + 1) * RING])
        wait_all(loads[f][0])
        block = tn(flat(buf[f, 0]), rows_refs[f][...]).astype(BF16)
        outs[2 * f][...] = block[:half]
        outs[2 * f + 1][...] = block[half:]


def far_blocks(lefts, pieces_a, pieces_b):
    rows, cols = pieces_a[0].shape
    block = lefts[0].shape[-1] // RING
    half = jax.ShapeDtypeStruct((block // 2, cols), BF16)
    tall = jax.ShapeDtypeStruct((RING * rows, cols), BF16)
    return pl.pallas_call(
        far_kernel,
        in_specs=[HBM] * (3 * RING),
        out_specs=[VMEM] * 6,
        out_shape=[half] * 4 + [tall] * 2,
        scratch_shapes=left_scratch(block, 1) + [pltpu.SemaphoreType.DMA((2 * RING,))],
        compiler_params=params(),
        cost_estimate=cost(4 * RING * rows * block * cols, 16 * RING * rows * cols),
        name="far",
    )(*[in_hbm(value) for value in (*lefts, *pieces_a, *pieces_b)])


def side_kernel(*refs):
    lefts, rows_refs, near, outs = refs[:RING], refs[RING : RING + 2], refs[RING + 2 : RING + 6], refs[RING + 6 : RING + 10]
    buf, sems = refs[RING + 10 :]
    loads = left_loads(lefts, buf, sems, (1, 3))
    half = near[0].shape[0]
    for f in range(2):
        from_left, from_right = near[2 * f : 2 * f + 2]
        to_right, to_left = outs[2 * f : 2 * f + 2]
        wait_all(loads[f][0])
        block = tn(flat(buf[f, 0]), rows_refs[f][...])
        to_right[:half, :] = (block[:half] + from_left[...].astype(F32)).astype(BF16)
        to_right[half:, :] = block[half:].astype(BF16)
        wait_all(loads[f][1])
        block = tn(flat(buf[f, 1]), rows_refs[f][...])
        to_left[:half, :] = block[:half].astype(BF16)
        to_left[half:, :] = (block[half:] + from_right[...].astype(F32)).astype(BF16)


def side_blocks(lefts, rows, near):
    depth, cols = rows[0].shape
    block = lefts[0].shape[-1] // RING
    shape = jax.ShapeDtypeStruct((block, cols), BF16)
    return pl.pallas_call(
        side_kernel,
        in_specs=[HBM] * RING + [VMEM] * 6,
        out_specs=[VMEM] * 4,
        out_shape=[shape] * 4,
        scratch_shapes=left_scratch(block, 2),
        compiler_params=params(),
        cost_estimate=cost(8 * depth * block * cols, 8 * depth * cols),
        name="side",
    )(*[in_hbm(left) for left in lefts], *rows, *near)


def own_kernel(*refs):
    lefts, rows_refs, parts, outs = refs[:RING], refs[RING : RING + 2], refs[RING + 2 : RING + 6], refs[RING + 6 : RING + 8]
    buf, sems, part_buf, part_sems, out_buf, out_sems = refs[RING + 8 :]
    gets = [pltpu.make_async_copy(parts[i], part_buf.at[i], part_sems.at[i]) for i in range(4)]
    for get in gets:
        get.start()
    loads = left_loads(lefts, buf, sems, (0,))
    chunks = out_sems.shape[1]
    puts = []
    for f in range(2):
        wait_all(loads[f][0])
        block = tn(flat(buf[f, 0]), rows_refs[f][...])
        wait_all(gets[2 * f : 2 * f + 2])
        size = block.shape[0] // chunks
        for c in range(chunks):
            at = slice(c * size, (c + 1) * size)
            out_buf[f, at] = (
                block[at] + part_buf[2 * f, at].astype(F32) + part_buf[2 * f + 1, at].astype(F32)
            )
            put = pltpu.make_async_copy(out_buf.at[f, at], outs[f].at[at], out_sems.at[f, c])
            put.start()
            puts.append(put)
    wait_all(puts)


def own_blocks(lefts, rows, parts):
    depth, cols = rows[0].shape
    block = lefts[0].shape[-1] // RING
    return pl.pallas_call(
        own_kernel,
        in_specs=[HBM] * RING + [VMEM] * 2 + [ANY] * 4,
        out_specs=[HBM] * 2,
        out_shape=[pltpu.HBM((block, cols), F32)] * 2,
        scratch_shapes=left_scratch(block, 1)
        + [pltpu.VMEM((4, block, cols), BF16), pltpu.SemaphoreType.DMA((4,))]
        + [pltpu.VMEM((2, block, cols), F32), pltpu.SemaphoreType.DMA((2, 4))],
        compiler_params=params(),
        cost_estimate=cost(4 * depth * block * cols, 16 * depth * cols),
        name="own",
    )(*[in_hbm(left) for left in lefts], *rows, *parts)


def per_device(states, gains, proj_a, proj_b, cotangent, src_len, tgt_len, dest):
    weight_a = proj_a[0]
    weight_b = proj_b[0]
    rows = states[0]
    keep, send, by_x, by_z = forward(rows, gains, cotangent, weight_a, weight_b)
    swap = [(0, 1), (1, 0)]
    got = lax.ppermute(send, "section", swap)
    slots = pack(keep, got, src_len, dest)
    width = slots.shape[1]
    slots = slots.reshape(SEQ_DEV, MAXLEN, width)
    slots = lax.all_to_all(slots, ("z", "x"), split_axis=0, concat_axis=0, tiled=True)
    slots = slots.reshape(SLOTS, width)
    pieces = exchanged(by_x, "x") + exchanged(by_z, "z")
    slots, pieces = lax.optimization_barrier((slots, pieces))
    pieces[0], pieces[RING] = in_hbm(pieces[0]), in_hbm(pieces[RING])
    lefts = gathered(stacked(pieces).reshape(2, RING, QUARTER, width), "mp")
    front, back = attend(keep, got, slots, src_len, tgt_len, dest)
    back = back.reshape(SEQ_DEV, MAXLEN, width)
    back = lax.all_to_all(back, ("z", "x"), split_axis=0, concat_axis=0, tiled=True)
    keep, send = unpack(back.reshape(SLOTS, width), front, src_len, dest)
    got = lax.ppermute(send, "section", swap)
    got, lefts[1], lefts[2] = lax.optimization_barrier((got, lefts[1], lefts[2]))
    first, second = join(keep, got)

    rights_a, rights_b = spread(first, "x"), spread(second, "z")
    partial = dnorm_partial(first, second, weight_a, weight_b)
    parts = lax.all_to_all(
        partial.reshape(RING, TOK // RING, -1), "mp", split_axis=0, concat_axis=0, tiled=True
    )
    quarter = rms_back(rows, gains, parts)
    grad_states = place(gathered(quarter, "mp"))

    outs = far_blocks(lefts, rights_a, rights_b)
    near = [shift(out, axis, k) for out, axis, k in zip(outs[:4], "zzxx", (1, 3, 1, 3), strict=True)]
    sides = side_blocks(lefts, outs[4:], near)
    sides = [shift(out, axis, k) for out, axis, k in zip(sides, "zzxx", (1, 3, 1, 3), strict=True)]
    grad_a, grad_b = own_blocks(lefts, outs[4:], sides)
    return (grad_states[None], grad_a[None], grad_b[None])


def solution(mesh):
    split = jax.sharding.Mesh(mesh.devices.reshape(2, RING, RING, RING), ("section", "z", "x", "mp"))
    dp = ("z", "x")
    return jax.shard_map(
        per_device,
        mesh=split,
        in_specs=(
            P("section", dp, None),
            P("section", None),
            P("section", None, "mp"),
            P("section", None, "mp"),
            P(dp, None),
            P(),
            P(),
            P(),
        ),
        out_specs=(P("section", dp, None), P("section", dp, "mp"), P("section", dp, "mp")),
        check_vma=False,
    )
```

```python
import jax
import jax.numpy as jnp
from jax import lax
from jax.experimental import pallas as pl
from jax.experimental.pallas import tpu as pltpu
from jax.sharding import PartitionSpec as P

HEAD_DIM = 64
SEQ_DEV = 16
MAXLEN = 16
TOK = 128
SLOTS = 256
RING = 4
QUARTER = TOK // RING
ORDER = (0, 3, 1, 2)
EPS = 1e-06
F32 = jnp.float32
BF16 = jnp.bfloat16
VMEM = pl.BlockSpec(memory_space=pltpu.VMEM)
ANY = pl.BlockSpec(memory_space=pl.ANY)
HBM = pl.BlockSpec(memory_space=pltpu.HBM)


def iota(shape, dim):
    return lax.broadcasted_iota(jnp.int32, shape, dim)


def total(value, axis):
    return jnp.sum(value.astype(F32), axis=axis, keepdims=True)


def tn(left, right):
    return lax.dot_general(left, right, (((0,), (0,)), ((), ())), preferred_element_type=F32)


def in_hbm(value):
    return pltpu.with_memory_space_constraint(value, pltpu.HBM)


def cost(flops, nbytes):
    return pl.CostEstimate(flops=flops, bytes_accessed=nbytes, transcendentals=0)


def params(mib=12, **more):
    return pltpu.CompilerParams(vmem_limit_bytes=mib << 20, **more)


def column_of(row):
    square = jnp.broadcast_to(row, (SEQ_DEV, SEQ_DEV))
    same = iota((SEQ_DEV, SEQ_DEV), 0) == iota((SEQ_DEV, SEQ_DEV), 1)
    return total(jnp.where(same, square, 0), 1)


def member_index():
    return lax.axis_index("z") * RING + lax.axis_index("x")


def slot_onehot(member, src_len, dest):
    i, j = iota((SEQ_DEV, SEQ_DEV), 0), iota((SEQ_DEV, SEQ_DEV), 1)
    lengths = src_len[pl.ds(member, 1), :]
    ends = total(jnp.where(j <= i, jnp.broadcast_to(lengths, (SEQ_DEV, SEQ_DEV)), 0), 1)
    begins = ends - column_of(lengths)
    place = column_of(dest[pl.ds(member, 1), :] >> 4) * MAXLEN
    row = iota((SEQ_DEV, TOK), 1).astype(F32)
    inside = (row >= begins) & (row < ends)
    target = total(jnp.where(inside, place + row - begins, 0.0), 0)
    hit = iota((SLOTS, TOK), 0).astype(F32) == target
    return jnp.where(hit, 1.0, 0.0).astype(BF16)


def pair_mask(member, src_len, tgt_len, dest):
    i, j = iota((SEQ_DEV, SEQ_DEV), 0), iota((SEQ_DEV, SEQ_DEV), 1)
    column = column_of(tgt_len[pl.ds(member, 1), :])
    ends = total(jnp.where(i <= j, jnp.broadcast_to(column, (SEQ_DEV, SEQ_DEV)), 0.0), 0)
    row = iota((TOK, SEQ_DEV), 0).astype(F32)
    mine = total(jnp.where(row >= ends, 1.0, 0.0), 1)
    codes = dest[...]
    to_me = (codes >> 4) == member
    target = total(jnp.where(to_me, codes & 15, 0), 1)
    length = total(jnp.where(to_me, src_len[...], 0), 1)
    lane = iota((SEQ_DEV, SLOTS), 1)
    own = (lane >> 4) == iota((SEQ_DEV, SLOTS), 0)
    target = total(jnp.where(own, target, 0.0), 0)
    length = total(jnp.where(own, length, 0.0), 0)
    step = (iota((1, SLOTS), 1) & 15).astype(F32)
    target = jnp.where(step < length, target, -1.0)
    return mine == target


def forward_kernel(
    x_hbm, gain_hbm, cot_hbm, a_hbm, b_hbm, keep_ref, send_ref, *rest
):
    mine_hbm, other_hbm = rest[:2]
    x_ref, gain_ref, a_buf, b_buf, normed_ref, left_ref, in_sem, a_sem, b_sem, out_sem = rest[2:]
    count, step, cols = a_buf.shape
    core = lax.axis_index("section")
    get_x = pltpu.make_async_copy(x_hbm, x_ref, in_sem.at[0])
    get_gain = pltpu.make_async_copy(gain_hbm, gain_ref, in_sem.at[1])
    get_left = pltpu.make_async_copy(cot_hbm, left_ref, in_sem.at[2])
    get_x.start()
    get_gain.start()

    @pl.when(core != 0)
    def _():
        get_left.start()

    def fetch(k):
        rows = pl.ds(k * step, step)
        return (
            pltpu.make_async_copy(a_hbm.at[rows, :], a_buf.at[k], a_sem.at[k]),
            pltpu.make_async_copy(b_hbm.at[rows, :], b_buf.at[k], b_sem.at[k]),
        )

    for k in range(count):
        for copy in fetch(k):
            copy.start()
    get_x.wait()
    get_gain.wait()
    xf = x_ref[...].astype(F32)
    scale = lax.rsqrt(jnp.mean(xf * xf, axis=-1, keepdims=True) + EPS)
    normed_ref[...] = (xf * scale * gain_ref[...]).astype(BF16)

    @pl.when(core == 0)
    def _():
        left_ref[...] = normed_ref[...]

    @pl.when(core != 0)
    def _():
        get_left.wait()

    z, x = lax.axis_index("z"), lax.axis_index("x")
    quarter = pl.ds(pl.multiple_of(lax.axis_index("mp") * QUARTER, QUARTER), QUARTER)
    block = cols // RING
    copies = []
    for k in range(RING):
        for j in range(RING):
            to = slice(j * block, (j + 1) * block)
            at_x = ((z + j) % RING * RING + (x + k) % RING) * block
            at_z = ((z + k) % RING * RING + (x + j) % RING) * block
            at_mine = jnp.where(core == 0, at_x, at_z)
            at_other = jnp.where(core == 0, at_z, at_x)
            for source, at, out in ((left_ref, at_mine, mine_hbm), (normed_ref, at_other, other_hbm)):
                copies.append(
                    pltpu.make_async_copy(
                        source.at[quarter, pl.ds(pl.multiple_of(at, block), block)],
                        out.at[k, :, to],
                        out_sem.at[len(copies)],
                    )
                )
                copies[-1].start()

    acc_a = acc_b = None
    for k in range(count):
        for copy in fetch(k):
            copy.wait()
        at = slice(k * step, (k + 1) * step)
        part_a = jnp.dot(normed_ref[:, at], a_buf[k], preferred_element_type=F32)
        part_b = jnp.dot(left_ref[:, at], b_buf[k], preferred_element_type=F32)
        acc_a = part_a if acc_a is None else acc_a + part_a
        acc_b = part_b if acc_b is None else acc_b + part_b
    half = cols // 2
    parts = [[acc[:, i * half : (i + 1) * half].astype(BF16) for acc in (acc_a, acc_b)] for i in range(2)]

    def put(ref, pieces):
        ref[:, :half] = pieces[0]
        ref[:, half:] = pieces[1]

    @pl.when(core == 0)
    def _():
        put(keep_ref, parts[0])
        put(send_ref, parts[1])

    @pl.when(core != 0)
    def _():
        put(keep_ref, parts[1])
        put(send_ref, parts[0])

    for copy in copies:
        copy.wait()


def forward(x, gain, cot, weight_a, weight_b):
    rows, width = x.shape
    cols = weight_a.shape[1]
    step = 512
    count = width // step
    half = jax.ShapeDtypeStruct((rows, cols), BF16)
    return pl.pallas_call(
        forward_kernel,
        in_specs=[HBM] * 5,
        out_specs=[VMEM] * 2 + [HBM] * 2,
        out_shape=[half] * 2 + [pltpu.HBM((RING, QUARTER, cols), BF16)] * 2,
        scratch_shapes=[pltpu.VMEM((rows, width), BF16), pltpu.VMEM((1, width), F32)]
        + [pltpu.VMEM((count, step, cols), BF16)] * 2
        + [pltpu.VMEM((rows, width), BF16)] * 2
        + [pltpu.SemaphoreType.DMA((3,))]
        + [pltpu.SemaphoreType.DMA((count,))] * 2
        + [pltpu.SemaphoreType.DMA((2 * RING * RING,))],
        compiler_params=params(32),
        cost_estimate=cost(4 * rows * width * cols, 4 * width * cols),
        name="forward",
    )(in_hbm(x), in_hbm(gain), in_hbm(cot), in_hbm(weight_a), in_hbm(weight_b))


def placed(places, refs, sems):
    copies = [
        pltpu.make_async_copy(refs[source].at[at], refs[out].at[to], sems.at[i])
        for i, (source, at, out, to) in enumerate(places)
    ]
    for copy in copies:
        copy.start()
    return copies


def wait_all(copies):
    for copy in copies:
        copy.wait()


PAIRS = [(m, (k,), 2 + i, (m,)) for i, k in enumerate((0, 1, 3, 2)) for m in range(2)]
STACK = [(p, (m,), RING, (m, p)) for p in range(RING) for m in range(2)]


def pack_kernel(keep_ref, got_ref, src_ref, dest_ref, mine_ref, other_ref, out_ref, *rest):
    copies = placed(PAIRS, (mine_ref, other_ref, *rest[:RING]), rest[RING])
    spread = slot_onehot(member_index(), src_ref, dest_ref)

    @pl.when(lax.axis_index("section") == 0)
    def _():
        out_ref[...] = jnp.dot(spread, keep_ref[...], preferred_element_type=F32).astype(BF16)

    @pl.when(lax.axis_index("section") != 0)
    def _():
        out_ref[...] = jnp.dot(spread, got_ref[...], preferred_element_type=F32).astype(BF16)

    wait_all(copies)


def pack(keep, got, src_len, dest, mine, other):
    width = keep.shape[1]
    _, rows, cols = mine.shape
    outs = pl.pallas_call(
        pack_kernel,
        in_specs=[VMEM] * 4 + [HBM, ANY],
        out_specs=[VMEM] + [HBM] * RING,
        out_shape=[jax.ShapeDtypeStruct((SLOTS, width), BF16)]
        + [pltpu.HBM((2, rows, cols), BF16)] * RING,
        scratch_shapes=[pltpu.SemaphoreType.DMA((len(PAIRS),))],
        compiler_params=params(),
        cost_estimate=cost(2 * SLOTS * TOK * width, 2 * SLOTS * width),
        name="pack",
    )(keep, got, src_len, dest, in_hbm(mine), other)
    return outs[0], outs[1:]


def attend_kernel(
    keep_ref, got_ref, slots_ref, src_ref, tgt_ref, dest_ref, *rest
):
    front_ref, back_ref, stack_ref, own_ref, sems = rest[RING:]
    copies = placed(STACK, (*rest[:RING], stack_ref), sems)
    mask = pair_mask(member_index(), src_ref, tgt_ref, dest_ref)

    @pl.when(lax.axis_index("section") == 0)
    def _():
        own_ref[...] = got_ref[...]

    @pl.when(lax.axis_index("section") != 0)
    def _():
        own_ref[...] = keep_ref[...]

    half = own_ref.shape[1] // 2
    pair = 2 * HEAD_DIM
    low = iota((1, pair), 1) < HEAD_DIM
    nothing = jnp.zeros((), BF16)

    def both(value):
        return jnp.concatenate(
            [jnp.where(low, value, nothing), jnp.where(low, nothing, value)], axis=0
        )

    def nt(left, right):
        return lax.dot_general(left, right, (((1,), (1,)), ((), ())), preferred_element_type=F32)

    def one(score, dweight):
        expo = jnp.where(mask, jnp.exp(score), 0.0)
        weight = expo * (1.0 / jnp.sum(expo, axis=-1, keepdims=True))
        mean = jnp.sum(weight * dweight, axis=-1, keepdims=True)
        return weight.astype(BF16), (weight * (dweight - mean)).astype(BF16)

    def fold(value):
        return jnp.where(low, value[:SLOTS], value[SLOTS:]).astype(BF16)

    for p in range(half // pair):
        first = slice(p * pair, (p + 1) * pair)
        second = slice(half + p * pair, half + (p + 1) * pair)
        query, dout = own_ref[:, first], own_ref[:, second]
        keys, values = both(slots_ref[:, first]), both(slots_ref[:, second])
        score, dweight = nt(query, keys), nt(dout, values)
        weight_0, dscore_0 = one(score[:, :SLOTS], dweight[:, :SLOTS])
        weight_1, dscore_1 = one(score[:, SLOTS:], dweight[:, SLOTS:])
        weight = jnp.concatenate([weight_0, weight_1], axis=1)
        dscore = jnp.concatenate([dscore_0, dscore_1], axis=1)
        front_ref[:, first] = jnp.dot(dscore, keys, preferred_element_type=F32).astype(BF16)
        front_ref[:, second] = jnp.dot(weight, values, preferred_element_type=F32).astype(BF16)
        back_ref[:, first] = fold(tn(dscore, query))
        back_ref[:, second] = fold(tn(weight, dout))
    wait_all(copies)


def attend(keep, got, slots, src_len, tgt_len, dest, pieces):
    rows, width = keep.shape
    _, quarter, cols = pieces[0].shape
    return pl.pallas_call(
        attend_kernel,
        in_specs=[VMEM] * 6 + [HBM] + [ANY] * (RING - 1),
        out_specs=[VMEM] * 2 + [HBM],
        out_shape=[
            jax.ShapeDtypeStruct((rows, width), BF16),
            jax.ShapeDtypeStruct((SLOTS, width), BF16),
            pltpu.HBM((2, RING, quarter, cols), BF16),
        ],
        scratch_shapes=[pltpu.VMEM((rows, width), BF16), pltpu.SemaphoreType.DMA((len(STACK),))],
        compiler_params=params(),
        cost_estimate=cost(24 * rows * SLOTS * width, 8 * SLOTS * width),
        name="attend",
    )(keep, got, slots, src_len, tgt_len, dest, in_hbm(pieces[0]), *pieces[1:])


def unpack_kernel(back_ref, front_ref, src_ref, dest_ref, keep_ref, send_ref):
    spread = slot_onehot(member_index(), src_ref, dest_ref)
    rows = tn(spread, back_ref[...]).astype(BF16)
    half = rows.shape[1] // 2
    core = lax.axis_index("section")

    @pl.when(core == 0)
    def _():
        keep_ref[:, :half] = rows[:, :half]
        keep_ref[:, half:] = front_ref[:, :half]
        send_ref[:, :half] = front_ref[:, half:]
        send_ref[:, half:] = rows[:, half:]

    @pl.when(core != 0)
    def _():
        keep_ref[:, :half] = front_ref[:, half:]
        keep_ref[:, half:] = rows[:, half:]
        send_ref[:, :half] = rows[:, :half]
        send_ref[:, half:] = front_ref[:, :half]


def unpack(back, front, src_len, dest):
    width = front.shape[1]
    half = jax.ShapeDtypeStruct((TOK, width), BF16)
    return pl.pallas_call(
        unpack_kernel,
        in_specs=[VMEM] * 4,
        out_specs=[VMEM] * 2,
        out_shape=[half, half],
        compiler_params=params(),
        cost_estimate=cost(2 * SLOTS * TOK * width, 4 * SLOTS * width),
        name="unpack",
    )(back, front, src_len, dest)


def join_kernel(keep_ref, got_ref, rows_ref, other_ref):
    width = keep_ref.shape[1]
    half = width // 2
    core = lax.axis_index("section")
    mine = pl.multiple_of(core * half, half)
    theirs = pl.multiple_of((1 - core) * half, half)
    for ref, at in ((keep_ref, mine), (got_ref, theirs)):
        rows_ref[:, pl.ds(at, half)] = ref[:, :half]
        rows_ref[:, pl.ds(pl.multiple_of(width + at, half), half)] = ref[:, half:]
        other_ref[:, pl.ds(at, half)] = ref[:, half:]


def join(keep, got):
    rows, width = keep.shape
    return pl.pallas_call(
        join_kernel,
        in_specs=[VMEM, VMEM],
        out_specs=[VMEM] * 2,
        out_shape=[
            jax.ShapeDtypeStruct((rows, 2 * width), BF16),
            jax.ShapeDtypeStruct((rows, width), BF16),
        ],
        compiler_params=params(),
        cost_estimate=cost(0, 8 * keep.size),
        name="join",
    )(keep, got)


def dnorm_kernel(rows_ref, got_ref, a_hbm, b_hbm, out_ref, a_buf, b_buf, a_sem, b_sem):
    count, step, cols = a_buf.shape
    core = lax.axis_index("section")

    def nt(left, right):
        return lax.dot_general(left, right, (((1,), (1,)), ((), ())), preferred_element_type=F32)

    def fetches(hbm, buf, sem):
        return [
            pltpu.make_async_copy(hbm.at[pl.ds(k * step, step), :], buf.at[k], sem.at[k])
            for k in range(count)
        ]

    get_a, get_b = fetches(a_hbm, a_buf, a_sem), fetches(b_hbm, b_buf, b_sem)

    @pl.when(core == 0)
    def _():
        for k in range(count):
            get_a[k].start()
            get_b[k].start()
        for k in range(count):
            get_a[k].wait()
            get_b[k].wait()
            block = nt(rows_ref[:, :cols], a_buf[k]) + nt(got_ref[...], b_buf[k])
            out_ref[:, k * step : (k + 1) * step] = block.astype(BF16)

    @pl.when(core != 0)
    def _():
        for k in range(count):
            get_a[k].start()
        for k in range(count):
            get_a[k].wait()
            out_ref[:, k * step : (k + 1) * step] = nt(got_ref[...], a_buf[k]).astype(BF16)


def dnorm_partial(rows, got, weight_a, weight_b):
    width, cols = weight_a.shape
    step = 512
    count = width // step
    return pl.pallas_call(
        dnorm_kernel,
        in_specs=[VMEM] * 2 + [HBM] * 2,
        out_specs=VMEM,
        out_shape=jax.ShapeDtypeStruct((TOK, width), BF16),
        scratch_shapes=[pltpu.VMEM((count, step, cols), BF16)] * 2
        + [pltpu.SemaphoreType.DMA((count,))] * 2,
        compiler_params=params(24),
        cost_estimate=cost(4 * TOK * width * cols, 4 * width * cols),
        name="dnorm",
    )(rows, got, in_hbm(weight_a), in_hbm(weight_b))


def rms_back_kernel(x_hbm, gain_ref, parts_ref, out_ref, x_ref, sem):
    rows = out_ref.shape[0]
    mine = pl.multiple_of(lax.axis_index("mp") * rows, rows)
    get_x = pltpu.make_async_copy(x_hbm.at[pl.ds(mine, rows), :], x_ref, sem)
    get_x.start()
    dnorm = parts_ref[0].astype(F32)
    for i in range(1, RING):
        dnorm += parts_ref[i].astype(F32)
    get_x.wait()
    xf = x_ref[...].astype(F32)
    scale = lax.rsqrt(jnp.mean(xf * xf, axis=-1, keepdims=True) + EPS)
    upper = gain_ref[...] * dnorm
    inner = jnp.mean(xf * upper, axis=-1, keepdims=True)
    out_ref[...] = (scale * upper - xf * (scale * scale * scale * inner)).astype(BF16)


def rms_back(x, gain, parts):
    rows, width = parts.shape[1:]
    return pl.pallas_call(
        rms_back_kernel,
        in_specs=[HBM] + [VMEM] * 2,
        out_specs=VMEM,
        out_shape=jax.ShapeDtypeStruct((rows, width), BF16),
        scratch_shapes=[pltpu.VMEM((rows, width), BF16), pltpu.SemaphoreType.DMA],
        compiler_params=params(),
        cost_estimate=cost(10 * rows * width, 12 * rows * width),
        name="rms_back",
    )(in_hbm(x), gain, parts)


def place_kernel(*refs):
    pieces, (out_hbm, sems) = refs[:RING], refs[RING:]
    rows = pieces[0].shape[0]
    copies = []
    for i, k in enumerate(ORDER):
        at = pl.multiple_of((lax.axis_index("mp") + k) % RING * rows, rows)
        copies.append(pltpu.make_async_copy(pieces[i], out_hbm.at[pl.ds(at, rows), :], sems.at[i]))
        copies[-1].start()
    for copy in copies:
        copy.wait()


def place(pieces):
    rows, width = pieces[0].shape
    return pl.pallas_call(
        place_kernel,
        in_specs=[ANY] * RING,
        out_specs=HBM,
        out_shape=pltpu.HBM((RING * rows, width), BF16),
        scratch_shapes=[pltpu.SemaphoreType.DMA((RING,))],
        compiler_params=params(),
        cost_estimate=cost(0, 4 * RING * rows * width),
        name="place",
    )(*pieces)


def shift(value, axis, k):
    return lax.ppermute(value, axis, [(i, (i + k) % RING) for i in range(RING)])


def gathered(block, axis):
    left = shift(block, axis, 1)
    return [block, left, shift(block, axis, 3), shift(left, axis, 1)]


def moved(value, k, along, across=False):
    pairs = []
    for core in range(2):
        for z in range(RING):
            for x in range(RING):
                to = {"z": z, "x": x}
                to[along[core]] = (to[along[core]] + k) % RING
                target = (1 - core if across else core, to["z"], to["x"])
                pairs.append(
                    ((core * RING + z) * RING + x, (target[0] * RING + target[1]) * RING + target[2])
                )
    return lax.ppermute(value, ("section", "z", "x"), pairs)


GATHER, REDUCE = "xz", "zx"


def fetched(own, others):
    return [own] + [moved(others[k], k, GATHER) for k in (1, 3, 2)]


def left_loads(lefts, buf, sems, ks):
    block = buf.shape[-1]
    mine = lax.axis_index("mp")
    loads = [[[] for _ in ks] for _ in range(2)]
    for f in range(2):
        for i, k in enumerate(ks):
            for j, (left, distance) in enumerate(zip(lefts, ORDER, strict=True)):
                at = pl.multiple_of((mine + distance) % RING * QUARTER, QUARTER)
                loads[f][i].append(
                    pltpu.make_async_copy(
                        left.at[f, :, :, pl.ds(k * block, block)],
                        buf.at[f, i, :, pl.ds(at, QUARTER), :],
                        sems.at[f, i, j],
                    )
                )
                loads[f][i][-1].start()
    return loads


def left_scratch(block, count):
    return [
        pltpu.VMEM((2, count, RING, TOK, block), BF16),
        pltpu.SemaphoreType.DMA((2, count, RING)),
    ]


def flat(value):
    return value.reshape(RING * TOK, value.shape[-1])


def far_kernel(*refs):
    lefts, pieces = refs[:RING], refs[RING : 2 * RING]
    top_ref, low_ref, rows_ref, buf, sems, row_sems = refs[2 * RING :]
    gets = [
        pltpu.make_async_copy(piece, rows_ref.at[pl.ds(i * TOK, TOK), :], row_sems.at[i])
        for i, piece in enumerate(pieces)
    ]
    for get in gets:
        get.start()
    loads = left_loads(lefts, buf, sems, (2,))
    wait_all(gets)
    half, cols = top_ref.shape[0], top_ref.shape[1] // 2
    for m in range(2):
        at = slice(m * cols, (m + 1) * cols)
        wait_all(loads[m][0])
        block = tn(flat(buf[m, 0]), rows_ref[:, at]).astype(BF16)
        top_ref[:, at] = block[:half]
        low_ref[:, at] = block[half:]


def far_block(lefts, pieces):
    rows, cols = pieces[0].shape
    block = lefts[0].shape[-1] // RING
    half = jax.ShapeDtypeStruct((block // 2, cols), BF16)
    return pl.pallas_call(
        far_kernel,
        in_specs=[HBM] * (2 * RING),
        out_specs=[VMEM] * 3,
        out_shape=[half, half, jax.ShapeDtypeStruct((RING * rows, cols), BF16)],
        scratch_shapes=left_scratch(block, 1) + [pltpu.SemaphoreType.DMA((RING,))],
        compiler_params=params(),
        cost_estimate=cost(2 * RING * rows * block * cols, 8 * RING * rows * cols),
        name="far",
    )(*[in_hbm(value) for value in (*lefts, *pieces)])


def side_kernel(*refs):
    lefts, (rows_ref, from_left, from_right) = refs[:RING], refs[RING : RING + 3]
    rights, to_lefts, other_ref, buf, sems = refs[RING + 3 : RING + 5], refs[RING + 5 : RING + 7], *refs[RING + 7 :]
    loads = left_loads(lefts, buf, sems, (1, 3, 0))
    half, cols = from_left.shape[0], other_ref.shape[1]
    for m in range(2):
        at = slice(m * cols, (m + 1) * cols)

        def product(i, m=m, at=at):
            wait_all(loads[m][i])
            return tn(flat(buf[m, i]), rows_ref[:, at])

        block = product(0)
        rights[m][:half, :] = (block[:half] + from_left[:, at].astype(F32)).astype(BF16)
        rights[m][half:, :] = block[half:].astype(BF16)
        block = product(1)
        to_lefts[m][:half, :] = block[:half].astype(BF16)
        to_lefts[m][half:, :] = (block[half:] + from_right[:, at].astype(F32)).astype(BF16)
    wait_all(loads[0][2])
    wait_all(loads[1][2])
    other_ref[...] = tn(flat(buf[1, 2]), rows_ref[:, cols:]).astype(BF16)


def side_blocks(lefts, rows, from_left, from_right):
    depth, cols = rows.shape
    block = lefts[0].shape[-1] // RING
    shape = jax.ShapeDtypeStruct((block, cols // 2), BF16)
    return pl.pallas_call(
        side_kernel,
        in_specs=[HBM] * RING + [VMEM] * 3,
        out_specs=[VMEM] * 5,
        out_shape=[shape] * 5,
        scratch_shapes=left_scratch(block, 3),
        compiler_params=params(16),
        cost_estimate=cost(5 * depth * block * cols, 4 * depth * cols),
        name="side",
    )(*[in_hbm(left) for left in lefts], rows, from_left, from_right)


def own_kernel(*refs):
    lefts, rows_ref, parts, outs = refs[:RING], refs[RING], refs[RING + 1 : RING + 6], refs[RING + 6 : RING + 8]
    buf, sems, part_buf, part_sems, out_buf, out_sems = refs[RING + 8 :]
    gets = [pltpu.make_async_copy(parts[i], part_buf.at[i], part_sems.at[i]) for i in range(5)]
    for get in gets:
        get.start()
    mine = lax.axis_index("mp")
    loads = []
    for j, (left, distance) in enumerate(zip(lefts, ORDER, strict=True)):
        at = pl.multiple_of((mine + distance) % RING * QUARTER, QUARTER)
        loads.append(
            pltpu.make_async_copy(
                left.at[0, :, :, pl.ds(0, buf.shape[-1])],
                buf.at[:, pl.ds(at, QUARTER), :],
                sems.at[j],
            )
        )
        loads[-1].start()
    core = lax.axis_index("section")
    chunks = out_sems.shape[1]
    size = out_buf.shape[1] // chunks

    def put(m, c, out):
        at = slice(c * size, (c + 1) * size)
        return pltpu.make_async_copy(out_buf.at[m, at], out.at[at], out_sems.at[m, c])

    def write(m, c):
        @pl.when(core == m)
        def _():
            put(m, c, outs[0]).start()

        @pl.when(core != m)
        def _():
            put(m, c, outs[1]).start()

    wait_all(loads)
    block = tn(flat(buf[...]), rows_ref[:, : out_buf.shape[2]])
    wait_all(gets[:2])
    for c in range(chunks):
        at = slice(c * size, (c + 1) * size)
        out_buf[0, at] = block[at] + part_buf[0, at].astype(F32) + part_buf[1, at].astype(F32)
        write(0, c)
    wait_all(gets[2:])
    for c in range(chunks):
        at = slice(c * size, (c + 1) * size)
        out_buf[1, at] = (
            part_buf[4, at].astype(F32) + part_buf[2, at].astype(F32) + part_buf[3, at].astype(F32)
        )
        write(1, c)
    for m in range(2):
        for c in range(chunks):
            put(m, c, outs[0]).wait()


def own_blocks(lefts, rows, parts):
    depth, cols = rows.shape
    cols = cols // 2
    block = lefts[0].shape[-1] // RING
    return pl.pallas_call(
        own_kernel,
        in_specs=[HBM] * RING + [VMEM] + [ANY] * 5,
        out_specs=[HBM] * 2,
        out_shape=[pltpu.HBM((block, cols), F32)] * 2,
        scratch_shapes=[pltpu.VMEM((RING, TOK, block), BF16), pltpu.SemaphoreType.DMA((RING,))]
        + [pltpu.VMEM((5, block, cols), BF16), pltpu.SemaphoreType.DMA((5,))]
        + [pltpu.VMEM((2, block, cols), F32), pltpu.SemaphoreType.DMA((2, 4))],
        compiler_params=params(16),
        cost_estimate=cost(2 * depth * block * cols, 16 * depth * cols),
        name="own",
    )(*[in_hbm(left) for left in lefts], rows, *parts)


def per_device(states, gains, proj_a, proj_b, cotangent, src_len, tgt_len, dest):
    weight_a = proj_a[0]
    weight_b = proj_b[0]
    rows = states[0]
    keep, send, mine, other = forward(rows, gains, cotangent, weight_a, weight_b)
    swap = [(0, 1), (1, 0)]
    got = lax.ppermute(send, "section", swap)
    slots, slices = pack(keep, got, src_len, dest, mine, lax.ppermute(other, "section", swap))
    width = slots.shape[1]
    slots = slots.reshape(SEQ_DEV, MAXLEN, width)
    slots = lax.all_to_all(slots, ("z", "x"), split_axis=0, concat_axis=0, tiled=True)
    slots = slots.reshape(SLOTS, width)
    pieces = fetched(slices[0], {1: slices[1], 3: slices[2], 2: slices[3]})
    front, back, own = attend(keep, got, slots, src_len, tgt_len, dest, pieces)
    lefts = gathered(own, "mp")
    back = back.reshape(SEQ_DEV, MAXLEN, width)
    back = lax.all_to_all(back, ("z", "x"), split_axis=0, concat_axis=0, tiled=True)
    keep, send = unpack(back.reshape(SLOTS, width), front, src_len, dest)
    got = lax.ppermute(send, "section", swap)
    kind, others = join(keep, got)

    rights = fetched(kind, {k: kind for k in (1, 2, 3)})
    others = lax.ppermute(others, "section", swap)
    others, lefts[1], lefts[2] = lax.optimization_barrier((others, lefts[1], lefts[2]))
    partial = dnorm_partial(kind, others, weight_a, weight_b)
    partial, rights[1], rights[2] = lax.optimization_barrier((partial, rights[1], rights[2]))
    parts = lax.all_to_all(
        partial.reshape(RING, TOK // RING, -1), "mp", split_axis=0, concat_axis=0, tiled=True
    )
    quarter = rms_back(rows, gains, parts)
    grad_states = place(gathered(quarter, "mp"))

    top, low, stack = far_block(lefts, rights)
    from_left, from_right = moved(top, 1, REDUCE), moved(low, 3, REDUCE)
    right, right_other, left, left_other, own_other = side_blocks(lefts, stack, from_left, from_right)
    sums = [
        moved(right, 1, REDUCE),
        moved(left, 3, REDUCE),
        moved(right_other, 1, REDUCE, True),
        moved(left_other, 3, REDUCE, True),
        lax.ppermute(own_other, "section", swap),
    ]
    grad_a, grad_b = own_blocks(lefts, stack, sums)
    return (grad_states[None], grad_a[None], grad_b[None])


def solution(mesh):
    split = jax.sharding.Mesh(mesh.devices.reshape(2, RING, RING, RING), ("section", "z", "x", "mp"))
    dp = ("z", "x")
    return jax.shard_map(
        per_device,
        mesh=split,
        in_specs=(
            P("section", dp, None),
            P("section", None),
            P("section", None, "mp"),
            P("section", None, "mp"),
            P(dp, None),
            P(),
            P(),
            P(),
        ),
        out_specs=(P("section", dp, None), P("section", dp, "mp"), P("section", dp, "mp")),
        check_vma=False,
    )
```

```python
import jax
import jax.numpy as jnp
from jax import lax
from jax.experimental import pallas as pl
from jax.experimental.pallas import tpu as pltpu
from jax.sharding import PartitionSpec as P

HEAD_DIM = 64
SEQ_DEV = 16
MAXLEN = 16
TOK = 128
SLOTS = 256
RING = 4
QUARTER = TOK // RING
ORDER = (0, 3, 1, 2)
EPS = 1e-06
F32 = jnp.float32
BF16 = jnp.bfloat16
VMEM = pl.BlockSpec(memory_space=pltpu.VMEM)
ANY = pl.BlockSpec(memory_space=pl.ANY)
HBM = pl.BlockSpec(memory_space=pltpu.HBM)


def iota(shape, dim):
    return lax.broadcasted_iota(jnp.int32, shape, dim)


def total(value, axis):
    return jnp.sum(value.astype(F32), axis=axis, keepdims=True)


def tn(left, right):
    return lax.dot_general(left, right, (((0,), (0,)), ((), ())), preferred_element_type=F32)


def in_hbm(value):
    return pltpu.with_memory_space_constraint(value, pltpu.HBM)


def cost(flops, nbytes):
    return pl.CostEstimate(flops=flops, bytes_accessed=nbytes, transcendentals=0)


def params(mib=12, **more):
    return pltpu.CompilerParams(vmem_limit_bytes=mib << 20, **more)


def column_of(row):
    square = jnp.broadcast_to(row, (SEQ_DEV, SEQ_DEV))
    same = iota((SEQ_DEV, SEQ_DEV), 0) == iota((SEQ_DEV, SEQ_DEV), 1)
    return total(jnp.where(same, square, 0), 1)


def member_index():
    return lax.axis_index("z") * RING + lax.axis_index("x")


def slot_onehot(member, src_len, dest):
    i, j = iota((SEQ_DEV, SEQ_DEV), 0), iota((SEQ_DEV, SEQ_DEV), 1)
    lengths = src_len[pl.ds(member, 1), :]
    ends = total(jnp.where(j <= i, jnp.broadcast_to(lengths, (SEQ_DEV, SEQ_DEV)), 0), 1)
    begins = ends - column_of(lengths)
    place = column_of(dest[pl.ds(member, 1), :] >> 4) * MAXLEN
    row = iota((SEQ_DEV, TOK), 1).astype(F32)
    inside = (row >= begins) & (row < ends)
    target = total(jnp.where(inside, place + row - begins, 0.0), 0)
    hit = iota((SLOTS, TOK), 0).astype(F32) == target
    return jnp.where(hit, 1.0, 0.0).astype(BF16)


def pair_mask(member, src_len, tgt_len, dest):
    i, j = iota((SEQ_DEV, SEQ_DEV), 0), iota((SEQ_DEV, SEQ_DEV), 1)
    column = column_of(tgt_len[pl.ds(member, 1), :])
    ends = total(jnp.where(i <= j, jnp.broadcast_to(column, (SEQ_DEV, SEQ_DEV)), 0.0), 0)
    row = iota((TOK, SEQ_DEV), 0).astype(F32)
    mine = total(jnp.where(row >= ends, 1.0, 0.0), 1)
    codes = dest[...]
    to_me = (codes >> 4) == member
    target = total(jnp.where(to_me, codes & 15, 0), 1)
    length = total(jnp.where(to_me, src_len[...], 0), 1)
    lane = iota((SEQ_DEV, SLOTS), 1)
    own = (lane >> 4) == iota((SEQ_DEV, SLOTS), 0)
    target = total(jnp.where(own, target, 0.0), 0)
    length = total(jnp.where(own, length, 0.0), 0)
    step = (iota((1, SLOTS), 1) & 15).astype(F32)
    target = jnp.where(step < length, target, -1.0)
    return mine == target


def forward_kernel(
    x_hbm, gain_hbm, cot_hbm, a_hbm, b_hbm, keep_ref, send_ref, *rest
):
    mine_ref, other_ref = rest[:2]
    x_ref, gain_ref, a_buf, b_buf, normed_ref, left_ref, in_sem, a_sem, b_sem, out_sem = rest[2:]
    count, step, cols = a_buf.shape
    core = lax.axis_index("section")
    get_x = pltpu.make_async_copy(x_hbm, x_ref, in_sem.at[0])
    get_gain = pltpu.make_async_copy(gain_hbm, gain_ref, in_sem.at[1])
    get_left = pltpu.make_async_copy(cot_hbm, left_ref, in_sem.at[2])
    get_x.start()
    get_gain.start()

    @pl.when(core != 0)
    def _():
        get_left.start()

    def fetch(k):
        rows = pl.ds(k * step, step)
        return (
            pltpu.make_async_copy(a_hbm.at[rows, :], a_buf.at[k], a_sem.at[k]),
            pltpu.make_async_copy(b_hbm.at[rows, :], b_buf.at[k], b_sem.at[k]),
        )

    for k in range(count):
        for copy in fetch(k):
            copy.start()
    get_x.wait()
    get_gain.wait()
    xf = x_ref[...].astype(F32)
    scale = lax.rsqrt(jnp.mean(xf * xf, axis=-1, keepdims=True) + EPS)
    normed_ref[...] = (xf * scale * gain_ref[...]).astype(BF16)

    @pl.when(core == 0)
    def _():
        left_ref[...] = normed_ref[...]

    @pl.when(core != 0)
    def _():
        get_left.wait()

    z, x = lax.axis_index("z"), lax.axis_index("x")
    quarter = pl.ds(pl.multiple_of(lax.axis_index("mp") * QUARTER, QUARTER), QUARTER)
    block = cols // RING
    copies = []
    for k in range(RING):
        for j in range(RING):
            to = slice(j * block, (j + 1) * block)
            at_x = ((z + j) % RING * RING + (x + k) % RING) * block
            at_z = ((z + k) % RING * RING + (x + j) % RING) * block
            at_mine = jnp.where(core == 0, at_x, at_z)
            at_other = jnp.where(core == 0, at_z, at_x)
            for source, at, out in ((left_ref, at_mine, mine_ref), (normed_ref, at_other, other_ref)):
                copies.append(
                    pltpu.make_async_copy(
                        source.at[quarter, pl.ds(pl.multiple_of(at, block), block)],
                        out.at[k, :, to],
                        out_sem.at[len(copies)],
                    )
                )
                copies[-1].start()

    acc_a = acc_b = None
    for k in range(count):
        for copy in fetch(k):
            copy.wait()
        at = slice(k * step, (k + 1) * step)
        part_a = jnp.dot(normed_ref[:, at], a_buf[k], preferred_element_type=F32)
        part_b = jnp.dot(left_ref[:, at], b_buf[k], preferred_element_type=F32)
        acc_a = part_a if acc_a is None else acc_a + part_a
        acc_b = part_b if acc_b is None else acc_b + part_b
    half = cols // 2
    parts = [[acc[:, i * half : (i + 1) * half].astype(BF16) for acc in (acc_a, acc_b)] for i in range(2)]

    def put(ref, pieces):
        ref[:, :half] = pieces[0]
        ref[:, half:] = pieces[1]

    @pl.when(core == 0)
    def _():
        put(keep_ref, parts[0])
        put(send_ref, parts[1])

    @pl.when(core != 0)
    def _():
        put(keep_ref, parts[1])
        put(send_ref, parts[0])

    for copy in copies:
        copy.wait()


def forward(x, gain, cot, weight_a, weight_b):
    rows, width = x.shape
    cols = weight_a.shape[1]
    step = 512
    count = width // step
    half = jax.ShapeDtypeStruct((rows, cols), BF16)
    return pl.pallas_call(
        forward_kernel,
        in_specs=[HBM] * 5,
        out_specs=[VMEM] * 4,
        out_shape=[half] * 2 + [jax.ShapeDtypeStruct((RING, QUARTER, cols), BF16)] * 2,
        scratch_shapes=[pltpu.VMEM((rows, width), BF16), pltpu.VMEM((1, width), F32)]
        + [pltpu.VMEM((count, step, cols), BF16)] * 2
        + [pltpu.VMEM((rows, width), BF16)] * 2
        + [pltpu.SemaphoreType.DMA((3,))]
        + [pltpu.SemaphoreType.DMA((count,))] * 2
        + [pltpu.SemaphoreType.DMA((2 * RING * RING,))],
        compiler_params=params(32),
        cost_estimate=cost(4 * rows * width * cols, 4 * width * cols),
        name="forward",
    )(in_hbm(x), in_hbm(gain), in_hbm(cot), in_hbm(weight_a), in_hbm(weight_b))


def wait_all(copies):
    for copy in copies:
        copy.wait()


def pack_kernel(keep_ref, got_ref, src_ref, dest_ref, mine_ref, other_ref, out_ref, *rest):
    for out, k in zip(rest, (0, 1, 3, 2), strict=True):
        out[0] = mine_ref[k]
        out[1] = other_ref[k]
    spread = slot_onehot(member_index(), src_ref, dest_ref)

    @pl.when(lax.axis_index("section") == 0)
    def _():
        out_ref[...] = jnp.dot(spread, keep_ref[...], preferred_element_type=F32).astype(BF16)

    @pl.when(lax.axis_index("section") != 0)
    def _():
        out_ref[...] = jnp.dot(spread, got_ref[...], preferred_element_type=F32).astype(BF16)


def pack(keep, got, src_len, dest, mine, other):
    width = keep.shape[1]
    _, rows, cols = mine.shape
    outs = pl.pallas_call(
        pack_kernel,
        in_specs=[VMEM] * 6,
        out_specs=[VMEM] * (1 + RING),
        out_shape=[jax.ShapeDtypeStruct((SLOTS, width), BF16)]
        + [jax.ShapeDtypeStruct((2, rows, cols), BF16)] * RING,
        compiler_params=params(),
        cost_estimate=cost(2 * SLOTS * TOK * width, 2 * SLOTS * width),
        name="pack",
    )(keep, got, src_len, dest, mine, other)
    return outs[0], outs[1:]


def attend_kernel(
    keep_ref, got_ref, slots_ref, src_ref, tgt_ref, dest_ref, *rest
):
    front_ref, back_ref, stack_ref, own_ref = rest[RING:]
    for p in range(RING):
        for m in range(2):
            stack_ref[m, p] = rest[p][m]
    mask = pair_mask(member_index(), src_ref, tgt_ref, dest_ref)

    @pl.when(lax.axis_index("section") == 0)
    def _():
        own_ref[...] = got_ref[...]

    @pl.when(lax.axis_index("section") != 0)
    def _():
        own_ref[...] = keep_ref[...]

    half = own_ref.shape[1] // 2
    pair = 2 * HEAD_DIM
    low = iota((1, pair), 1) < HEAD_DIM
    nothing = jnp.zeros((), BF16)

    def both(value):
        return jnp.concatenate(
            [jnp.where(low, value, nothing), jnp.where(low, nothing, value)], axis=0
        )

    def nt(left, right):
        return lax.dot_general(left, right, (((1,), (1,)), ((), ())), preferred_element_type=F32)

    def one(score, dweight):
        expo = jnp.where(mask, jnp.exp(score), 0.0)
        weight = expo * (1.0 / jnp.sum(expo, axis=-1, keepdims=True))
        mean = jnp.sum(weight * dweight, axis=-1, keepdims=True)
        return weight.astype(BF16), (weight * (dweight - mean)).astype(BF16)

    def fold(value):
        return jnp.where(low, value[:SLOTS], value[SLOTS:]).astype(BF16)

    for p in range(half // pair):
        first = slice(p * pair, (p + 1) * pair)
        second = slice(half + p * pair, half + (p + 1) * pair)
        query, dout = own_ref[:, first], own_ref[:, second]
        keys, values = both(slots_ref[:, first]), both(slots_ref[:, second])
        score, dweight = nt(query, keys), nt(dout, values)
        weight_0, dscore_0 = one(score[:, :SLOTS], dweight[:, :SLOTS])
        weight_1, dscore_1 = one(score[:, SLOTS:], dweight[:, SLOTS:])
        weight = jnp.concatenate([weight_0, weight_1], axis=1)
        dscore = jnp.concatenate([dscore_0, dscore_1], axis=1)
        front_ref[:, first] = jnp.dot(dscore, keys, preferred_element_type=F32).astype(BF16)
        front_ref[:, second] = jnp.dot(weight, values, preferred_element_type=F32).astype(BF16)
        back_ref[:, first] = fold(tn(dscore, query))
        back_ref[:, second] = fold(tn(weight, dout))


def attend(keep, got, slots, src_len, tgt_len, dest, pieces):
    rows, width = keep.shape
    _, quarter, cols = pieces[0].shape
    return pl.pallas_call(
        attend_kernel,
        in_specs=[VMEM] * (6 + RING),
        out_specs=[VMEM] * 3,
        out_shape=[
            jax.ShapeDtypeStruct((rows, width), BF16),
            jax.ShapeDtypeStruct((SLOTS, width), BF16),
            jax.ShapeDtypeStruct((2, RING, quarter, cols), BF16),
        ],
        scratch_shapes=[pltpu.VMEM((rows, width), BF16)],
        compiler_params=params(),
        cost_estimate=cost(24 * rows * SLOTS * width, 8 * SLOTS * width),
        name="attend",
    )(keep, got, slots, src_len, tgt_len, dest, *pieces)


def unpack_kernel(back_ref, front_ref, src_ref, dest_ref, keep_ref, send_ref):
    spread = slot_onehot(member_index(), src_ref, dest_ref)
    rows = tn(spread, back_ref[...]).astype(BF16)
    half = rows.shape[1] // 2
    core = lax.axis_index("section")

    @pl.when(core == 0)
    def _():
        keep_ref[:, :half] = rows[:, :half]
        keep_ref[:, half:] = front_ref[:, :half]
        send_ref[:, :half] = front_ref[:, half:]
        send_ref[:, half:] = rows[:, half:]

    @pl.when(core != 0)
    def _():
        keep_ref[:, :half] = front_ref[:, half:]
        keep_ref[:, half:] = rows[:, half:]
        send_ref[:, :half] = rows[:, :half]
        send_ref[:, half:] = front_ref[:, :half]


def unpack(back, front, src_len, dest):
    width = front.shape[1]
    half = jax.ShapeDtypeStruct((TOK, width), BF16)
    return pl.pallas_call(
        unpack_kernel,
        in_specs=[VMEM] * 4,
        out_specs=[VMEM] * 2,
        out_shape=[half, half],
        compiler_params=params(),
        cost_estimate=cost(2 * SLOTS * TOK * width, 4 * SLOTS * width),
        name="unpack",
    )(back, front, src_len, dest)


def join_kernel(keep_ref, got_ref, rows_ref, other_ref):
    width = keep_ref.shape[1]
    half = width // 2
    core = lax.axis_index("section")
    mine = pl.multiple_of(core * half, half)
    theirs = pl.multiple_of((1 - core) * half, half)
    for ref, at in ((keep_ref, mine), (got_ref, theirs)):
        rows_ref[:, pl.ds(at, half)] = ref[:, :half]
        rows_ref[:, pl.ds(pl.multiple_of(width + at, half), half)] = ref[:, half:]
        other_ref[:, pl.ds(at, half)] = ref[:, half:]


def join(keep, got):
    rows, width = keep.shape
    return pl.pallas_call(
        join_kernel,
        in_specs=[VMEM, VMEM],
        out_specs=[VMEM] * 2,
        out_shape=[
            jax.ShapeDtypeStruct((rows, 2 * width), BF16),
            jax.ShapeDtypeStruct((rows, width), BF16),
        ],
        compiler_params=params(),
        cost_estimate=cost(0, 8 * keep.size),
        name="join",
    )(keep, got)


def dnorm_kernel(rows_ref, got_ref, a_hbm, b_hbm, out_ref, a_buf, b_buf, a_sem, b_sem):
    count, step, cols = a_buf.shape
    core = lax.axis_index("section")

    def fetches(hbm, buf, sem):
        return [
            pltpu.make_async_copy(hbm.at[pl.ds(k * step, step), :], buf.at[k], sem.at[k])
            for k in range(count)
        ]

    get_a, get_b = fetches(a_hbm, a_buf, a_sem), fetches(b_hbm, b_buf, b_sem)

    def products(terms):
        for k in range(count):
            for copies, _, _ in terms:
                copies[k].start()
        turned = [rows.T for _, _, rows in terms]
        for k in range(count):
            block = None
            for (copies, weight, _), right in zip(terms, turned, strict=True):
                copies[k].wait()
                part = jnp.dot(weight[k], right, preferred_element_type=F32)
                block = part if block is None else block + part
            out_ref[:, k * step : (k + 1) * step] = block.T.astype(BF16)

    @pl.when(core == 0)
    def _():
        products([(get_a, a_buf, rows_ref[:, :cols]), (get_b, b_buf, got_ref[...])])

    @pl.when(core != 0)
    def _():
        products([(get_a, a_buf, got_ref[...])])


def dnorm_partial(rows, got, weight_a, weight_b):
    width, cols = weight_a.shape
    step = 512
    count = width // step
    return pl.pallas_call(
        dnorm_kernel,
        in_specs=[VMEM] * 2 + [HBM] * 2,
        out_specs=VMEM,
        out_shape=jax.ShapeDtypeStruct((TOK, width), BF16),
        scratch_shapes=[pltpu.VMEM((count, step, cols), BF16)] * 2
        + [pltpu.SemaphoreType.DMA((count,))] * 2,
        compiler_params=params(24),
        cost_estimate=cost(4 * TOK * width * cols, 4 * width * cols),
        name="dnorm",
    )(rows, got, in_hbm(weight_a), in_hbm(weight_b))


def rms_back_kernel(x_hbm, gain_ref, parts_ref, out_ref, x_ref, sem):
    rows = out_ref.shape[0]
    mine = pl.multiple_of(lax.axis_index("mp") * rows, rows)
    get_x = pltpu.make_async_copy(x_hbm.at[pl.ds(mine, rows), :], x_ref, sem)
    get_x.start()
    dnorm = parts_ref[0].astype(F32)
    for i in range(1, RING):
        dnorm += parts_ref[i].astype(F32)
    get_x.wait()
    xf = x_ref[...].astype(F32)
    scale = lax.rsqrt(jnp.mean(xf * xf, axis=-1, keepdims=True) + EPS)
    upper = gain_ref[...] * dnorm
    inner = jnp.mean(xf * upper, axis=-1, keepdims=True)
    out_ref[...] = (scale * upper - xf * (scale * scale * scale * inner)).astype(BF16)


def rms_back(x, gain, parts):
    rows, width = parts.shape[1:]
    return pl.pallas_call(
        rms_back_kernel,
        in_specs=[HBM] + [VMEM] * 2,
        out_specs=VMEM,
        out_shape=jax.ShapeDtypeStruct((rows, width), BF16),
        scratch_shapes=[pltpu.VMEM((rows, width), BF16), pltpu.SemaphoreType.DMA],
        compiler_params=params(),
        cost_estimate=cost(10 * rows * width, 12 * rows * width),
        name="rms_back",
    )(in_hbm(x), gain, parts)


def place_kernel(*refs):
    pieces, (out_hbm, sems) = refs[:RING], refs[RING:]
    rows = pieces[0].shape[0]
    copies = []
    for i, k in enumerate(ORDER):
        at = pl.multiple_of((lax.axis_index("mp") + k) % RING * rows, rows)
        copies.append(pltpu.make_async_copy(pieces[i], out_hbm.at[pl.ds(at, rows), :], sems.at[i]))
        copies[-1].start()
    for copy in copies:
        copy.wait()


def place(pieces):
    rows, width = pieces[0].shape
    return pl.pallas_call(
        place_kernel,
        in_specs=[ANY] * RING,
        out_specs=HBM,
        out_shape=pltpu.HBM((RING * rows, width), BF16),
        scratch_shapes=[pltpu.SemaphoreType.DMA((RING,))],
        compiler_params=params(),
        cost_estimate=cost(0, 4 * RING * rows * width),
        name="place",
    )(*pieces)


def shift(value, axis, k):
    return lax.ppermute(value, axis, [(i, (i + k) % RING) for i in range(RING)])


def gathered(block, axis):
    left = shift(block, axis, 1)
    return [block, left, shift(block, axis, 3), shift(left, axis, 1)]


def moved(value, k, along, across=False):
    pairs = []
    for core in range(2):
        for z in range(RING):
            for x in range(RING):
                to = {"z": z, "x": x}
                to[along[core]] = (to[along[core]] + k) % RING
                target = (1 - core if across else core, to["z"], to["x"])
                pairs.append(
                    ((core * RING + z) * RING + x, (target[0] * RING + target[1]) * RING + target[2])
                )
    return lax.ppermute(value, ("section", "z", "x"), pairs)


GATHER, REDUCE = "xz", "zx"


def fetched(own, others):
    return [own] + [moved(others[k], k, GATHER) for k in (1, 3, 2)]


def left_loads(lefts, buf, sems, ks):
    block = buf.shape[-1]
    mine = lax.axis_index("mp")
    loads = [[[] for _ in ks] for _ in range(2)]
    for f in range(2):
        for i, k in enumerate(ks):
            for j, (left, distance) in enumerate(zip(lefts, ORDER, strict=True)):
                at = pl.multiple_of((mine + distance) % RING * QUARTER, QUARTER)
                loads[f][i].append(
                    pltpu.make_async_copy(
                        left.at[f, :, :, pl.ds(k * block, block)],
                        buf.at[f, i, :, pl.ds(at, QUARTER), :],
                        sems.at[f, i, j],
                    )
                )
                loads[f][i][-1].start()
    return loads


def left_scratch(block, count):
    return [
        pltpu.VMEM((2, count, RING, TOK, block), BF16),
        pltpu.SemaphoreType.DMA((2, count, RING)),
    ]


def flat(value):
    return value.reshape(RING * TOK, value.shape[-1])


def far_kernel(*refs):
    lefts, pieces = refs[:RING], refs[RING : 2 * RING]
    top_ref, low_ref, rows_ref, buf, sems, row_sems = refs[2 * RING :]
    gets = [
        pltpu.make_async_copy(piece, rows_ref.at[pl.ds(i * TOK, TOK), :], row_sems.at[i])
        for i, piece in enumerate(pieces)
    ]
    for get in gets:
        get.start()
    loads = left_loads(lefts, buf, sems, (2,))
    wait_all(gets)
    half, cols = top_ref.shape[0], top_ref.shape[1] // 2
    for m in range(2):
        at = slice(m * cols, (m + 1) * cols)
        wait_all(loads[m][0])
        block = tn(flat(buf[m, 0]), rows_ref[:, at]).astype(BF16)
        top_ref[:, at] = block[:half]
        low_ref[:, at] = block[half:]


def far_block(lefts, pieces):
    rows, cols = pieces[0].shape
    block = lefts[0].shape[-1] // RING
    half = jax.ShapeDtypeStruct((block // 2, cols), BF16)
    return pl.pallas_call(
        far_kernel,
        in_specs=[HBM] * (2 * RING),
        out_specs=[VMEM] * 3,
        out_shape=[half, half, jax.ShapeDtypeStruct((RING * rows, cols), BF16)],
        scratch_shapes=left_scratch(block, 1) + [pltpu.SemaphoreType.DMA((RING,))],
        compiler_params=params(),
        cost_estimate=cost(2 * RING * rows * block * cols, 8 * RING * rows * cols),
        name="far",
    )(*[in_hbm(value) for value in (*lefts, *pieces)])


def side_kernel(*refs):
    lefts, (rows_ref, from_left, from_right) = refs[:RING], refs[RING : RING + 3]
    rights, to_lefts, buf, sems = refs[RING + 3 : RING + 5], refs[RING + 5 : RING + 7], *refs[RING + 7 :]
    loads = left_loads(lefts, buf, sems, (1, 3))
    half, cols = from_left.shape[0], rights[0].shape[1]
    for m in range(2):
        at = slice(m * cols, (m + 1) * cols)

        def product(i, m=m, at=at):
            wait_all(loads[m][i])
            return tn(flat(buf[m, i]), rows_ref[:, at])

        block = product(0)
        rights[m][:half, :] = (block[:half] + from_left[:, at].astype(F32)).astype(BF16)
        rights[m][half:, :] = block[half:].astype(BF16)
        block = product(1)
        to_lefts[m][:half, :] = block[:half].astype(BF16)
        to_lefts[m][half:, :] = (block[half:] + from_right[:, at].astype(F32)).astype(BF16)


def side_blocks(lefts, rows, from_left, from_right):
    depth, cols = rows.shape
    block = lefts[0].shape[-1] // RING
    shape = jax.ShapeDtypeStruct((block, cols // 2), BF16)
    return pl.pallas_call(
        side_kernel,
        in_specs=[HBM] * RING + [VMEM] * 3,
        out_specs=[VMEM] * 4,
        out_shape=[shape] * 4,
        scratch_shapes=left_scratch(block, 2),
        compiler_params=params(),
        cost_estimate=cost(4 * depth * block * cols, 4 * depth * cols),
        name="side",
    )(*[in_hbm(left) for left in lefts], rows, from_left, from_right)


def middle_kernel(*refs):
    lefts, (rows_ref, own_hbm, other_ref, own_ref, buf, sems, out_sem) = refs[:RING], refs[RING:]
    loads = left_loads(lefts, buf, sems, (0,))
    cols = own_ref.shape[1]
    wait_all(loads[0][0])
    own_ref[...] = tn(flat(buf[0, 0]), rows_ref[:, :cols]).astype(BF16)
    put = pltpu.make_async_copy(own_ref, own_hbm, out_sem)
    put.start()
    wait_all(loads[1][0])
    other_ref[...] = tn(flat(buf[1, 0]), rows_ref[:, cols:]).astype(BF16)
    put.wait()


def middle_blocks(lefts, rows):
    depth, cols = rows.shape
    block = lefts[0].shape[-1] // RING
    return pl.pallas_call(
        middle_kernel,
        in_specs=[HBM] * RING + [VMEM],
        out_specs=[HBM, VMEM],
        out_shape=[
            pltpu.HBM((block, cols // 2), BF16),
            jax.ShapeDtypeStruct((block, cols // 2), BF16),
        ],
        scratch_shapes=[pltpu.VMEM((block, cols // 2), BF16)]
        + left_scratch(block, 1)
        + [pltpu.SemaphoreType.DMA],
        compiler_params=params(),
        cost_estimate=cost(2 * depth * block * cols, 4 * depth * cols),
        name="middle",
    )(*[in_hbm(left) for left in lefts], rows)


def own_kernel(own_hbm, other_ref, *refs):
    parts, outs, (own_ref, out_buf, own_sem, out_sems) = refs[:4], refs[4:6], refs[6:]
    get = pltpu.make_async_copy(own_hbm, own_ref, own_sem)
    get.start()
    core = lax.axis_index("section")
    chunks = out_sems.shape[1]
    size = out_buf.shape[1] // chunks

    def put(m, c, out):
        at = slice(c * size, (c + 1) * size)
        return pltpu.make_async_copy(out_buf.at[m, at], out.at[at], out_sems.at[m, c])

    def write(m, c):
        @pl.when(core == m)
        def _():
            put(m, c, outs[0]).start()

        @pl.when(core != m)
        def _():
            put(m, c, outs[1]).start()

    for m, base in ((1, other_ref), (0, own_ref)):
        if m == 0:
            get.wait()
        for c in range(chunks):
            at = slice(c * size, (c + 1) * size)
            total_of = base[at].astype(F32) + parts[2 * m][at].astype(F32)
            out_buf[m, at] = total_of + parts[2 * m + 1][at].astype(F32)
            write(m, c)
    for m in range(2):
        for c in range(chunks):
            put(m, c, outs[0]).wait()


def own_blocks(own, other, parts):
    block, cols = own.shape
    return pl.pallas_call(
        own_kernel,
        in_specs=[HBM] + [VMEM] * 5,
        out_specs=[HBM] * 2,
        out_shape=[pltpu.HBM((block, cols), F32)] * 2,
        scratch_shapes=[
            pltpu.VMEM((block, cols), BF16),
            pltpu.VMEM((2, block, cols), F32),
            pltpu.SemaphoreType.DMA,
            pltpu.SemaphoreType.DMA((2, 4)),
        ],
        compiler_params=params(),
        cost_estimate=cost(4 * block * cols, 20 * block * cols),
        name="own",
    )(in_hbm(own), other, *parts)


def per_device(states, gains, proj_a, proj_b, cotangent, src_len, tgt_len, dest):
    weight_a = proj_a[0]
    weight_b = proj_b[0]
    rows = states[0]
    keep, send, mine, other = forward(rows, gains, cotangent, weight_a, weight_b)
    swap = [(0, 1), (1, 0)]
    got = lax.ppermute(send, "section", swap)
    slots, slices = pack(keep, got, src_len, dest, mine, lax.ppermute(other, "section", swap))
    width = slots.shape[1]
    slots = slots.reshape(SEQ_DEV, MAXLEN, width)
    slots = lax.all_to_all(slots, ("z", "x"), split_axis=0, concat_axis=0, tiled=True)
    slots = slots.reshape(SLOTS, width)
    pieces = fetched(slices[0], {1: slices[1], 3: slices[2], 2: slices[3]})
    front, back, own = attend(keep, got, slots, src_len, tgt_len, dest, pieces)
    lefts = gathered(own, "mp")
    back = back.reshape(SEQ_DEV, MAXLEN, width)
    back = lax.all_to_all(back, ("z", "x"), split_axis=0, concat_axis=0, tiled=True)
    keep, send = unpack(back.reshape(SLOTS, width), front, src_len, dest)
    got = lax.ppermute(send, "section", swap)
    kind, others = join(keep, got)

    rights = fetched(kind, {k: kind for k in (1, 2, 3)})
    others = lax.ppermute(others, "section", swap)
    others, lefts[1], lefts[2] = lax.optimization_barrier((others, lefts[1], lefts[2]))
    partial = dnorm_partial(kind, others, weight_a, weight_b)
    partial, rights[1], rights[2] = lax.optimization_barrier((partial, rights[1], rights[2]))
    parts = lax.all_to_all(
        partial.reshape(RING, TOK // RING, -1), "mp", split_axis=0, concat_axis=0, tiled=True
    )
    top, low, stack = far_block(lefts, rights)
    from_left, from_right = moved(top, 1, REDUCE), moved(low, 3, REDUCE)
    parts, _, _ = lax.optimization_barrier((parts, from_left, from_right))
    right, right_other, left, left_other = side_blocks(lefts, stack, from_left, from_right)
    own, own_other = middle_blocks(lefts, stack)
    sums = [
        moved(right, 1, REDUCE),
        moved(left, 3, REDUCE),
        moved(right_other, 1, REDUCE, True),
        moved(left_other, 3, REDUCE, True),
    ]
    quarter = rms_back(rows, gains, parts)
    grad_states = place(gathered(quarter, "mp"))
    grad_a, grad_b = own_blocks(own, lax.ppermute(own_other, "section", swap), sums)
    return (grad_states[None], grad_a[None], grad_b[None])


def solution(mesh):
    split = jax.sharding.Mesh(mesh.devices.reshape(2, RING, RING, RING), ("section", "z", "x", "mp"))
    dp = ("z", "x")
    return jax.shard_map(
        per_device,
        mesh=split,
        in_specs=(
            P("section", dp, None),
            P("section", None),
            P("section", None, "mp"),
            P("section", None, "mp"),
            P(dp, None),
            P(),
            P(),
            P(),
        ),
        out_specs=(P("section", dp, None), P("section", dp, "mp"), P("section", dp, "mp")),
        check_vma=False,
    )
```

```python
import jax
import jax.numpy as jnp
from jax import lax
from jax.experimental import pallas as pl
from jax.experimental.pallas import tpu as pltpu
from jax.sharding import PartitionSpec as P

HEAD_DIM = 64
SEQ_DEV = 16
MAXLEN = 16
TOK = 128
SLOTS = 256
RING = 4
QUARTER = TOK // RING
ORDER = (0, 3, 1, 2)
EPS = 1e-06
SHARE = 16
F32 = jnp.float32
BF16 = jnp.bfloat16
VMEM = pl.BlockSpec(memory_space=pltpu.VMEM)
ANY = pl.BlockSpec(memory_space=pl.ANY)
HBM = pl.BlockSpec(memory_space=pltpu.HBM)


def iota(shape, dim):
    return lax.broadcasted_iota(jnp.int32, shape, dim)


def total(value, axis):
    return jnp.sum(value.astype(F32), axis=axis, keepdims=True)


def tn(left, right):
    return lax.dot_general(left, right, (((0,), (0,)), ((), ())), preferred_element_type=F32)


def in_hbm(value):
    return pltpu.with_memory_space_constraint(value, pltpu.HBM)


def cost(flops, nbytes):
    return pl.CostEstimate(flops=flops // SHARE, bytes_accessed=nbytes // SHARE, transcendentals=0)


def params(mib=12, **more):
    return pltpu.CompilerParams(vmem_limit_bytes=mib << 20, **more)


def column_of(row):
    square = jnp.broadcast_to(row, (SEQ_DEV, SEQ_DEV))
    same = iota((SEQ_DEV, SEQ_DEV), 0) == iota((SEQ_DEV, SEQ_DEV), 1)
    return total(jnp.where(same, square, 0), 1)


def member_index():
    return lax.axis_index("z") * RING + lax.axis_index("x")


def slot_onehot(member, src_len, dest):
    i, j = iota((SEQ_DEV, SEQ_DEV), 0), iota((SEQ_DEV, SEQ_DEV), 1)
    lengths = src_len[pl.ds(member, 1), :]
    ends = total(jnp.where(j <= i, jnp.broadcast_to(lengths, (SEQ_DEV, SEQ_DEV)), 0), 1)
    begins = ends - column_of(lengths)
    place = column_of(dest[pl.ds(member, 1), :] >> 4) * MAXLEN
    row = iota((SEQ_DEV, TOK), 1).astype(F32)
    inside = (row >= begins) & (row < ends)
    target = total(jnp.where(inside, place + row - begins, 0.0), 0)
    hit = iota((SLOTS, TOK), 0).astype(F32) == target
    return jnp.where(hit, 1.0, 0.0).astype(BF16)


def pair_mask(member, src_len, tgt_len, dest):
    i, j = iota((SEQ_DEV, SEQ_DEV), 0), iota((SEQ_DEV, SEQ_DEV), 1)
    column = column_of(tgt_len[pl.ds(member, 1), :])
    ends = total(jnp.where(i <= j, jnp.broadcast_to(column, (SEQ_DEV, SEQ_DEV)), 0.0), 0)
    row = iota((TOK, SEQ_DEV), 0).astype(F32)
    mine = total(jnp.where(row >= ends, 1.0, 0.0), 1)
    codes = dest[...]
    to_me = (codes >> 4) == member
    target = total(jnp.where(to_me, codes & 15, 0), 1)
    length = total(jnp.where(to_me, src_len[...], 0), 1)
    lane = iota((SEQ_DEV, SLOTS), 1)
    own = (lane >> 4) == iota((SEQ_DEV, SLOTS), 0)
    target = total(jnp.where(own, target, 0.0), 0)
    length = total(jnp.where(own, length, 0.0), 0)
    step = (iota((1, SLOTS), 1) & 15).astype(F32)
    target = jnp.where(step < length, target, -1.0)
    return mine == target


def forward_kernel(
    x_hbm, gain_hbm, cot_hbm, a_hbm, b_hbm, keep_ref, send_ref, *rest
):
    mine_ref, other_ref = rest[:2]
    x_ref, gain_ref, a_buf, b_buf, normed_ref, left_ref, in_sem, a_sem, b_sem, out_sem = rest[2:]
    count, step, cols = a_buf.shape
    core = lax.axis_index("section")
    get_x = pltpu.make_async_copy(x_hbm, x_ref, in_sem.at[0])
    get_gain = pltpu.make_async_copy(gain_hbm, gain_ref, in_sem.at[1])
    get_left = pltpu.make_async_copy(cot_hbm, left_ref, in_sem.at[2])
    get_x.start()
    get_gain.start()

    @pl.when(core != 0)
    def _():
        get_left.start()

    def fetch(k):
        rows = pl.ds(k * step, step)
        return (
            pltpu.make_async_copy(a_hbm.at[rows, :], a_buf.at[k], a_sem.at[k]),
            pltpu.make_async_copy(b_hbm.at[rows, :], b_buf.at[k], b_sem.at[k]),
        )

    for k in range(count):
        for copy in fetch(k):
            copy.start()
    get_x.wait()
    get_gain.wait()
    xf = x_ref[...].astype(F32)
    scale = lax.rsqrt(jnp.mean(xf * xf, axis=-1, keepdims=True) + EPS)
    normed_ref[...] = (xf * scale * gain_ref[...]).astype(BF16)

    @pl.when(core == 0)
    def _():
        left_ref[...] = normed_ref[...]

    @pl.when(core != 0)
    def _():
        get_left.wait()

    z, x = lax.axis_index("z"), lax.axis_index("x")
    quarter = pl.ds(pl.multiple_of(lax.axis_index("mp") * QUARTER, QUARTER), QUARTER)
    block = cols // RING
    copies = []
    for k in range(RING):
        for j in range(RING):
            to = slice(j * block, (j + 1) * block)
            at_x = ((z + j) % RING * RING + (x + k) % RING) * block
            at_z = ((z + k) % RING * RING + (x + j) % RING) * block
            at_mine = jnp.where(core == 0, at_x, at_z)
            at_other = jnp.where(core == 0, at_z, at_x)
            for source, at, out in ((left_ref, at_mine, mine_ref), (normed_ref, at_other, other_ref)):
                copies.append(
                    pltpu.make_async_copy(
                        source.at[quarter, pl.ds(pl.multiple_of(at, block), block)],
                        out.at[k, :, to],
                        out_sem.at[len(copies)],
                    )
                )
                copies[-1].start()

    acc_a = acc_b = None
    for k in range(count):
        for copy in fetch(k):
            copy.wait()
        at = slice(k * step, (k + 1) * step)
        part_a = jnp.dot(normed_ref[:, at], a_buf[k], preferred_element_type=F32)
        part_b = jnp.dot(left_ref[:, at], b_buf[k], preferred_element_type=F32)
        acc_a = part_a if acc_a is None else acc_a + part_a
        acc_b = part_b if acc_b is None else acc_b + part_b
    half = cols // 2
    parts = [[acc[:, i * half : (i + 1) * half].astype(BF16) for acc in (acc_a, acc_b)] for i in range(2)]

    def put(ref, pieces):
        ref[:, :half] = pieces[0]
        ref[:, half:] = pieces[1]

    @pl.when(core == 0)
    def _():
        put(keep_ref, parts[0])
        put(send_ref, parts[1])

    @pl.when(core != 0)
    def _():
        put(keep_ref, parts[1])
        put(send_ref, parts[0])

    for copy in copies:
        copy.wait()


def forward(x, gain, cot, weight_a, weight_b):
    rows, width = x.shape
    cols = weight_a.shape[1]
    step = 512
    count = width // step
    half = jax.ShapeDtypeStruct((rows, cols), BF16)
    return pl.pallas_call(
        forward_kernel,
        in_specs=[HBM] * 5,
        out_specs=[VMEM] * 4,
        out_shape=[half] * 2 + [jax.ShapeDtypeStruct((RING, QUARTER, cols), BF16)] * 2,
        scratch_shapes=[pltpu.VMEM((rows, width), BF16), pltpu.VMEM((1, width), F32)]
        + [pltpu.VMEM((count, step, cols), BF16)] * 2
        + [pltpu.VMEM((rows, width), BF16)] * 2
        + [pltpu.SemaphoreType.DMA((3,))]
        + [pltpu.SemaphoreType.DMA((count,))] * 2
        + [pltpu.SemaphoreType.DMA((2 * RING * RING,))],
        compiler_params=params(32),
        cost_estimate=cost(4 * rows * width * cols, 4 * width * cols),
        name="forward",
    )(in_hbm(x), in_hbm(gain), in_hbm(cot), in_hbm(weight_a), in_hbm(weight_b))


def wait_all(copies):
    for copy in copies:
        copy.wait()


def pack_kernel(keep_ref, got_ref, src_ref, dest_ref, mine_ref, other_ref, out_ref, *rest):
    for out, k in zip(rest, (0, 1, 3, 2), strict=True):
        out[0] = mine_ref[k]
        out[1] = other_ref[k]
    spread = slot_onehot(member_index(), src_ref, dest_ref)

    @pl.when(lax.axis_index("section") == 0)
    def _():
        out_ref[...] = jnp.dot(spread, keep_ref[...], preferred_element_type=F32).astype(BF16)

    @pl.when(lax.axis_index("section") != 0)
    def _():
        out_ref[...] = jnp.dot(spread, got_ref[...], preferred_element_type=F32).astype(BF16)


def pack(keep, got, src_len, dest, mine, other):
    width = keep.shape[1]
    _, rows, cols = mine.shape
    outs = pl.pallas_call(
        pack_kernel,
        in_specs=[VMEM] * 6,
        out_specs=[VMEM] * (1 + RING),
        out_shape=[jax.ShapeDtypeStruct((SLOTS, width), BF16)]
        + [jax.ShapeDtypeStruct((2, rows, cols), BF16)] * RING,
        compiler_params=params(),
        cost_estimate=cost(2 * SLOTS * TOK * width, 2 * SLOTS * width),
        name="pack",
    )(keep, got, src_len, dest, mine, other)
    return outs[0], outs[1:]


def attend_kernel(
    keep_ref, got_ref, slots_ref, src_ref, tgt_ref, dest_ref, *rest
):
    front_ref, back_ref, stack_ref, own_ref = rest[RING:]
    for p in range(RING):
        for m in range(2):
            stack_ref[m, p] = rest[p][m]
    mask = pair_mask(member_index(), src_ref, tgt_ref, dest_ref)

    @pl.when(lax.axis_index("section") == 0)
    def _():
        own_ref[...] = got_ref[...]

    @pl.when(lax.axis_index("section") != 0)
    def _():
        own_ref[...] = keep_ref[...]

    half = own_ref.shape[1] // 2
    pair = 2 * HEAD_DIM
    low = iota((1, pair), 1) < HEAD_DIM
    nothing = jnp.zeros((), BF16)

    def both(value):
        return jnp.concatenate(
            [jnp.where(low, value, nothing), jnp.where(low, nothing, value)], axis=0
        )

    def nt(left, right):
        return lax.dot_general(left, right, (((1,), (1,)), ((), ())), preferred_element_type=F32)

    def one(score, dweight):
        expo = jnp.where(mask, jnp.exp(score), 0.0)
        weight = expo * (1.0 / jnp.sum(expo, axis=-1, keepdims=True))
        mean = jnp.sum(weight * dweight, axis=-1, keepdims=True)
        return weight.astype(BF16), (weight * (dweight - mean)).astype(BF16)

    def fold(value):
        return jnp.where(low, value[:SLOTS], value[SLOTS:]).astype(BF16)

    for p in range(half // pair):
        first = slice(p * pair, (p + 1) * pair)
        second = slice(half + p * pair, half + (p + 1) * pair)
        query, dout = own_ref[:, first], own_ref[:, second]
        keys, values = both(slots_ref[:, first]), both(slots_ref[:, second])
        score, dweight = nt(query, keys), nt(dout, values)
        weight_0, dscore_0 = one(score[:, :SLOTS], dweight[:, :SLOTS])
        weight_1, dscore_1 = one(score[:, SLOTS:], dweight[:, SLOTS:])
        weight = jnp.concatenate([weight_0, weight_1], axis=1)
        dscore = jnp.concatenate([dscore_0, dscore_1], axis=1)
        front_ref[:, first] = jnp.dot(dscore, keys, preferred_element_type=F32).astype(BF16)
        front_ref[:, second] = jnp.dot(weight, values, preferred_element_type=F32).astype(BF16)
        back_ref[:, first] = fold(tn(dscore, query))
        back_ref[:, second] = fold(tn(weight, dout))


def attend(keep, got, slots, src_len, tgt_len, dest, pieces):
    rows, width = keep.shape
    _, quarter, cols = pieces[0].shape
    return pl.pallas_call(
        attend_kernel,
        in_specs=[VMEM] * (6 + RING),
        out_specs=[VMEM] * 3,
        out_shape=[
            jax.ShapeDtypeStruct((rows, width), BF16),
            jax.ShapeDtypeStruct((SLOTS, width), BF16),
            jax.ShapeDtypeStruct((2, RING, quarter, cols), BF16),
        ],
        scratch_shapes=[pltpu.VMEM((rows, width), BF16)],
        compiler_params=params(),
        cost_estimate=cost(24 * rows * SLOTS * width, 8 * SLOTS * width),
        name="attend",
    )(keep, got, slots, src_len, tgt_len, dest, *pieces)


def unpack_kernel(back_ref, front_ref, src_ref, dest_ref, keep_ref, send_ref):
    spread = slot_onehot(member_index(), src_ref, dest_ref)
    rows = tn(spread, back_ref[...]).astype(BF16)
    half = rows.shape[1] // 2
    core = lax.axis_index("section")

    @pl.when(core == 0)
    def _():
        keep_ref[:, :half] = rows[:, :half]
        keep_ref[:, half:] = front_ref[:, :half]
        send_ref[:, :half] = front_ref[:, half:]
        send_ref[:, half:] = rows[:, half:]

    @pl.when(core != 0)
    def _():
        keep_ref[:, :half] = front_ref[:, half:]
        keep_ref[:, half:] = rows[:, half:]
        send_ref[:, :half] = rows[:, :half]
        send_ref[:, half:] = front_ref[:, :half]


def unpack(back, front, src_len, dest):
    width = front.shape[1]
    half = jax.ShapeDtypeStruct((TOK, width), BF16)
    return pl.pallas_call(
        unpack_kernel,
        in_specs=[VMEM] * 4,
        out_specs=[VMEM] * 2,
        out_shape=[half, half],
        compiler_params=params(),
        cost_estimate=cost(2 * SLOTS * TOK * width, 4 * SLOTS * width),
        name="unpack",
    )(back, front, src_len, dest)


def join_kernel(keep_ref, got_ref, rows_ref, other_ref):
    width = keep_ref.shape[1]
    half = width // 2
    core = lax.axis_index("section")
    mine = pl.multiple_of(core * half, half)
    theirs = pl.multiple_of((1 - core) * half, half)
    for ref, at in ((keep_ref, mine), (got_ref, theirs)):
        rows_ref[:, pl.ds(at, half)] = ref[:, :half]
        rows_ref[:, pl.ds(pl.multiple_of(width + at, half), half)] = ref[:, half:]
        other_ref[:, pl.ds(at, half)] = ref[:, half:]


def join(keep, got):
    rows, width = keep.shape
    return pl.pallas_call(
        join_kernel,
        in_specs=[VMEM, VMEM],
        out_specs=[VMEM] * 2,
        out_shape=[
            jax.ShapeDtypeStruct((rows, 2 * width), BF16),
            jax.ShapeDtypeStruct((rows, width), BF16),
        ],
        compiler_params=params(),
        cost_estimate=cost(0, 8 * keep.size),
        name="join",
    )(keep, got)


def dnorm_kernel(rows_ref, got_ref, a_hbm, b_hbm, out_hbm, a_buf, b_buf, out_buf, a_sem, b_sem, out_sem):
    count, step, cols = a_buf.shape
    core = lax.axis_index("section")

    def nt(left, right):
        return lax.dot_general(left, right, (((1,), (1,)), ((), ())), preferred_element_type=F32)

    def fetches(hbm, buf, sem):
        return [
            pltpu.make_async_copy(hbm.at[pl.ds(k * step, step), :], buf.at[k], sem.at[k])
            for k in range(count)
        ]

    get_a, get_b = fetches(a_hbm, a_buf, a_sem), fetches(b_hbm, b_buf, b_sem)

    def put(k):
        at = slice(k * step, (k + 1) * step)
        return pltpu.make_async_copy(out_buf.at[:, at], out_hbm.at[:, at], out_sem.at[k])

    @pl.when(core == 0)
    def _():
        for k in range(count):
            get_a[k].start()
            get_b[k].start()
        for k in range(count):
            get_a[k].wait()
            get_b[k].wait()
            block = nt(rows_ref[:, :cols], a_buf[k]) + nt(got_ref[...], b_buf[k])
            out_buf[:, k * step : (k + 1) * step] = block.astype(BF16)
            put(k).start()

    @pl.when(core != 0)
    def _():
        for k in range(count):
            get_a[k].start()
        for k in range(count):
            get_a[k].wait()
            out_buf[:, k * step : (k + 1) * step] = nt(got_ref[...], a_buf[k]).astype(BF16)
            put(k).start()

    for k in range(count):
        put(k).wait()


def dnorm_partial(rows, got, weight_a, weight_b):
    width, cols = weight_a.shape
    step = 512
    count = width // step
    return pl.pallas_call(
        dnorm_kernel,
        in_specs=[VMEM] * 2 + [HBM] * 2,
        out_specs=HBM,
        out_shape=pltpu.HBM((TOK, width), BF16),
        scratch_shapes=[pltpu.VMEM((count, step, cols), BF16)] * 2
        + [pltpu.VMEM((TOK, width), BF16)]
        + [pltpu.SemaphoreType.DMA((count,))] * 3,
        compiler_params=params(24),
        cost_estimate=cost(4 * TOK * width * cols, 4 * width * cols),
        name="dnorm",
    )(rows, got, in_hbm(weight_a), in_hbm(weight_b))


def rms_back_kernel(x_hbm, gain_ref, parts_ref, out_ref, x_ref, sem):
    rows = out_ref.shape[0]
    mine = pl.multiple_of(lax.axis_index("mp") * rows, rows)
    get_x = pltpu.make_async_copy(x_hbm.at[pl.ds(mine, rows), :], x_ref, sem)
    get_x.start()
    dnorm = parts_ref[0].astype(F32)
    for i in range(1, RING):
        dnorm += parts_ref[i].astype(F32)
    get_x.wait()
    xf = x_ref[...].astype(F32)
    scale = lax.rsqrt(jnp.mean(xf * xf, axis=-1, keepdims=True) + EPS)
    upper = gain_ref[...] * dnorm
    inner = jnp.mean(xf * upper, axis=-1, keepdims=True)
    out_ref[...] = (scale * upper - xf * (scale * scale * scale * inner)).astype(BF16)


def rms_back(x, gain, parts):
    rows, width = parts.shape[1:]
    return pl.pallas_call(
        rms_back_kernel,
        in_specs=[HBM] + [VMEM] * 2,
        out_specs=VMEM,
        out_shape=jax.ShapeDtypeStruct((rows, width), BF16),
        scratch_shapes=[pltpu.VMEM((rows, width), BF16), pltpu.SemaphoreType.DMA],
        compiler_params=params(),
        cost_estimate=cost(10 * rows * width, 12 * rows * width),
        name="rms_back",
    )(in_hbm(x), gain, parts)


def place_kernel(*refs):
    pieces, (out_hbm, sems) = refs[:RING], refs[RING:]
    rows = pieces[0].shape[0]
    copies = []
    for i, k in enumerate(ORDER):
        at = pl.multiple_of((lax.axis_index("mp") + k) % RING * rows, rows)
        copies.append(pltpu.make_async_copy(pieces[i], out_hbm.at[pl.ds(at, rows), :], sems.at[i]))
        copies[-1].start()
    for copy in copies:
        copy.wait()


def place(pieces):
    rows, width = pieces[0].shape
    return pl.pallas_call(
        place_kernel,
        in_specs=[ANY] * RING,
        out_specs=HBM,
        out_shape=pltpu.HBM((RING * rows, width), BF16),
        scratch_shapes=[pltpu.SemaphoreType.DMA((RING,))],
        compiler_params=params(),
        cost_estimate=cost(0, 4 * RING * rows * width),
        name="place",
    )(*pieces)


def shift(value, axis, k):
    return lax.ppermute(value, axis, [(i, (i + k) % RING) for i in range(RING)])


def gathered(block, axis):
    left, right = lax.optimization_barrier((shift(block, axis, 1), shift(block, axis, 3)))
    return [block, left, right, shift(left, axis, 1)]


def moved(value, k, along, across=False):
    pairs = []
    for core in range(2):
        for z in range(RING):
            for x in range(RING):
                to = {"z": z, "x": x}
                to[along[core]] = (to[along[core]] + k) % RING
                target = (1 - core if across else core, to["z"], to["x"])
                pairs.append(
                    ((core * RING + z) * RING + x, (target[0] * RING + target[1]) * RING + target[2])
                )
    return lax.ppermute(value, ("section", "z", "x"), pairs)


GATHER, REDUCE = "xz", "zx"


def fetched(own, others):
    return [own] + [moved(others[k], k, GATHER) for k in (1, 3, 2)]


def left_loads(lefts, buf, sems, ks):
    block = buf.shape[-1]
    mine = lax.axis_index("mp")
    loads = [[[] for _ in ks] for _ in range(2)]
    for f in range(2):
        for i, k in enumerate(ks):
            for j, (left, distance) in enumerate(zip(lefts, ORDER, strict=True)):
                at = pl.multiple_of((mine + distance) % RING * QUARTER, QUARTER)
                loads[f][i].append(
                    pltpu.make_async_copy(
                        left.at[f, :, :, pl.ds(k * block, block)],
                        buf.at[f, i, :, pl.ds(at, QUARTER), :],
                        sems.at[f, i, j],
                    )
                )
                loads[f][i][-1].start()
    return loads


def left_scratch(block, count):
    return [
        pltpu.VMEM((2, count, RING, TOK, block), BF16),
        pltpu.SemaphoreType.DMA((2, count, RING)),
    ]


def flat(value):
    return value.reshape(RING * TOK, value.shape[-1])


def far_kernel(*refs):
    lefts, pieces = refs[:RING], refs[RING : 2 * RING]
    top_ref, low_ref, rows_ref, buf, sems = refs[2 * RING :]
    loads = left_loads(lefts, buf, sems, (2,))
    for i, piece in enumerate(pieces):
        rows_ref[i * TOK : (i + 1) * TOK, :] = piece[...]
    half, cols = top_ref.shape[0], top_ref.shape[1] // 2
    for m in range(2):
        at = slice(m * cols, (m + 1) * cols)
        wait_all(loads[m][0])
        block = tn(flat(buf[m, 0]), rows_ref[:, at]).astype(BF16)
        top_ref[:, at] = block[:half]
        low_ref[:, at] = block[half:]


def far_block(lefts, pieces):
    rows, cols = pieces[0].shape
    block = lefts[0].shape[-1] // RING
    half = jax.ShapeDtypeStruct((block // 2, cols), BF16)
    return pl.pallas_call(
        far_kernel,
        in_specs=[HBM] * RING + [VMEM] * RING,
        out_specs=[VMEM] * 3,
        out_shape=[half, half, jax.ShapeDtypeStruct((RING * rows, cols), BF16)],
        scratch_shapes=left_scratch(block, 1),
        compiler_params=params(),
        cost_estimate=cost(2 * RING * rows * block * cols, 8 * RING * rows * cols),
        name="far",
    )(*[in_hbm(left) for left in lefts], *pieces)


def side_kernel(*refs):
    lefts, (rows_ref, from_left, from_right) = refs[:RING], refs[RING : RING + 3]
    rights, to_lefts, buf, sems = refs[RING + 3 : RING + 5], refs[RING + 5 : RING + 7], *refs[RING + 7 :]
    loads = left_loads(lefts, buf, sems, (1, 3))
    half, cols = from_left.shape[0], rights[0].shape[1]
    for m in range(2):
        at = slice(m * cols, (m + 1) * cols)

        def product(i, m=m, at=at):
            wait_all(loads[m][i])
            return tn(flat(buf[m, i]), rows_ref[:, at])

        block = product(0)
        rights[m][:half, :] = (block[:half] + from_left[:, at].astype(F32)).astype(BF16)
        rights[m][half:, :] = block[half:].astype(BF16)
        block = product(1)
        to_lefts[m][:half, :] = block[:half].astype(BF16)
        to_lefts[m][half:, :] = (block[half:] + from_right[:, at].astype(F32)).astype(BF16)


def side_blocks(lefts, rows, from_left, from_right):
    depth, cols = rows.shape
    block = lefts[0].shape[-1] // RING
    shape = jax.ShapeDtypeStruct((block, cols // 2), BF16)
    return pl.pallas_call(
        side_kernel,
        in_specs=[HBM] * RING + [VMEM] * 3,
        out_specs=[VMEM] * 4,
        out_shape=[shape] * 4,
        scratch_shapes=left_scratch(block, 2),
        compiler_params=params(),
        cost_estimate=cost(4 * depth * block * cols, 4 * depth * cols),
        name="side",
    )(*[in_hbm(left) for left in lefts], rows, from_left, from_right)


def middle_kernel(*refs):
    lefts, (rows_ref, own_hbm, other_hbm, out_buf, buf, sems, out_sems) = refs[:RING], refs[RING:]
    loads = left_loads(lefts, buf, sems, (0,))
    cols = out_buf.shape[2]
    puts = []
    for m, out in enumerate((own_hbm, other_hbm)):
        wait_all(loads[m][0])
        at = slice(m * cols, (m + 1) * cols)
        out_buf[m] = tn(flat(buf[m, 0]), rows_ref[:, at]).astype(BF16)
        puts.append(pltpu.make_async_copy(out_buf.at[m], out, out_sems.at[m]))
        puts[-1].start()
    wait_all(puts)


def middle_blocks(lefts, rows):
    depth, cols = rows.shape
    block = lefts[0].shape[-1] // RING
    return pl.pallas_call(
        middle_kernel,
        in_specs=[HBM] * RING + [VMEM],
        out_specs=[HBM] * 2,
        out_shape=[pltpu.HBM((block, cols // 2), BF16)] * 2,
        scratch_shapes=[pltpu.VMEM((2, block, cols // 2), BF16)]
        + left_scratch(block, 1)
        + [pltpu.SemaphoreType.DMA((2,))],
        compiler_params=params(),
        cost_estimate=cost(2 * depth * block * cols, 4 * depth * cols),
        name="middle",
    )(*[in_hbm(left) for left in lefts], rows)


def own_kernel(own_hbm, other_ref, *refs):
    parts, outs, (own_ref, out_buf, own_sem, out_sems) = refs[:4], refs[4:6], refs[6:]
    get = pltpu.make_async_copy(own_hbm, own_ref, own_sem)
    get.start()
    core = lax.axis_index("section")
    chunks = out_sems.shape[1]
    size = out_buf.shape[1] // chunks

    def put(m, c, out):
        at = slice(c * size, (c + 1) * size)
        return pltpu.make_async_copy(out_buf.at[m, at], out.at[at], out_sems.at[m, c])

    def write(m, c):
        @pl.when(core == m)
        def _():
            put(m, c, outs[0]).start()

        @pl.when(core != m)
        def _():
            put(m, c, outs[1]).start()

    for m, base in ((1, other_ref), (0, own_ref)):
        if m == 0:
            get.wait()
        for c in range(chunks):
            at = slice(c * size, (c + 1) * size)
            total_of = base[at].astype(F32) + parts[2 * m][at].astype(F32)
            out_buf[m, at] = total_of + parts[2 * m + 1][at].astype(F32)
            write(m, c)
    for m in range(2):
        for c in range(chunks):
            put(m, c, outs[0]).wait()


def own_blocks(own, other, parts):
    block, cols = own.shape
    return pl.pallas_call(
        own_kernel,
        in_specs=[HBM] + [VMEM] * 5,
        out_specs=[HBM] * 2,
        out_shape=[pltpu.HBM((block, cols), F32)] * 2,
        scratch_shapes=[
            pltpu.VMEM((block, cols), BF16),
            pltpu.VMEM((2, block, cols), F32),
            pltpu.SemaphoreType.DMA,
            pltpu.SemaphoreType.DMA((2, 4)),
        ],
        compiler_params=params(),
        cost_estimate=cost(4 * block * cols, 20 * block * cols),
        name="own",
    )(in_hbm(own), other, *parts)


def per_device(states, gains, proj_a, proj_b, cotangent, src_len, tgt_len, dest):
    weight_a = proj_a[0]
    weight_b = proj_b[0]
    rows = states[0]
    keep, send, mine, other = forward(rows, gains, cotangent, weight_a, weight_b)
    swap = [(0, 1), (1, 0)]
    got = lax.ppermute(send, "section", swap)
    slots, slices = pack(keep, got, src_len, dest, mine, lax.ppermute(other, "section", swap))
    width = slots.shape[1]
    slots = slots.reshape(SEQ_DEV, MAXLEN, width)
    slots = lax.all_to_all(slots, ("z", "x"), split_axis=0, concat_axis=0, tiled=True)
    slots = slots.reshape(SLOTS, width)
    pieces = fetched(slices[0], {1: slices[1], 3: slices[2], 2: slices[3]})
    front, back, own = attend(keep, got, slots, src_len, tgt_len, dest, pieces)
    lefts = gathered(own, "mp")
    back = back.reshape(SEQ_DEV, MAXLEN, width)
    back = lax.all_to_all(back, ("z", "x"), split_axis=0, concat_axis=0, tiled=True)
    keep, send = unpack(back.reshape(SLOTS, width), front, src_len, dest)
    got = lax.ppermute(send, "section", swap)
    kind, others = join(keep, got)

    rights = fetched(kind, {k: kind for k in (1, 2, 3)})
    others = lax.ppermute(others, "section", swap)
    others, lefts[1], lefts[2] = lax.optimization_barrier((others, lefts[1], lefts[2]))
    partial = dnorm_partial(kind, others, weight_a, weight_b)
    partial, rights[1], rights[2] = lax.optimization_barrier((partial, rights[1], rights[2]))
    parts = lax.all_to_all(
        partial.reshape(RING, TOK // RING, -1), "mp", split_axis=0, concat_axis=0, tiled=True
    )
    top, low, stack = far_block(lefts, rights)
    from_left, from_right = moved(top, 1, REDUCE), moved(low, 3, REDUCE)
    parts, _, _ = lax.optimization_barrier((parts, from_left, from_right))
    right, right_other, left, left_other = side_blocks(lefts, stack, from_left, from_right)
    own, own_other = middle_blocks(lefts, stack)
    own_other, _ = lax.optimization_barrier((own_other, right))
    sums = [
        moved(right, 1, REDUCE),
        moved(left, 3, REDUCE),
        moved(right_other, 1, REDUCE, True),
        moved(left_other, 3, REDUCE, True),
    ]
    quarter = rms_back(rows, gains, parts)
    grad_states = place(gathered(quarter, "mp"))
    grad_a, grad_b = own_blocks(own, lax.ppermute(own_other, "section", swap), sums)
    return (grad_states[None], grad_a[None], grad_b[None])


def solution(mesh):
    split = jax.sharding.Mesh(mesh.devices.reshape(2, RING, RING, RING), ("section", "z", "x", "mp"))
    dp = ("z", "x")
    return jax.shard_map(
        per_device,
        mesh=split,
        in_specs=(
            P("section", dp, None),
            P("section", None),
            P("section", None, "mp"),
            P("section", None, "mp"),
            P(dp, None),
            P(),
            P(),
            P(),
        ),
        out_specs=(P("section", dp, None), P("section", dp, "mp"), P("section", dp, "mp")),
        check_vma=False,
    )
```

```python
import jax
import jax.numpy as jnp
from jax import lax
from jax.experimental import pallas as pl
from jax.experimental.pallas import tpu as pltpu
from jax.sharding import PartitionSpec as P

HEAD_DIM = 64
SEQ_DEV = 16
MAXLEN = 16
TOK = 128
SLOTS = 256
RING = 4
QUARTER = TOK // RING
ORDER = (0, 3, 1, 2)
EPS = 1e-06
SHARE = 16
F32 = jnp.float32
BF16 = jnp.bfloat16
VMEM = pl.BlockSpec(memory_space=pltpu.VMEM)
ANY = pl.BlockSpec(memory_space=pl.ANY)
HBM = pl.BlockSpec(memory_space=pltpu.HBM)


def iota(shape, dim):
    return lax.broadcasted_iota(jnp.int32, shape, dim)


def total(value, axis):
    return jnp.sum(value.astype(F32), axis=axis, keepdims=True)


def tn(left, right):
    return lax.dot_general(left, right, (((0,), (0,)), ((), ())), preferred_element_type=F32)


def in_hbm(value):
    return pltpu.with_memory_space_constraint(value, pltpu.HBM)


def cost(flops, nbytes):
    return pl.CostEstimate(flops=flops // SHARE, bytes_accessed=nbytes // SHARE, transcendentals=0)


def params(mib=12, **more):
    return pltpu.CompilerParams(vmem_limit_bytes=mib << 20, **more)


def column_of(row):
    square = jnp.broadcast_to(row, (SEQ_DEV, SEQ_DEV))
    same = iota((SEQ_DEV, SEQ_DEV), 0) == iota((SEQ_DEV, SEQ_DEV), 1)
    return total(jnp.where(same, square, 0), 1)


def member_index():
    return lax.axis_index("z") * RING + lax.axis_index("x")


def slot_onehot(member, src_len, dest):
    i, j = iota((SEQ_DEV, SEQ_DEV), 0), iota((SEQ_DEV, SEQ_DEV), 1)
    lengths = src_len[pl.ds(member, 1), :]
    ends = total(jnp.where(j <= i, jnp.broadcast_to(lengths, (SEQ_DEV, SEQ_DEV)), 0), 1)
    begins = ends - column_of(lengths)
    place = column_of(dest[pl.ds(member, 1), :] >> 4) * MAXLEN
    row = iota((SEQ_DEV, TOK), 1).astype(F32)
    inside = (row >= begins) & (row < ends)
    target = total(jnp.where(inside, place + row - begins, 0.0), 0)
    hit = iota((SLOTS, TOK), 0).astype(F32) == target
    return jnp.where(hit, 1.0, 0.0).astype(BF16)


def pair_mask(member, src_len, tgt_len, dest):
    i, j = iota((SEQ_DEV, SEQ_DEV), 0), iota((SEQ_DEV, SEQ_DEV), 1)
    column = column_of(tgt_len[pl.ds(member, 1), :])
    ends = total(jnp.where(i <= j, jnp.broadcast_to(column, (SEQ_DEV, SEQ_DEV)), 0.0), 0)
    row = iota((TOK, SEQ_DEV), 0).astype(F32)
    mine = total(jnp.where(row >= ends, 1.0, 0.0), 1)
    codes = dest[...]
    to_me = (codes >> 4) == member
    target = total(jnp.where(to_me, codes & 15, 0), 1)
    length = total(jnp.where(to_me, src_len[...], 0), 1)
    lane = iota((SEQ_DEV, SLOTS), 1)
    own = (lane >> 4) == iota((SEQ_DEV, SLOTS), 0)
    target = total(jnp.where(own, target, 0.0), 0)
    length = total(jnp.where(own, length, 0.0), 0)
    step = (iota((1, SLOTS), 1) & 15).astype(F32)
    target = jnp.where(step < length, target, -1.0)
    return mine == target


def forward_kernel(
    x_hbm, gain_hbm, cot_hbm, a_hbm, b_hbm, keep_ref, send_ref, *rest
):
    mine_ref, other_ref = rest[:2]
    x_ref, gain_ref, a_buf, b_buf, normed_ref, left_ref, in_sem, a_sem, b_sem, out_sem = rest[2:]
    count, step, cols = a_buf.shape
    core = lax.axis_index("section")
    get_x = pltpu.make_async_copy(x_hbm, x_ref, in_sem.at[0])
    get_gain = pltpu.make_async_copy(gain_hbm, gain_ref, in_sem.at[1])
    get_left = pltpu.make_async_copy(cot_hbm, left_ref, in_sem.at[2])
    get_x.start()
    get_gain.start()

    @pl.when(core != 0)
    def _():
        get_left.start()

    def fetch(k):
        rows = pl.ds(k * step, step)
        return (
            pltpu.make_async_copy(a_hbm.at[rows, :], a_buf.at[k], a_sem.at[k]),
            pltpu.make_async_copy(b_hbm.at[rows, :], b_buf.at[k], b_sem.at[k]),
        )

    for k in range(count):
        for copy in fetch(k):
            copy.start()
    get_x.wait()
    get_gain.wait()
    xf = x_ref[...].astype(F32)
    scale = lax.rsqrt(jnp.mean(xf * xf, axis=-1, keepdims=True) + EPS)
    normed_ref[...] = (xf * scale * gain_ref[...]).astype(BF16)

    @pl.when(core == 0)
    def _():
        left_ref[...] = normed_ref[...]

    @pl.when(core != 0)
    def _():
        get_left.wait()

    z, x = lax.axis_index("z"), lax.axis_index("x")
    quarter = pl.ds(pl.multiple_of(lax.axis_index("mp") * QUARTER, QUARTER), QUARTER)
    block = cols // RING
    copies = []
    for k in range(RING):
        for j in range(RING):
            to = slice(j * block, (j + 1) * block)
            at_x = ((z + j) % RING * RING + (x + k) % RING) * block
            at_z = ((z + k) % RING * RING + (x + j) % RING) * block
            at_mine = jnp.where(core == 0, at_x, at_z)
            at_other = jnp.where(core == 0, at_z, at_x)
            for source, at, out in ((left_ref, at_mine, mine_ref), (normed_ref, at_other, other_ref)):
                copies.append(
                    pltpu.make_async_copy(
                        source.at[quarter, pl.ds(pl.multiple_of(at, block), block)],
                        out.at[k, :, to],
                        out_sem.at[len(copies)],
                    )
                )
                copies[-1].start()

    acc_a = acc_b = None
    for k in range(count):
        for copy in fetch(k):
            copy.wait()
        at = slice(k * step, (k + 1) * step)
        part_a = jnp.dot(normed_ref[:, at], a_buf[k], preferred_element_type=F32)
        part_b = jnp.dot(left_ref[:, at], b_buf[k], preferred_element_type=F32)
        acc_a = part_a if acc_a is None else acc_a + part_a
        acc_b = part_b if acc_b is None else acc_b + part_b
    half = cols // 2
    parts = [[acc[:, i * half : (i + 1) * half].astype(BF16) for acc in (acc_a, acc_b)] for i in range(2)]

    def put(ref, pieces):
        ref[:, :half] = pieces[0]
        ref[:, half:] = pieces[1]

    @pl.when(core == 0)
    def _():
        put(keep_ref, parts[0])
        put(send_ref, parts[1])

    @pl.when(core != 0)
    def _():
        put(keep_ref, parts[1])
        put(send_ref, parts[0])

    for copy in copies:
        copy.wait()


def forward(x, gain, cot, weight_a, weight_b):
    rows, width = x.shape
    cols = weight_a.shape[1]
    step = 512
    count = width // step
    half = jax.ShapeDtypeStruct((rows, cols), BF16)
    return pl.pallas_call(
        forward_kernel,
        in_specs=[HBM] * 5,
        out_specs=[VMEM] * 4,
        out_shape=[half] * 2 + [jax.ShapeDtypeStruct((RING, QUARTER, cols), BF16)] * 2,
        scratch_shapes=[pltpu.VMEM((rows, width), BF16), pltpu.VMEM((1, width), F32)]
        + [pltpu.VMEM((count, step, cols), BF16)] * 2
        + [pltpu.VMEM((rows, width), BF16)] * 2
        + [pltpu.SemaphoreType.DMA((3,))]
        + [pltpu.SemaphoreType.DMA((count,))] * 2
        + [pltpu.SemaphoreType.DMA((2 * RING * RING,))],
        compiler_params=params(32),
        cost_estimate=cost(4 * rows * width * cols, 4 * width * cols),
        name="forward",
    )(in_hbm(x), in_hbm(gain), in_hbm(cot), in_hbm(weight_a), in_hbm(weight_b))


def wait_all(copies):
    for copy in copies:
        copy.wait()


def pack_kernel(keep_ref, got_ref, src_ref, dest_ref, mine_ref, other_ref, out_ref, *rest):
    for out, k in zip(rest, (0, 1, 3, 2), strict=True):
        out[0] = mine_ref[k]
        out[1] = other_ref[k]
    spread = slot_onehot(member_index(), src_ref, dest_ref)

    @pl.when(lax.axis_index("section") == 0)
    def _():
        out_ref[...] = jnp.dot(spread, keep_ref[...], preferred_element_type=F32).astype(BF16)

    @pl.when(lax.axis_index("section") != 0)
    def _():
        out_ref[...] = jnp.dot(spread, got_ref[...], preferred_element_type=F32).astype(BF16)


def pack(keep, got, src_len, dest, mine, other):
    width = keep.shape[1]
    _, rows, cols = mine.shape
    outs = pl.pallas_call(
        pack_kernel,
        in_specs=[VMEM] * 6,
        out_specs=[VMEM] * (1 + RING),
        out_shape=[jax.ShapeDtypeStruct((SLOTS, width), BF16)]
        + [jax.ShapeDtypeStruct((2, rows, cols), BF16)] * RING,
        compiler_params=params(),
        cost_estimate=cost(2 * SLOTS * TOK * width, 2 * SLOTS * width),
        name="pack",
    )(keep, got, src_len, dest, mine, other)
    return outs[0], outs[1:]


def attend_kernel(
    keep_ref, got_ref, slots_ref, src_ref, tgt_ref, dest_ref, *rest
):
    front_ref, back_ref, stack_ref, own_ref = rest[RING:]
    for p in range(RING):
        for m in range(2):
            stack_ref[m, p] = rest[p][m]
    mask = pair_mask(member_index(), src_ref, tgt_ref, dest_ref)

    @pl.when(lax.axis_index("section") == 0)
    def _():
        own_ref[...] = got_ref[...]

    @pl.when(lax.axis_index("section") != 0)
    def _():
        own_ref[...] = keep_ref[...]

    half = own_ref.shape[1] // 2
    pair = 2 * HEAD_DIM
    low = iota((1, pair), 1) < HEAD_DIM
    nothing = jnp.zeros((), BF16)

    def both(value):
        return jnp.concatenate(
            [jnp.where(low, value, nothing), jnp.where(low, nothing, value)], axis=0
        )

    def nt(left, right):
        return lax.dot_general(left, right, (((1,), (1,)), ((), ())), preferred_element_type=F32)

    def one(score, dweight):
        expo = jnp.where(mask, jnp.exp(score), 0.0)
        weight = expo * (1.0 / jnp.sum(expo, axis=-1, keepdims=True))
        mean = jnp.sum(weight * dweight, axis=-1, keepdims=True)
        return weight.astype(BF16), (weight * (dweight - mean)).astype(BF16)

    def fold(value):
        return jnp.where(low, value[:SLOTS], value[SLOTS:]).astype(BF16)

    for p in range(half // pair):
        first = slice(p * pair, (p + 1) * pair)
        second = slice(half + p * pair, half + (p + 1) * pair)
        query, dout = own_ref[:, first], own_ref[:, second]
        keys, values = both(slots_ref[:, first]), both(slots_ref[:, second])
        score, dweight = nt(query, keys), nt(dout, values)
        weight_0, dscore_0 = one(score[:, :SLOTS], dweight[:, :SLOTS])
        weight_1, dscore_1 = one(score[:, SLOTS:], dweight[:, SLOTS:])
        weight = jnp.concatenate([weight_0, weight_1], axis=1)
        dscore = jnp.concatenate([dscore_0, dscore_1], axis=1)
        front_ref[:, first] = jnp.dot(dscore, keys, preferred_element_type=F32).astype(BF16)
        front_ref[:, second] = jnp.dot(weight, values, preferred_element_type=F32).astype(BF16)
        back_ref[:, first] = fold(tn(dscore, query))
        back_ref[:, second] = fold(tn(weight, dout))


def attend(keep, got, slots, src_len, tgt_len, dest, pieces):
    rows, width = keep.shape
    _, quarter, cols = pieces[0].shape
    return pl.pallas_call(
        attend_kernel,
        in_specs=[VMEM] * (6 + RING),
        out_specs=[VMEM] * 3,
        out_shape=[
            jax.ShapeDtypeStruct((rows, width), BF16),
            jax.ShapeDtypeStruct((SLOTS, width), BF16),
            jax.ShapeDtypeStruct((2, RING, quarter, cols), BF16),
        ],
        scratch_shapes=[pltpu.VMEM((rows, width), BF16)],
        compiler_params=params(),
        cost_estimate=cost(24 * rows * SLOTS * width, 8 * SLOTS * width),
        name="attend",
    )(keep, got, slots, src_len, tgt_len, dest, *pieces)


def unpack_kernel(back_ref, front_ref, src_ref, dest_ref, keep_ref, send_ref):
    spread = slot_onehot(member_index(), src_ref, dest_ref)
    rows = tn(spread, back_ref[...]).astype(BF16)
    half = rows.shape[1] // 2
    core = lax.axis_index("section")

    @pl.when(core == 0)
    def _():
        keep_ref[:, :half] = rows[:, :half]
        keep_ref[:, half:] = front_ref[:, :half]
        send_ref[:, :half] = front_ref[:, half:]
        send_ref[:, half:] = rows[:, half:]

    @pl.when(core != 0)
    def _():
        keep_ref[:, :half] = front_ref[:, half:]
        keep_ref[:, half:] = rows[:, half:]
        send_ref[:, :half] = rows[:, :half]
        send_ref[:, half:] = front_ref[:, :half]


def unpack(back, front, src_len, dest):
    width = front.shape[1]
    half = jax.ShapeDtypeStruct((TOK, width), BF16)
    return pl.pallas_call(
        unpack_kernel,
        in_specs=[VMEM] * 4,
        out_specs=[VMEM] * 2,
        out_shape=[half, half],
        compiler_params=params(),
        cost_estimate=cost(2 * SLOTS * TOK * width, 4 * SLOTS * width),
        name="unpack",
    )(back, front, src_len, dest)


def join_kernel(keep_ref, got_ref, rows_ref, other_ref):
    width = keep_ref.shape[1]
    half = width // 2
    core = lax.axis_index("section")
    mine = pl.multiple_of(core * half, half)
    theirs = pl.multiple_of((1 - core) * half, half)
    for ref, at in ((keep_ref, mine), (got_ref, theirs)):
        rows_ref[:, pl.ds(at, half)] = ref[:, :half]
        rows_ref[:, pl.ds(pl.multiple_of(width + at, half), half)] = ref[:, half:]
        other_ref[:, pl.ds(at, half)] = ref[:, half:]


def join(keep, got):
    rows, width = keep.shape
    return pl.pallas_call(
        join_kernel,
        in_specs=[VMEM, VMEM],
        out_specs=[VMEM] * 2,
        out_shape=[
            jax.ShapeDtypeStruct((rows, 2 * width), BF16),
            jax.ShapeDtypeStruct((rows, width), BF16),
        ],
        compiler_params=params(),
        cost_estimate=cost(0, 8 * keep.size),
        name="join",
    )(keep, got)


def dnorm_kernel(rows_ref, got_ref, a_hbm, b_hbm, out_hbm, a_buf, b_buf, out_buf, a_sem, b_sem, out_sem):
    count, step, cols = a_buf.shape
    core = lax.axis_index("section")

    def nt(left, right):
        return lax.dot_general(left, right, (((1,), (1,)), ((), ())), preferred_element_type=F32)

    def fetches(hbm, buf, sem):
        return [
            pltpu.make_async_copy(hbm.at[pl.ds(k * step, step), :], buf.at[k], sem.at[k])
            for k in range(count)
        ]

    get_a, get_b = fetches(a_hbm, a_buf, a_sem), fetches(b_hbm, b_buf, b_sem)

    def put(k):
        at = slice(k * step, (k + 1) * step)
        return pltpu.make_async_copy(out_buf.at[:, at], out_hbm.at[:, at], out_sem.at[k])

    @pl.when(core == 0)
    def _():
        for k in range(count):
            get_a[k].start()
            get_b[k].start()
        for k in range(count):
            get_a[k].wait()
            get_b[k].wait()
            block = nt(rows_ref[:, :cols], a_buf[k]) + nt(got_ref[...], b_buf[k])
            out_buf[:, k * step : (k + 1) * step] = block.astype(BF16)
            put(k).start()

    @pl.when(core != 0)
    def _():
        for k in range(count):
            get_a[k].start()
        for k in range(count):
            get_a[k].wait()
            out_buf[:, k * step : (k + 1) * step] = nt(got_ref[...], a_buf[k]).astype(BF16)
            put(k).start()

    for k in range(count):
        put(k).wait()


def dnorm_partial(rows, got, weight_a, weight_b):
    width, cols = weight_a.shape
    step = 512
    count = width // step
    return pl.pallas_call(
        dnorm_kernel,
        in_specs=[VMEM] * 2 + [HBM] * 2,
        out_specs=HBM,
        out_shape=pltpu.HBM((TOK, width), BF16),
        scratch_shapes=[pltpu.VMEM((count, step, cols), BF16)] * 2
        + [pltpu.VMEM((TOK, width), BF16)]
        + [pltpu.SemaphoreType.DMA((count,))] * 3,
        compiler_params=params(24),
        cost_estimate=cost(4 * TOK * width * cols, 4 * width * cols),
        name="dnorm",
    )(rows, got, in_hbm(weight_a), in_hbm(weight_b))


def rms_back_kernel(x_hbm, gain_ref, parts_ref, out_ref, x_ref, sem):
    rows = out_ref.shape[0]
    mine = pl.multiple_of(lax.axis_index("mp") * rows, rows)
    get_x = pltpu.make_async_copy(x_hbm.at[pl.ds(mine, rows), :], x_ref, sem)
    get_x.start()
    dnorm = parts_ref[0].astype(F32)
    for i in range(1, RING):
        dnorm += parts_ref[i].astype(F32)
    get_x.wait()
    xf = x_ref[...].astype(F32)
    scale = lax.rsqrt(jnp.mean(xf * xf, axis=-1, keepdims=True) + EPS)
    upper = gain_ref[...] * dnorm
    inner = jnp.mean(xf * upper, axis=-1, keepdims=True)
    out_ref[...] = (scale * upper - xf * (scale * scale * scale * inner)).astype(BF16)


def rms_back(x, gain, parts):
    rows, width = parts.shape[1:]
    return pl.pallas_call(
        rms_back_kernel,
        in_specs=[HBM] + [VMEM] * 2,
        out_specs=VMEM,
        out_shape=jax.ShapeDtypeStruct((rows, width), BF16),
        scratch_shapes=[pltpu.VMEM((rows, width), BF16), pltpu.SemaphoreType.DMA],
        compiler_params=params(),
        cost_estimate=cost(10 * rows * width, 12 * rows * width),
        name="rms_back",
    )(in_hbm(x), gain, parts)


def place_kernel(*refs):
    pieces, (out_hbm, sems) = refs[:RING], refs[RING:]
    rows = pieces[0].shape[0]
    copies = []
    for i, k in enumerate(ORDER):
        at = pl.multiple_of((lax.axis_index("mp") + k) % RING * rows, rows)
        copies.append(pltpu.make_async_copy(pieces[i], out_hbm.at[pl.ds(at, rows), :], sems.at[i]))
        copies[-1].start()
    for copy in copies:
        copy.wait()


def place(pieces):
    rows, width = pieces[0].shape
    return pl.pallas_call(
        place_kernel,
        in_specs=[ANY] * RING,
        out_specs=HBM,
        out_shape=pltpu.HBM((RING * rows, width), BF16),
        scratch_shapes=[pltpu.SemaphoreType.DMA((RING,))],
        compiler_params=params(),
        cost_estimate=cost(0, 4 * RING * rows * width),
        name="place",
    )(*pieces)


def shift(value, axis, k):
    return lax.ppermute(value, axis, [(i, (i + k) % RING) for i in range(RING)])


def gathered(block, axis):
    left, right = lax.optimization_barrier((shift(block, axis, 1), shift(block, axis, 3)))
    return [block, left, right, shift(left, axis, 1)]


def moved(value, k, along):
    pairs = []
    for core in range(2):
        for z in range(RING):
            for x in range(RING):
                to = {"z": z, "x": x}
                to[along[core]] = (to[along[core]] + k) % RING
                base = core * RING
                pairs.append(((base + z) * RING + x, (base + to["z"]) * RING + to["x"]))
    return lax.ppermute(value, ("section", "z", "x"), pairs)


GATHER, REDUCE = "xz", "zx"


def fetched(own, others):
    return [own] + [moved(others[k], k, GATHER) for k in (1, 3, 2)]


def left_loads(lefts, buf, sems, ks):
    block = buf.shape[-1]
    mine = lax.axis_index("mp")
    loads = [[[] for _ in ks] for _ in range(2)]
    for f in range(2):
        for i, k in enumerate(ks):
            for j, (left, distance) in enumerate(zip(lefts, ORDER, strict=True)):
                at = pl.multiple_of((mine + distance) % RING * QUARTER, QUARTER)
                loads[f][i].append(
                    pltpu.make_async_copy(
                        left.at[f, :, :, pl.ds(k * block, block)],
                        buf.at[f, i, :, pl.ds(at, QUARTER), :],
                        sems.at[f, i, j],
                    )
                )
                loads[f][i][-1].start()
    return loads


def left_scratch(block, count):
    return [
        pltpu.VMEM((2, count, RING, TOK, block), BF16),
        pltpu.SemaphoreType.DMA((2, count, RING)),
    ]


def flat(value):
    return value.reshape(RING * TOK, value.shape[-1])


def far_kernel(*refs):
    lefts, pieces = refs[:RING], refs[RING : 2 * RING]
    top_ref, low_ref, rows_ref, buf, sems = refs[2 * RING :]
    loads = left_loads(lefts, buf, sems, (2,))
    for i, piece in enumerate(pieces):
        rows_ref[i * TOK : (i + 1) * TOK, :] = piece[...]
    half, cols = top_ref.shape[0], top_ref.shape[1] // 2
    for m in range(2):
        at = slice(m * cols, (m + 1) * cols)
        wait_all(loads[m][0])
        block = tn(flat(buf[m, 0]), rows_ref[:, at]).astype(BF16)
        top_ref[:, at] = block[:half]
        low_ref[:, at] = block[half:]


def far_block(lefts, pieces):
    rows, cols = pieces[0].shape
    block = lefts[0].shape[-1] // RING
    half = jax.ShapeDtypeStruct((block // 2, cols), BF16)
    return pl.pallas_call(
        far_kernel,
        in_specs=[HBM] * RING + [VMEM] * RING,
        out_specs=[VMEM] * 3,
        out_shape=[half, half, jax.ShapeDtypeStruct((RING * rows, cols), BF16)],
        scratch_shapes=left_scratch(block, 1),
        compiler_params=params(),
        cost_estimate=cost(2 * RING * rows * block * cols, 8 * RING * rows * cols),
        name="far",
    )(*[in_hbm(left) for left in lefts], *pieces)


def side_kernel(*refs):
    lefts, (rows_ref, from_left, from_right, right, left, buf, sems) = refs[:RING], refs[RING:]
    loads = left_loads(lefts, buf, sems, (1, 3))
    half, cols = from_left.shape[0], right.shape[1] // 2
    for m in range(2):
        at = slice(m * cols, (m + 1) * cols)

        def product(i, m=m, at=at):
            wait_all(loads[m][i])
            return tn(flat(buf[m, i]), rows_ref[:, at])

        block = product(0)
        right[:half, at] = (block[:half] + from_left[:, at].astype(F32)).astype(BF16)
        right[half:, at] = block[half:].astype(BF16)
        block = product(1)
        left[:half, at] = block[:half].astype(BF16)
        left[half:, at] = (block[half:] + from_right[:, at].astype(F32)).astype(BF16)


def side_blocks(lefts, rows, from_left, from_right):
    depth, cols = rows.shape
    block = lefts[0].shape[-1] // RING
    shape = jax.ShapeDtypeStruct((block, cols), BF16)
    return pl.pallas_call(
        side_kernel,
        in_specs=[HBM] * RING + [VMEM] * 3,
        out_specs=[VMEM] * 2,
        out_shape=[shape] * 2,
        scratch_shapes=left_scratch(block, 2),
        compiler_params=params(),
        cost_estimate=cost(4 * depth * block * cols, 4 * depth * cols),
        name="side",
    )(*[in_hbm(left) for left in lefts], rows, from_left, from_right)


def middle_kernel(*refs):
    lefts, (rows_ref, own_hbm, other_hbm, out_buf, buf, sems, out_sems) = refs[:RING], refs[RING:]
    loads = left_loads(lefts, buf, sems, (0,))
    cols = out_buf.shape[2]
    puts = []
    for m, out in enumerate((own_hbm, other_hbm)):
        wait_all(loads[m][0])
        at = slice(m * cols, (m + 1) * cols)
        out_buf[m] = tn(flat(buf[m, 0]), rows_ref[:, at]).astype(BF16)
        puts.append(pltpu.make_async_copy(out_buf.at[m], out, out_sems.at[m]))
        puts[-1].start()
    wait_all(puts)


def middle_blocks(lefts, rows):
    depth, cols = rows.shape
    block = lefts[0].shape[-1] // RING
    return pl.pallas_call(
        middle_kernel,
        in_specs=[HBM] * RING + [VMEM],
        out_specs=[HBM] * 2,
        out_shape=[pltpu.HBM((block, cols // 2), BF16)] * 2,
        scratch_shapes=[pltpu.VMEM((2, block, cols // 2), BF16)]
        + left_scratch(block, 1)
        + [pltpu.SemaphoreType.DMA((2,))],
        compiler_params=params(),
        cost_estimate=cost(2 * depth * block * cols, 4 * depth * cols),
        name="middle",
    )(*[in_hbm(left) for left in lefts], rows)


def cross_kernel(own_hbm, a_ref, b_ref, out_ref, own_ref, sem):
    get = pltpu.make_async_copy(own_hbm, own_ref, sem)
    get.start()
    cols = out_ref.shape[1]
    both = a_ref[:, cols:].astype(F32) + b_ref[:, cols:].astype(F32)
    get.wait()
    out_ref[...] = (own_ref[...].astype(F32) + both).astype(BF16)


def cross_sum(own, a, b):
    block, cols = own.shape
    return pl.pallas_call(
        cross_kernel,
        in_specs=[HBM] + [VMEM] * 2,
        out_specs=VMEM,
        out_shape=jax.ShapeDtypeStruct((block, cols), BF16),
        scratch_shapes=[pltpu.VMEM((block, cols), BF16), pltpu.SemaphoreType.DMA],
        compiler_params=params(),
        cost_estimate=cost(2 * block * cols, 8 * block * cols),
        name="cross",
    )(in_hbm(own), a, b)


CHUNKS = 4


def write_out(values, first, second, buf, sems, is_first):
    size = buf.shape[0] // CHUNKS

    def put(c, out):
        at = slice(c * size, (c + 1) * size)
        return pltpu.make_async_copy(buf.at[at], out.at[at], sems.at[c])

    for c in range(CHUNKS):
        at = slice(c * size, (c + 1) * size)
        buf[at] = values(at)

        @pl.when(is_first)
        def _(c=c):
            put(c, first).start()

        @pl.when(jnp.logical_not(is_first))
        def _(c=c):
            put(c, second).start()

    for c in range(CHUNKS):
        put(c, first).wait()


def own_kernel(own_hbm, a_ref, b_ref, first, second, own_ref, buf, sem, sems):
    get = pltpu.make_async_copy(own_hbm, own_ref, sem)
    get.start()
    cols = own_ref.shape[1]
    get.wait()

    def values(at):
        both = a_ref[at, :cols].astype(F32) + b_ref[at, :cols].astype(F32)
        return own_ref[at].astype(F32) + both

    write_out(values, first, second, buf, sems, lax.axis_index("section") == 0)


def own_sum(own, a, b):
    block, cols = own.shape
    return pl.pallas_call(
        own_kernel,
        in_specs=[HBM] + [VMEM] * 2,
        out_specs=[HBM] * 2,
        out_shape=[pltpu.HBM((block, cols), F32)] * 2,
        scratch_shapes=[
            pltpu.VMEM((block, cols), BF16),
            pltpu.VMEM((block, cols), F32),
            pltpu.SemaphoreType.DMA,
            pltpu.SemaphoreType.DMA((CHUNKS,)),
        ],
        compiler_params=params(),
        cost_estimate=cost(2 * block * cols, 10 * block * cols),
        name="own",
    )(in_hbm(own), a, b)


def last_kernel(got_ref, first_in, second_in, first, second, buf, sems):
    def values(at):
        return got_ref[at].astype(F32)

    write_out(values, first, second, buf, sems, lax.axis_index("section") != 0)


def last_write(got, first, second):
    block, cols = got.shape
    return pl.pallas_call(
        last_kernel,
        in_specs=[VMEM] + [HBM] * 2,
        out_specs=[HBM] * 2,
        out_shape=[pltpu.HBM((block, cols), F32)] * 2,
        input_output_aliases={1: 0, 2: 1},
        scratch_shapes=[pltpu.VMEM((block, cols), F32), pltpu.SemaphoreType.DMA((CHUNKS,))],
        compiler_params=params(),
        cost_estimate=cost(block * cols, 6 * block * cols),
        name="last",
    )(got, in_hbm(first), in_hbm(second))


def per_device(states, gains, proj_a, proj_b, cotangent, src_len, tgt_len, dest):
    weight_a = proj_a[0]
    weight_b = proj_b[0]
    rows = states[0]
    keep, send, mine, other = forward(rows, gains, cotangent, weight_a, weight_b)
    swap = [(0, 1), (1, 0)]
    got = lax.ppermute(send, "section", swap)
    slots, slices = pack(keep, got, src_len, dest, mine, lax.ppermute(other, "section", swap))
    width = slots.shape[1]
    slots = slots.reshape(SEQ_DEV, MAXLEN, width)
    slots = lax.all_to_all(slots, ("z", "x"), split_axis=0, concat_axis=0, tiled=True)
    slots = slots.reshape(SLOTS, width)
    pieces = fetched(slices[0], {1: slices[1], 3: slices[2], 2: slices[3]})
    front, back, own = attend(keep, got, slots, src_len, tgt_len, dest, pieces)
    lefts = gathered(own, "mp")
    back = back.reshape(SEQ_DEV, MAXLEN, width)
    back = lax.all_to_all(back, ("z", "x"), split_axis=0, concat_axis=0, tiled=True)
    keep, send = unpack(back.reshape(SLOTS, width), front, src_len, dest)
    got = lax.ppermute(send, "section", swap)
    kind, others = join(keep, got)

    rights = fetched(kind, {k: kind for k in (1, 2, 3)})
    others = lax.ppermute(others, "section", swap)
    others, lefts[1], lefts[2] = lax.optimization_barrier((others, lefts[1], lefts[2]))
    partial = dnorm_partial(kind, others, weight_a, weight_b)
    partial, rights[1], rights[2] = lax.optimization_barrier((partial, rights[1], rights[2]))
    parts = lax.all_to_all(
        partial.reshape(RING, TOK // RING, -1), "mp", split_axis=0, concat_axis=0, tiled=True
    )
    top, low, stack = far_block(lefts, rights)
    from_left, from_right = moved(top, 1, REDUCE), moved(low, 3, REDUCE)
    own, own_other = middle_blocks(lefts, stack)
    stack, own, own_other = lax.optimization_barrier((stack, own, own_other))
    right, left = side_blocks(lefts, stack, from_left, from_right)
    left, parts = lax.optimization_barrier((left, parts))
    right, left = moved(right, 1, REDUCE), moved(left, 3, REDUCE)
    quarter = rms_back(rows, gains, parts)
    quarters = gathered(quarter, "mp")
    crossed = lax.ppermute(cross_sum(own_other, right, left), "section", swap)
    grad_a, grad_b = own_sum(own, right, left)
    quarters[3], grad_a = lax.optimization_barrier((quarters[3], grad_a))
    grad_states = place(quarters)
    grad_a, grad_b = last_write(crossed, grad_a, grad_b)
    return (grad_states[None], grad_a[None], grad_b[None])


def solution(mesh):
    split = jax.sharding.Mesh(mesh.devices.reshape(2, RING, RING, RING), ("section", "z", "x", "mp"))
    dp = ("z", "x")
    return jax.shard_map(
        per_device,
        mesh=split,
        in_specs=(
            P("section", dp, None),
            P("section", None),
            P("section", None, "mp"),
            P("section", None, "mp"),
            P(dp, None),
            P(),
            P(),
            P(),
        ),
        out_specs=(P("section", dp, None), P("section", dp, "mp"), P("section", dp, "mp")),
        check_vma=False,
    )
```

```python
import jax
import jax.numpy as jnp
from jax import lax
from jax.experimental import pallas as pl
from jax.experimental.pallas import tpu as pltpu
from jax.sharding import PartitionSpec as P

HEAD_DIM = 64
SEQ_DEV = 16
MAXLEN = 16
TOK = 128
SLOTS = 256
RING = 4
QUARTER = TOK // RING
ORDER = (0, 3, 1, 2)
EPS = 1e-06
SHARE = 16
F32 = jnp.float32
BF16 = jnp.bfloat16
VMEM = pl.BlockSpec(memory_space=pltpu.VMEM)
ANY = pl.BlockSpec(memory_space=pl.ANY)
HBM = pl.BlockSpec(memory_space=pltpu.HBM)


def iota(shape, dim):
    return lax.broadcasted_iota(jnp.int32, shape, dim)


def total(value, axis):
    return jnp.sum(value.astype(F32), axis=axis, keepdims=True)


def tn(left, right):
    return lax.dot_general(left, right, (((0,), (0,)), ((), ())), preferred_element_type=F32)


def in_hbm(value):
    return pltpu.with_memory_space_constraint(value, pltpu.HBM)


def cost(flops, nbytes):
    return pl.CostEstimate(flops=flops // SHARE, bytes_accessed=nbytes // SHARE, transcendentals=0)


def params(mib=12, **more):
    return pltpu.CompilerParams(vmem_limit_bytes=mib << 20, **more)


def column_of(row):
    square = jnp.broadcast_to(row, (SEQ_DEV, SEQ_DEV))
    same = iota((SEQ_DEV, SEQ_DEV), 0) == iota((SEQ_DEV, SEQ_DEV), 1)
    return total(jnp.where(same, square, 0), 1)


def member_index():
    return lax.axis_index("z") * RING + lax.axis_index("x")


def slot_onehot(member, src_len, dest):
    i, j = iota((SEQ_DEV, SEQ_DEV), 0), iota((SEQ_DEV, SEQ_DEV), 1)
    lengths = src_len[pl.ds(member, 1), :]
    ends = total(jnp.where(j <= i, jnp.broadcast_to(lengths, (SEQ_DEV, SEQ_DEV)), 0), 1)
    begins = ends - column_of(lengths)
    place = column_of(dest[pl.ds(member, 1), :] >> 4) * MAXLEN
    row = iota((SEQ_DEV, TOK), 1).astype(F32)
    inside = (row >= begins) & (row < ends)
    target = total(jnp.where(inside, place + row - begins, 0.0), 0)
    hit = iota((SLOTS, TOK), 0).astype(F32) == target
    return jnp.where(hit, 1.0, 0.0).astype(BF16)


def pair_mask(member, src_len, tgt_len, dest):
    i, j = iota((SEQ_DEV, SEQ_DEV), 0), iota((SEQ_DEV, SEQ_DEV), 1)
    column = column_of(tgt_len[pl.ds(member, 1), :])
    ends = total(jnp.where(i <= j, jnp.broadcast_to(column, (SEQ_DEV, SEQ_DEV)), 0.0), 0)
    row = iota((TOK, SEQ_DEV), 0).astype(F32)
    mine = total(jnp.where(row >= ends, 1.0, 0.0), 1)
    codes = dest[...]
    to_me = (codes >> 4) == member
    target = total(jnp.where(to_me, codes & 15, 0), 1)
    length = total(jnp.where(to_me, src_len[...], 0), 1)
    lane = iota((SEQ_DEV, SLOTS), 1)
    own = (lane >> 4) == iota((SEQ_DEV, SLOTS), 0)
    target = total(jnp.where(own, target, 0.0), 0)
    length = total(jnp.where(own, length, 0.0), 0)
    step = (iota((1, SLOTS), 1) & 15).astype(F32)
    target = jnp.where(step < length, target, -1.0)
    return mine == target


def forward_kernel(
    x_hbm, gain_hbm, cot_hbm, a_hbm, b_hbm, keep_ref, send_ref, *rest
):
    mine_ref, other_ref = rest[:2]
    x_ref, gain_ref, a_buf, b_buf, normed_ref, left_ref, in_sem, a_sem, b_sem, out_sem = rest[2:]
    count, step, cols = a_buf.shape
    core = lax.axis_index("section")
    get_x = pltpu.make_async_copy(x_hbm, x_ref, in_sem.at[0])
    get_gain = pltpu.make_async_copy(gain_hbm, gain_ref, in_sem.at[1])
    get_left = pltpu.make_async_copy(cot_hbm, left_ref, in_sem.at[2])
    get_x.start()
    get_gain.start()

    @pl.when(core != 0)
    def _():
        get_left.start()

    def fetch(k):
        rows = pl.ds(k * step, step)
        return (
            pltpu.make_async_copy(a_hbm.at[rows, :], a_buf.at[k], a_sem.at[k]),
            pltpu.make_async_copy(b_hbm.at[rows, :], b_buf.at[k], b_sem.at[k]),
        )

    for k in range(count):
        for copy in fetch(k):
            copy.start()
    get_x.wait()
    get_gain.wait()
    xf = x_ref[...].astype(F32)
    scale = lax.rsqrt(jnp.mean(xf * xf, axis=-1, keepdims=True) + EPS)
    normed_ref[...] = (xf * scale * gain_ref[...]).astype(BF16)

    @pl.when(core == 0)
    def _():
        left_ref[...] = normed_ref[...]

    @pl.when(core != 0)
    def _():
        get_left.wait()

    z, x = lax.axis_index("z"), lax.axis_index("x")
    quarter = pl.ds(pl.multiple_of(lax.axis_index("mp") * QUARTER, QUARTER), QUARTER)
    block = cols // RING
    copies = []
    for k in range(RING):
        for j in range(RING):
            to = slice(j * block, (j + 1) * block)
            at_x = ((z + j) % RING * RING + (x + k) % RING) * block
            at_z = ((z + k) % RING * RING + (x + j) % RING) * block
            at_mine = jnp.where(core == 0, at_x, at_z)
            at_other = jnp.where(core == 0, at_z, at_x)
            for source, at, out in ((left_ref, at_mine, mine_ref), (normed_ref, at_other, other_ref)):
                copies.append(
                    pltpu.make_async_copy(
                        source.at[quarter, pl.ds(pl.multiple_of(at, block), block)],
                        out.at[k, :, to],
                        out_sem.at[len(copies)],
                    )
                )
                copies[-1].start()

    acc_a = acc_b = None
    for k in range(count):
        for copy in fetch(k):
            copy.wait()
        at = slice(k * step, (k + 1) * step)
        part_a = jnp.dot(normed_ref[:, at], a_buf[k], preferred_element_type=F32)
        part_b = jnp.dot(left_ref[:, at], b_buf[k], preferred_element_type=F32)
        acc_a = part_a if acc_a is None else acc_a + part_a
        acc_b = part_b if acc_b is None else acc_b + part_b
    half = cols // 2
    parts = [[acc[:, i * half : (i + 1) * half].astype(BF16) for acc in (acc_a, acc_b)] for i in range(2)]

    def put(ref, pieces):
        ref[:, :half] = pieces[0]
        ref[:, half:] = pieces[1]

    @pl.when(core == 0)
    def _():
        put(keep_ref, parts[0])
        put(send_ref, parts[1])

    @pl.when(core != 0)
    def _():
        put(keep_ref, parts[1])
        put(send_ref, parts[0])

    for copy in copies:
        copy.wait()


def forward(x, gain, cot, weight_a, weight_b):
    rows, width = x.shape
    cols = weight_a.shape[1]
    step = 512
    count = width // step
    half = jax.ShapeDtypeStruct((rows, cols), BF16)
    return pl.pallas_call(
        forward_kernel,
        in_specs=[HBM] * 5,
        out_specs=[VMEM] * 4,
        out_shape=[half] * 2 + [jax.ShapeDtypeStruct((RING, QUARTER, cols), BF16)] * 2,
        scratch_shapes=[pltpu.VMEM((rows, width), BF16), pltpu.VMEM((1, width), F32)]
        + [pltpu.VMEM((count, step, cols), BF16)] * 2
        + [pltpu.VMEM((rows, width), BF16)] * 2
        + [pltpu.SemaphoreType.DMA((3,))]
        + [pltpu.SemaphoreType.DMA((count,))] * 2
        + [pltpu.SemaphoreType.DMA((2 * RING * RING,))],
        compiler_params=params(32),
        cost_estimate=cost(4 * rows * width * cols, 4 * width * cols),
        name="forward",
    )(in_hbm(x), in_hbm(gain), in_hbm(cot), in_hbm(weight_a), in_hbm(weight_b))


def wait_all(copies):
    for copy in copies:
        copy.wait()


def pack_kernel(keep_ref, got_ref, src_ref, dest_ref, mine_ref, other_ref, out_ref, *rest):
    for out, k in zip(rest, (0, 1, 3, 2), strict=True):
        out[0] = mine_ref[k]
        out[1] = other_ref[k]
    spread = slot_onehot(member_index(), src_ref, dest_ref)

    @pl.when(lax.axis_index("section") == 0)
    def _():
        out_ref[...] = jnp.dot(spread, keep_ref[...], preferred_element_type=F32).astype(BF16)

    @pl.when(lax.axis_index("section") != 0)
    def _():
        out_ref[...] = jnp.dot(spread, got_ref[...], preferred_element_type=F32).astype(BF16)


def pack(keep, got, src_len, dest, mine, other):
    width = keep.shape[1]
    _, rows, cols = mine.shape
    outs = pl.pallas_call(
        pack_kernel,
        in_specs=[VMEM] * 6,
        out_specs=[VMEM] * (1 + RING),
        out_shape=[jax.ShapeDtypeStruct((SLOTS, width), BF16)]
        + [jax.ShapeDtypeStruct((2, rows, cols), BF16)] * RING,
        compiler_params=params(),
        cost_estimate=cost(2 * SLOTS * TOK * width, 2 * SLOTS * width),
        name="pack",
    )(keep, got, src_len, dest, mine, other)
    return outs[0], outs[1:]


def attend_kernel(
    keep_ref, got_ref, slots_ref, src_ref, tgt_ref, dest_ref, *rest
):
    front_ref, back_ref, stack_ref, own_ref = rest[RING:]
    for p in range(RING):
        for m in range(2):
            stack_ref[m, p] = rest[p][m]
    mask = pair_mask(member_index(), src_ref, tgt_ref, dest_ref)

    @pl.when(lax.axis_index("section") == 0)
    def _():
        own_ref[...] = got_ref[...]

    @pl.when(lax.axis_index("section") != 0)
    def _():
        own_ref[...] = keep_ref[...]

    half = own_ref.shape[1] // 2
    pair = 2 * HEAD_DIM
    low = iota((1, pair), 1) < HEAD_DIM
    nothing = jnp.zeros((), BF16)

    def both(value):
        return jnp.concatenate(
            [jnp.where(low, value, nothing), jnp.where(low, nothing, value)], axis=0
        )

    def nt(left, right):
        return lax.dot_general(left, right, (((1,), (1,)), ((), ())), preferred_element_type=F32)

    def one(score, dweight):
        expo = jnp.where(mask, jnp.exp(score), 0.0)
        weight = expo * (1.0 / jnp.sum(expo, axis=-1, keepdims=True))
        mean = jnp.sum(weight * dweight, axis=-1, keepdims=True)
        return weight.astype(BF16), (weight * (dweight - mean)).astype(BF16)

    def fold(value):
        return jnp.where(low, value[:SLOTS], value[SLOTS:]).astype(BF16)

    for p in range(half // pair):
        first = slice(p * pair, (p + 1) * pair)
        second = slice(half + p * pair, half + (p + 1) * pair)
        query, dout = own_ref[:, first], own_ref[:, second]
        keys, values = both(slots_ref[:, first]), both(slots_ref[:, second])
        score, dweight = nt(query, keys), nt(dout, values)
        weight_0, dscore_0 = one(score[:, :SLOTS], dweight[:, :SLOTS])
        weight_1, dscore_1 = one(score[:, SLOTS:], dweight[:, SLOTS:])
        weight = jnp.concatenate([weight_0, weight_1], axis=1)
        dscore = jnp.concatenate([dscore_0, dscore_1], axis=1)
        front_ref[:, first] = jnp.dot(dscore, keys, preferred_element_type=F32).astype(BF16)
        front_ref[:, second] = jnp.dot(weight, values, preferred_element_type=F32).astype(BF16)
        back_ref[:, first] = fold(tn(dscore, query))
        back_ref[:, second] = fold(tn(weight, dout))


def attend(keep, got, slots, src_len, tgt_len, dest, pieces):
    rows, width = keep.shape
    _, quarter, cols = pieces[0].shape
    return pl.pallas_call(
        attend_kernel,
        in_specs=[VMEM] * (6 + RING),
        out_specs=[VMEM] * 3,
        out_shape=[
            jax.ShapeDtypeStruct((rows, width), BF16),
            jax.ShapeDtypeStruct((SLOTS, width), BF16),
            jax.ShapeDtypeStruct((2, RING, quarter, cols), BF16),
        ],
        scratch_shapes=[pltpu.VMEM((rows, width), BF16)],
        compiler_params=params(),
        cost_estimate=cost(24 * rows * SLOTS * width, 8 * SLOTS * width),
        name="attend",
    )(keep, got, slots, src_len, tgt_len, dest, *pieces)


def unpack_kernel(back_ref, front_ref, src_ref, dest_ref, keep_ref, send_ref):
    spread = slot_onehot(member_index(), src_ref, dest_ref)
    rows = tn(spread, back_ref[...]).astype(BF16)
    half = rows.shape[1] // 2
    core = lax.axis_index("section")

    @pl.when(core == 0)
    def _():
        keep_ref[:, :half] = rows[:, :half]
        keep_ref[:, half:] = front_ref[:, :half]
        send_ref[:, :half] = front_ref[:, half:]
        send_ref[:, half:] = rows[:, half:]

    @pl.when(core != 0)
    def _():
        keep_ref[:, :half] = front_ref[:, half:]
        keep_ref[:, half:] = rows[:, half:]
        send_ref[:, :half] = rows[:, :half]
        send_ref[:, half:] = front_ref[:, :half]


def unpack(back, front, src_len, dest):
    width = front.shape[1]
    half = jax.ShapeDtypeStruct((TOK, width), BF16)
    return pl.pallas_call(
        unpack_kernel,
        in_specs=[VMEM] * 4,
        out_specs=[VMEM] * 2,
        out_shape=[half, half],
        compiler_params=params(),
        cost_estimate=cost(2 * SLOTS * TOK * width, 4 * SLOTS * width),
        name="unpack",
    )(back, front, src_len, dest)


def join_kernel(keep_ref, got_ref, rows_ref, other_ref):
    width = keep_ref.shape[1]
    half = width // 2
    core = lax.axis_index("section")
    mine = pl.multiple_of(core * half, half)
    theirs = pl.multiple_of((1 - core) * half, half)
    for ref, at in ((keep_ref, mine), (got_ref, theirs)):
        rows_ref[:, pl.ds(at, half)] = ref[:, :half]
        rows_ref[:, pl.ds(pl.multiple_of(width + at, half), half)] = ref[:, half:]
        other_ref[:, pl.ds(at, half)] = ref[:, half:]


def join(keep, got):
    rows, width = keep.shape
    return pl.pallas_call(
        join_kernel,
        in_specs=[VMEM, VMEM],
        out_specs=[VMEM] * 2,
        out_shape=[
            jax.ShapeDtypeStruct((rows, 2 * width), BF16),
            jax.ShapeDtypeStruct((rows, width), BF16),
        ],
        compiler_params=params(),
        cost_estimate=cost(0, 8 * keep.size),
        name="join",
    )(keep, got)


def dnorm_kernel(rows_ref, got_ref, a_hbm, b_hbm, out_hbm, a_buf, b_buf, out_buf, a_sem, b_sem, out_sem):
    count, step, cols = a_buf.shape
    core = lax.axis_index("section")

    def nt(left, right):
        return lax.dot_general(left, right, (((1,), (1,)), ((), ())), preferred_element_type=F32)

    def fetches(hbm, buf, sem):
        return [
            pltpu.make_async_copy(hbm.at[pl.ds(k * step, step), :], buf.at[k], sem.at[k])
            for k in range(count)
        ]

    get_a, get_b = fetches(a_hbm, a_buf, a_sem), fetches(b_hbm, b_buf, b_sem)

    def put(k):
        at = slice(k * step, (k + 1) * step)
        return pltpu.make_async_copy(out_buf.at[:, at], out_hbm.at[:, at], out_sem.at[k])

    @pl.when(core == 0)
    def _():
        for k in range(count):
            get_a[k].start()
            get_b[k].start()
        for k in range(count):
            get_a[k].wait()
            get_b[k].wait()
            block = nt(rows_ref[:, :cols], a_buf[k]) + nt(got_ref[...], b_buf[k])
            out_buf[:, k * step : (k + 1) * step] = block.astype(BF16)
            put(k).start()

    @pl.when(core != 0)
    def _():
        for k in range(count):
            get_a[k].start()
        for k in range(count):
            get_a[k].wait()
            out_buf[:, k * step : (k + 1) * step] = nt(got_ref[...], a_buf[k]).astype(BF16)
            put(k).start()

    for k in range(count):
        put(k).wait()


def dnorm_partial(rows, got, weight_a, weight_b):
    width, cols = weight_a.shape
    step = 512
    count = width // step
    return pl.pallas_call(
        dnorm_kernel,
        in_specs=[VMEM] * 2 + [HBM] * 2,
        out_specs=HBM,
        out_shape=pltpu.HBM((TOK, width), BF16),
        scratch_shapes=[pltpu.VMEM((count, step, cols), BF16)] * 2
        + [pltpu.VMEM((TOK, width), BF16)]
        + [pltpu.SemaphoreType.DMA((count,))] * 3,
        compiler_params=params(24),
        cost_estimate=cost(4 * TOK * width * cols, 4 * width * cols),
        name="dnorm",
    )(rows, got, in_hbm(weight_a), in_hbm(weight_b))


def rms_back_kernel(x_hbm, gain_ref, parts_ref, out_ref, x_ref, sem):
    rows = out_ref.shape[0]
    mine = pl.multiple_of(lax.axis_index("mp") * rows, rows)
    get_x = pltpu.make_async_copy(x_hbm.at[pl.ds(mine, rows), :], x_ref, sem)
    get_x.start()
    dnorm = parts_ref[0].astype(F32)
    for i in range(1, RING):
        dnorm += parts_ref[i].astype(F32)
    get_x.wait()
    xf = x_ref[...].astype(F32)
    scale = lax.rsqrt(jnp.mean(xf * xf, axis=-1, keepdims=True) + EPS)
    upper = gain_ref[...] * dnorm
    inner = jnp.mean(xf * upper, axis=-1, keepdims=True)
    out_ref[...] = (scale * upper - xf * (scale * scale * scale * inner)).astype(BF16)


def rms_back(x, gain, parts):
    rows, width = parts.shape[1:]
    return pl.pallas_call(
        rms_back_kernel,
        in_specs=[HBM] + [VMEM] * 2,
        out_specs=VMEM,
        out_shape=jax.ShapeDtypeStruct((rows, width), BF16),
        scratch_shapes=[pltpu.VMEM((rows, width), BF16), pltpu.SemaphoreType.DMA],
        compiler_params=params(),
        cost_estimate=cost(10 * rows * width, 12 * rows * width),
        name="rms_back",
    )(in_hbm(x), gain, parts)


def place_kernel(*refs):
    pieces, (out_hbm, sems) = refs[:RING], refs[RING:]
    rows = pieces[0].shape[0]
    copies = []
    for i, k in enumerate(ORDER):
        at = pl.multiple_of((lax.axis_index("mp") + k) % RING * rows, rows)
        copies.append(pltpu.make_async_copy(pieces[i], out_hbm.at[pl.ds(at, rows), :], sems.at[i]))
        copies[-1].start()
    for copy in copies:
        copy.wait()


def place(pieces):
    rows, width = pieces[0].shape
    return pl.pallas_call(
        place_kernel,
        in_specs=[ANY] * RING,
        out_specs=HBM,
        out_shape=pltpu.HBM((RING * rows, width), BF16),
        scratch_shapes=[pltpu.SemaphoreType.DMA((RING,))],
        compiler_params=params(),
        cost_estimate=cost(0, 4 * RING * rows * width),
        name="place",
    )(*pieces)


def shift(value, axis, k):
    return lax.ppermute(value, axis, [(i, (i + k) % RING) for i in range(RING)])


def gathered(block, axis):
    left, right = lax.optimization_barrier((shift(block, axis, 1), shift(block, axis, 3)))
    return [block, left, right, shift(left, axis, 1)]


def moved(value, k, along, across=False):
    pairs = []
    for core in range(2):
        for z in range(RING):
            for x in range(RING):
                to = {"z": z, "x": x}
                to[along[core]] = (to[along[core]] + k) % RING
                target = (1 - core if across else core, to["z"], to["x"])
                pairs.append(
                    ((core * RING + z) * RING + x, (target[0] * RING + target[1]) * RING + target[2])
                )
    return lax.ppermute(value, ("section", "z", "x"), pairs)


GATHER, REDUCE = "xz", "zx"


def fetched(own, others):
    return [own] + [moved(others[k], k, GATHER) for k in (1, 3, 2)]


def left_loads(lefts, buf, sems, ks):
    block = buf.shape[-1]
    mine = lax.axis_index("mp")
    loads = [[[] for _ in ks] for _ in range(2)]
    for f in range(2):
        for i, k in enumerate(ks):
            for j, (left, distance) in enumerate(zip(lefts, ORDER, strict=True)):
                at = pl.multiple_of((mine + distance) % RING * QUARTER, QUARTER)
                loads[f][i].append(
                    pltpu.make_async_copy(
                        left.at[f, :, :, pl.ds(k * block, block)],
                        buf.at[f, i, :, pl.ds(at, QUARTER), :],
                        sems.at[f, i, j],
                    )
                )
                loads[f][i][-1].start()
    return loads


def left_scratch(block, count):
    return [
        pltpu.VMEM((2, count, RING, TOK, block), BF16),
        pltpu.SemaphoreType.DMA((2, count, RING)),
    ]


def flat(value):
    return value.reshape(RING * TOK, value.shape[-1])


def far_kernel(*refs):
    lefts, pieces = refs[:RING], refs[RING : 2 * RING]
    top_ref, low_ref, rows_ref, other_ref, buf, sems = refs[2 * RING :]
    loads = left_loads(lefts, buf, sems, (2, 0))
    for i, piece in enumerate(pieces):
        rows_ref[i * TOK : (i + 1) * TOK, :] = piece[...]
    half, cols = top_ref.shape[0], top_ref.shape[1] // 2
    for m in range(2):
        at = slice(m * cols, (m + 1) * cols)
        wait_all(loads[m][0])
        block = tn(flat(buf[m, 0]), rows_ref[:, at]).astype(BF16)
        top_ref[:, at] = block[:half]
        low_ref[:, at] = block[half:]
    wait_all(loads[0][1])
    wait_all(loads[1][1])
    other_ref[...] = tn(flat(buf[1, 1]), rows_ref[:, cols:]).astype(BF16)


def far_block(lefts, pieces):
    rows, cols = pieces[0].shape
    block = lefts[0].shape[-1] // RING
    half = jax.ShapeDtypeStruct((block // 2, cols), BF16)
    return pl.pallas_call(
        far_kernel,
        in_specs=[HBM] * RING + [VMEM] * RING,
        out_specs=[VMEM] * 4,
        out_shape=[
            half,
            half,
            jax.ShapeDtypeStruct((RING * rows, cols), BF16),
            jax.ShapeDtypeStruct((block, cols // 2), BF16),
        ],
        scratch_shapes=left_scratch(block, 2),
        compiler_params=params(),
        cost_estimate=cost(3 * RING * rows * block * cols, 8 * RING * rows * cols),
        name="far",
    )(*[in_hbm(left) for left in lefts], *pieces)


def side_kernel(*refs):
    lefts, (rows_ref, from_left, from_right) = refs[:RING], refs[RING : RING + 3]
    rights, to_lefts, buf, sems = refs[RING + 3 : RING + 5], refs[RING + 5 : RING + 7], *refs[RING + 7 :]
    loads = left_loads(lefts, buf, sems, (1, 3))
    half, cols = from_left.shape[0], rights[0].shape[1]
    for m in range(2):
        at = slice(m * cols, (m + 1) * cols)

        def product(i, m=m, at=at):
            wait_all(loads[m][i])
            return tn(flat(buf[m, i]), rows_ref[:, at])

        block = product(0)
        rights[m][:half, :] = (block[:half] + from_left[:, at].astype(F32)).astype(BF16)
        rights[m][half:, :] = block[half:].astype(BF16)
        block = product(1)
        to_lefts[m][:half, :] = block[:half].astype(BF16)
        to_lefts[m][half:, :] = (block[half:] + from_right[:, at].astype(F32)).astype(BF16)


def side_blocks(lefts, rows, from_left, from_right):
    depth, cols = rows.shape
    block = lefts[0].shape[-1] // RING
    shape = jax.ShapeDtypeStruct((block, cols // 2), BF16)
    return pl.pallas_call(
        side_kernel,
        in_specs=[HBM] * RING + [VMEM] * 3,
        out_specs=[VMEM] * 4,
        out_shape=[shape] * 4,
        scratch_shapes=left_scratch(block, 2),
        compiler_params=params(),
        cost_estimate=cost(4 * depth * block * cols, 4 * depth * cols),
        name="side",
    )(*[in_hbm(left) for left in lefts], rows, from_left, from_right)


def middle_kernel(*refs):
    lefts, (rows_ref, own_hbm, out_buf, buf, sems, out_sem) = refs[:RING], refs[RING:]
    loads = left_loads(lefts, buf, sems, (0,))
    wait_all(loads[0][0])
    wait_all(loads[1][0])
    out_buf[...] = tn(flat(buf[0, 0]), rows_ref[:, : out_buf.shape[1]]).astype(BF16)
    put = pltpu.make_async_copy(out_buf, own_hbm, out_sem)
    put.start()
    put.wait()


def middle_block(lefts, rows):
    depth, cols = rows.shape
    block = lefts[0].shape[-1] // RING
    return pl.pallas_call(
        middle_kernel,
        in_specs=[HBM] * RING + [VMEM],
        out_specs=HBM,
        out_shape=pltpu.HBM((block, cols // 2), BF16),
        scratch_shapes=[pltpu.VMEM((block, cols // 2), BF16)]
        + left_scratch(block, 1)
        + [pltpu.SemaphoreType.DMA],
        compiler_params=params(),
        cost_estimate=cost(depth * block * cols, 4 * depth * cols),
        name="middle",
    )(*[in_hbm(left) for left in lefts], rows)


def own_kernel(own_hbm, other_hbm, *refs):
    parts, outs, (base_ref, out_buf, base_sems, out_sems) = refs[:4], refs[4:6], refs[6:]
    gets = [
        pltpu.make_async_copy(base, base_ref.at[m], base_sems.at[m])
        for m, base in enumerate((own_hbm, other_hbm))
    ]
    for get in gets:
        get.start()
    core = lax.axis_index("section")
    chunks = out_sems.shape[1]
    size = out_buf.shape[1] // chunks

    def put(m, c, out):
        at = slice(c * size, (c + 1) * size)
        return pltpu.make_async_copy(out_buf.at[m, at], out.at[at], out_sems.at[m, c])

    def write(m, c):
        @pl.when(core == m)
        def _():
            put(m, c, outs[0]).start()

        @pl.when(core != m)
        def _():
            put(m, c, outs[1]).start()

    for m in range(2):
        gets[m].wait()
        for c in range(chunks):
            at = slice(c * size, (c + 1) * size)
            total_of = base_ref[m, at].astype(F32) + parts[2 * m][at].astype(F32)
            out_buf[m, at] = total_of + parts[2 * m + 1][at].astype(F32)
            write(m, c)
    for m in range(2):
        for c in range(chunks):
            put(m, c, outs[0]).wait()


def own_blocks(own, other, parts):
    block, cols = own.shape
    return pl.pallas_call(
        own_kernel,
        in_specs=[HBM] * 2 + [VMEM] * 4,
        out_specs=[HBM] * 2,
        out_shape=[pltpu.HBM((block, cols), F32)] * 2,
        scratch_shapes=[
            pltpu.VMEM((2, block, cols), BF16),
            pltpu.VMEM((2, block, cols), F32),
            pltpu.SemaphoreType.DMA((2,)),
            pltpu.SemaphoreType.DMA((2, 4)),
        ],
        compiler_params=params(),
        cost_estimate=cost(4 * block * cols, 20 * block * cols),
        name="own",
    )(in_hbm(own), in_hbm(other), *parts)


def per_device(states, gains, proj_a, proj_b, cotangent, src_len, tgt_len, dest):
    weight_a = proj_a[0]
    weight_b = proj_b[0]
    rows = states[0]
    keep, send, mine, other = forward(rows, gains, cotangent, weight_a, weight_b)
    swap = [(0, 1), (1, 0)]
    got = lax.ppermute(send, "section", swap)
    slots, slices = pack(keep, got, src_len, dest, mine, lax.ppermute(other, "section", swap))
    width = slots.shape[1]
    slots = slots.reshape(SEQ_DEV, MAXLEN, width)
    slots = lax.all_to_all(slots, ("z", "x"), split_axis=0, concat_axis=0, tiled=True)
    slots = slots.reshape(SLOTS, width)
    pieces = fetched(slices[0], {1: slices[1], 3: slices[2], 2: slices[3]})
    front, back, own = attend(keep, got, slots, src_len, tgt_len, dest, pieces)
    lefts = gathered(own, "mp")
    back = back.reshape(SEQ_DEV, MAXLEN, width)
    back = lax.all_to_all(back, ("z", "x"), split_axis=0, concat_axis=0, tiled=True)
    keep, send = unpack(back.reshape(SLOTS, width), front, src_len, dest)
    got = lax.ppermute(send, "section", swap)
    kind, others = join(keep, got)

    rights = fetched(kind, {k: kind for k in (1, 2, 3)})
    others = lax.ppermute(others, "section", swap)
    others, lefts[1], lefts[2] = lax.optimization_barrier((others, lefts[1], lefts[2]))
    partial = dnorm_partial(kind, others, weight_a, weight_b)
    partial, rights[1], rights[2] = lax.optimization_barrier((partial, rights[1], rights[2]))
    parts = lax.all_to_all(
        partial.reshape(RING, TOK // RING, -1), "mp", split_axis=0, concat_axis=0, tiled=True
    )
    top, low, stack, own_other = far_block(lefts, rights)
    from_left, from_right = moved(top, 1, REDUCE), moved(low, 3, REDUCE)
    own = middle_block(lefts, stack)
    crossed = lax.ppermute(own_other, "section", swap)
    stack, own, crossed = lax.optimization_barrier((stack, own, crossed))
    right, right_other, left, left_other = side_blocks(lefts, stack, from_left, from_right)
    left_other, parts = lax.optimization_barrier((left_other, parts))
    sums = [
        moved(right, 1, REDUCE),
        moved(left, 3, REDUCE),
        moved(right_other, 1, REDUCE, True),
        moved(left_other, 3, REDUCE, True),
    ]
    quarter = rms_back(rows, gains, parts)
    grad_states = place(gathered(quarter, "mp"))
    grad_a, grad_b = own_blocks(own, crossed, sums)
    return (grad_states[None], grad_a[None], grad_b[None])


def solution(mesh):
    split = jax.sharding.Mesh(mesh.devices.reshape(2, RING, RING, RING), ("section", "z", "x", "mp"))
    dp = ("z", "x")
    return jax.shard_map(
        per_device,
        mesh=split,
        in_specs=(
            P("section", dp, None),
            P("section", None),
            P("section", None, "mp"),
            P("section", None, "mp"),
            P(dp, None),
            P(),
            P(),
            P(),
        ),
        out_specs=(P("section", dp, None), P("section", dp, "mp"), P("section", dp, "mp")),
        check_vma=False,
    )
```

```python
import jax
import jax.numpy as jnp
from jax import lax
from jax.experimental import pallas as pl
from jax.experimental.pallas import tpu as pltpu
from jax.sharding import PartitionSpec as P

HEAD_DIM = 64
SEQ_DEV = 16
MAXLEN = 16
TOK = 128
SLOTS = 256
RING = 4
QUARTER = TOK // RING
ORDER = (0, 3, 1, 2)
EPS = 1e-06
SHARE = 16
F32 = jnp.float32
BF16 = jnp.bfloat16
VMEM = pl.BlockSpec(memory_space=pltpu.VMEM)
ANY = pl.BlockSpec(memory_space=pl.ANY)
HBM = pl.BlockSpec(memory_space=pltpu.HBM)


def iota(shape, dim):
    return lax.broadcasted_iota(jnp.int32, shape, dim)


def total(value, axis):
    return jnp.sum(value.astype(F32), axis=axis, keepdims=True)


def tn(left, right):
    return lax.dot_general(left, right, (((0,), (0,)), ((), ())), preferred_element_type=F32)


def in_hbm(value):
    return pltpu.with_memory_space_constraint(value, pltpu.HBM)


def cost(flops, nbytes):
    return pl.CostEstimate(flops=flops // SHARE, bytes_accessed=nbytes // SHARE, transcendentals=0)


def params(mib=12, **more):
    return pltpu.CompilerParams(vmem_limit_bytes=mib << 20, **more)


def column_of(row):
    square = jnp.broadcast_to(row, (SEQ_DEV, SEQ_DEV))
    same = iota((SEQ_DEV, SEQ_DEV), 0) == iota((SEQ_DEV, SEQ_DEV), 1)
    return total(jnp.where(same, square, 0), 1)


def member_index():
    return lax.axis_index("z") * RING + lax.axis_index("x")


def slot_onehot(member, src_len, dest):
    i, j = iota((SEQ_DEV, SEQ_DEV), 0), iota((SEQ_DEV, SEQ_DEV), 1)
    lengths = src_len[pl.ds(member, 1), :]
    ends = total(jnp.where(j <= i, jnp.broadcast_to(lengths, (SEQ_DEV, SEQ_DEV)), 0), 1)
    begins = ends - column_of(lengths)
    place = column_of(dest[pl.ds(member, 1), :] >> 4) * MAXLEN
    row = iota((SEQ_DEV, TOK), 1).astype(F32)
    inside = (row >= begins) & (row < ends)
    target = total(jnp.where(inside, place + row - begins, 0.0), 0)
    hit = iota((SLOTS, TOK), 0).astype(F32) == target
    return jnp.where(hit, 1.0, 0.0).astype(BF16)


def pair_mask(member, src_len, tgt_len, dest):
    i, j = iota((SEQ_DEV, SEQ_DEV), 0), iota((SEQ_DEV, SEQ_DEV), 1)
    column = column_of(tgt_len[pl.ds(member, 1), :])
    ends = total(jnp.where(i <= j, jnp.broadcast_to(column, (SEQ_DEV, SEQ_DEV)), 0.0), 0)
    row = iota((TOK, SEQ_DEV), 0).astype(F32)
    mine = total(jnp.where(row >= ends, 1.0, 0.0), 1)
    codes = dest[...]
    to_me = (codes >> 4) == member
    target = total(jnp.where(to_me, codes & 15, 0), 1)
    length = total(jnp.where(to_me, src_len[...], 0), 1)
    lane = iota((SEQ_DEV, SLOTS), 1)
    own = (lane >> 4) == iota((SEQ_DEV, SLOTS), 0)
    target = total(jnp.where(own, target, 0.0), 0)
    length = total(jnp.where(own, length, 0.0), 0)
    step = (iota((1, SLOTS), 1) & 15).astype(F32)
    target = jnp.where(step < length, target, -1.0)
    return mine == target


def forward_kernel(
    x_hbm, gain_hbm, cot_hbm, a_hbm, b_hbm, keep_ref, send_ref, *rest
):
    mine_ref, other_ref = rest[:2]
    x_ref, gain_ref, a_buf, b_buf, normed_ref, left_ref, in_sem, a_sem, b_sem, out_sem = rest[2:]
    count, step, cols = a_buf.shape
    core = lax.axis_index("section")
    get_x = pltpu.make_async_copy(x_hbm, x_ref, in_sem.at[0])
    get_gain = pltpu.make_async_copy(gain_hbm, gain_ref, in_sem.at[1])
    get_left = pltpu.make_async_copy(cot_hbm, left_ref, in_sem.at[2])
    get_x.start()
    get_gain.start()

    @pl.when(core != 0)
    def _():
        get_left.start()

    def fetch(k):
        rows = pl.ds(k * step, step)
        return (
            pltpu.make_async_copy(a_hbm.at[rows, :], a_buf.at[k], a_sem.at[k]),
            pltpu.make_async_copy(b_hbm.at[rows, :], b_buf.at[k], b_sem.at[k]),
        )

    for k in range(count):
        for copy in fetch(k):
            copy.start()
    get_x.wait()
    get_gain.wait()
    xf = x_ref[...].astype(F32)
    scale = lax.rsqrt(jnp.mean(xf * xf, axis=-1, keepdims=True) + EPS)
    normed_ref[...] = (xf * scale * gain_ref[...]).astype(BF16)

    @pl.when(core == 0)
    def _():
        left_ref[...] = normed_ref[...]

    @pl.when(core != 0)
    def _():
        get_left.wait()

    z, x = lax.axis_index("z"), lax.axis_index("x")
    quarter = pl.ds(pl.multiple_of(lax.axis_index("mp") * QUARTER, QUARTER), QUARTER)
    block = cols // RING
    copies = []
    for k in range(RING):
        for j in range(RING):
            to = slice(j * block, (j + 1) * block)
            at_x = ((z + j) % RING * RING + (x + k) % RING) * block
            at_z = ((z + k) % RING * RING + (x + j) % RING) * block
            at_mine = jnp.where(core == 0, at_x, at_z)
            at_other = jnp.where(core == 0, at_z, at_x)
            for source, at, out in ((left_ref, at_mine, mine_ref), (normed_ref, at_other, other_ref)):
                copies.append(
                    pltpu.make_async_copy(
                        source.at[quarter, pl.ds(pl.multiple_of(at, block), block)],
                        out.at[k, :, to],
                        out_sem.at[len(copies)],
                    )
                )
                copies[-1].start()

    acc_a = acc_b = None
    for k in range(count):
        for copy in fetch(k):
            copy.wait()
        at = slice(k * step, (k + 1) * step)
        part_a = jnp.dot(normed_ref[:, at], a_buf[k], preferred_element_type=F32)
        part_b = jnp.dot(left_ref[:, at], b_buf[k], preferred_element_type=F32)
        acc_a = part_a if acc_a is None else acc_a + part_a
        acc_b = part_b if acc_b is None else acc_b + part_b
    half = cols // 2
    parts = [[acc[:, i * half : (i + 1) * half].astype(BF16) for acc in (acc_a, acc_b)] for i in range(2)]

    def put(ref, pieces):
        ref[:, :half] = pieces[0]
        ref[:, half:] = pieces[1]

    @pl.when(core == 0)
    def _():
        put(keep_ref, parts[0])
        put(send_ref, parts[1])

    @pl.when(core != 0)
    def _():
        put(keep_ref, parts[1])
        put(send_ref, parts[0])

    for copy in copies:
        copy.wait()


def forward(x, gain, cot, weight_a, weight_b):
    rows, width = x.shape
    cols = weight_a.shape[1]
    step = 512
    count = width // step
    half = jax.ShapeDtypeStruct((rows, cols), BF16)
    return pl.pallas_call(
        forward_kernel,
        in_specs=[HBM] * 5,
        out_specs=[VMEM] * 4,
        out_shape=[half] * 2 + [jax.ShapeDtypeStruct((RING, QUARTER, cols), BF16)] * 2,
        scratch_shapes=[pltpu.VMEM((rows, width), BF16), pltpu.VMEM((1, width), F32)]
        + [pltpu.VMEM((count, step, cols), BF16)] * 2
        + [pltpu.VMEM((rows, width), BF16)] * 2
        + [pltpu.SemaphoreType.DMA((3,))]
        + [pltpu.SemaphoreType.DMA((count,))] * 2
        + [pltpu.SemaphoreType.DMA((2 * RING * RING,))],
        compiler_params=params(32),
        cost_estimate=cost(4 * rows * width * cols, 4 * width * cols),
        name="forward",
    )(in_hbm(x), in_hbm(gain), in_hbm(cot), in_hbm(weight_a), in_hbm(weight_b))


def wait_all(copies):
    for copy in copies:
        copy.wait()


def pack_kernel(keep_ref, got_ref, src_ref, dest_ref, mine_ref, other_ref, out_ref, *rest):
    for out, k in zip(rest, (0, 1, 3, 2), strict=True):
        out[0] = mine_ref[k]
        out[1] = other_ref[k]
    spread = slot_onehot(member_index(), src_ref, dest_ref)

    @pl.when(lax.axis_index("section") == 0)
    def _():
        out_ref[...] = jnp.dot(spread, keep_ref[...], preferred_element_type=F32).astype(BF16)

    @pl.when(lax.axis_index("section") != 0)
    def _():
        out_ref[...] = jnp.dot(spread, got_ref[...], preferred_element_type=F32).astype(BF16)


def pack(keep, got, src_len, dest, mine, other):
    width = keep.shape[1]
    _, rows, cols = mine.shape
    outs = pl.pallas_call(
        pack_kernel,
        in_specs=[VMEM] * 6,
        out_specs=[VMEM] * (1 + RING),
        out_shape=[jax.ShapeDtypeStruct((SLOTS, width), BF16)]
        + [jax.ShapeDtypeStruct((2, rows, cols), BF16)] * RING,
        compiler_params=params(),
        cost_estimate=cost(2 * SLOTS * TOK * width, 2 * SLOTS * width),
        name="pack",
    )(keep, got, src_len, dest, mine, other)
    return outs[0], outs[1:]


def attend_kernel(
    keep_ref, got_ref, slots_ref, src_ref, tgt_ref, dest_ref, *rest
):
    front_ref, back_ref, stack_ref, own_ref = rest[RING:]
    for p in range(RING):
        for m in range(2):
            stack_ref[m, p] = rest[p][m]
    mask = pair_mask(member_index(), src_ref, tgt_ref, dest_ref)

    @pl.when(lax.axis_index("section") == 0)
    def _():
        own_ref[...] = got_ref[...]

    @pl.when(lax.axis_index("section") != 0)
    def _():
        own_ref[...] = keep_ref[...]

    half = own_ref.shape[1] // 2
    pair = 2 * HEAD_DIM
    low = iota((1, pair), 1) < HEAD_DIM
    nothing = jnp.zeros((), BF16)

    def both(value):
        return jnp.concatenate(
            [jnp.where(low, value, nothing), jnp.where(low, nothing, value)], axis=0
        )

    def nt(left, right):
        return lax.dot_general(left, right, (((1,), (1,)), ((), ())), preferred_element_type=F32)

    def one(score, dweight):
        expo = jnp.where(mask, jnp.exp(score), 0.0)
        weight = expo * (1.0 / jnp.sum(expo, axis=-1, keepdims=True))
        mean = jnp.sum(weight * dweight, axis=-1, keepdims=True)
        return weight.astype(BF16), (weight * (dweight - mean)).astype(BF16)

    def fold(value):
        return jnp.where(low, value[:SLOTS], value[SLOTS:]).astype(BF16)

    for p in range(half // pair):
        first = slice(p * pair, (p + 1) * pair)
        second = slice(half + p * pair, half + (p + 1) * pair)
        query, dout = own_ref[:, first], own_ref[:, second]
        keys, values = both(slots_ref[:, first]), both(slots_ref[:, second])
        score, dweight = nt(query, keys), nt(dout, values)
        weight_0, dscore_0 = one(score[:, :SLOTS], dweight[:, :SLOTS])
        weight_1, dscore_1 = one(score[:, SLOTS:], dweight[:, SLOTS:])
        weight = jnp.concatenate([weight_0, weight_1], axis=1)
        dscore = jnp.concatenate([dscore_0, dscore_1], axis=1)
        front_ref[:, first] = jnp.dot(dscore, keys, preferred_element_type=F32).astype(BF16)
        front_ref[:, second] = jnp.dot(weight, values, preferred_element_type=F32).astype(BF16)
        back_ref[:, first] = fold(tn(dscore, query))
        back_ref[:, second] = fold(tn(weight, dout))


def attend(keep, got, slots, src_len, tgt_len, dest, pieces):
    rows, width = keep.shape
    _, quarter, cols = pieces[0].shape
    return pl.pallas_call(
        attend_kernel,
        in_specs=[VMEM] * (6 + RING),
        out_specs=[VMEM] * 3,
        out_shape=[
            jax.ShapeDtypeStruct((rows, width), BF16),
            jax.ShapeDtypeStruct((SLOTS, width), BF16),
            jax.ShapeDtypeStruct((2, RING, quarter, cols), BF16),
        ],
        scratch_shapes=[pltpu.VMEM((rows, width), BF16)],
        compiler_params=params(),
        cost_estimate=cost(24 * rows * SLOTS * width, 8 * SLOTS * width),
        name="attend",
    )(keep, got, slots, src_len, tgt_len, dest, *pieces)


def unpack_kernel(back_ref, front_ref, src_ref, dest_ref, keep_ref, send_ref):
    spread = slot_onehot(member_index(), src_ref, dest_ref)
    rows = tn(spread, back_ref[...]).astype(BF16)
    half = rows.shape[1] // 2
    core = lax.axis_index("section")

    @pl.when(core == 0)
    def _():
        keep_ref[:, :half] = rows[:, :half]
        keep_ref[:, half:] = front_ref[:, :half]
        send_ref[:, :half] = front_ref[:, half:]
        send_ref[:, half:] = rows[:, half:]

    @pl.when(core != 0)
    def _():
        keep_ref[:, :half] = front_ref[:, half:]
        keep_ref[:, half:] = rows[:, half:]
        send_ref[:, :half] = rows[:, :half]
        send_ref[:, half:] = front_ref[:, :half]


def unpack(back, front, src_len, dest):
    width = front.shape[1]
    half = jax.ShapeDtypeStruct((TOK, width), BF16)
    return pl.pallas_call(
        unpack_kernel,
        in_specs=[VMEM] * 4,
        out_specs=[VMEM] * 2,
        out_shape=[half, half],
        compiler_params=params(),
        cost_estimate=cost(2 * SLOTS * TOK * width, 4 * SLOTS * width),
        name="unpack",
    )(back, front, src_len, dest)


def join_kernel(keep_ref, got_ref, rows_ref, other_ref):
    width = keep_ref.shape[1]
    half = width // 2
    core = lax.axis_index("section")
    mine = pl.multiple_of(core * half, half)
    theirs = pl.multiple_of((1 - core) * half, half)
    for ref, at in ((keep_ref, mine), (got_ref, theirs)):
        rows_ref[:, pl.ds(at, half)] = ref[:, :half]
        rows_ref[:, pl.ds(pl.multiple_of(width + at, half), half)] = ref[:, half:]
        other_ref[:, pl.ds(at, half)] = ref[:, half:]


def join(keep, got):
    rows, width = keep.shape
    return pl.pallas_call(
        join_kernel,
        in_specs=[VMEM, VMEM],
        out_specs=[VMEM] * 2,
        out_shape=[
            jax.ShapeDtypeStruct((rows, 2 * width), BF16),
            jax.ShapeDtypeStruct((rows, width), BF16),
        ],
        compiler_params=params(),
        cost_estimate=cost(0, 8 * keep.size),
        name="join",
    )(keep, got)


def dnorm_kernel(rows_ref, got_ref, a_hbm, b_hbm, out_hbm, a_buf, b_buf, out_buf, a_sem, b_sem, out_sem):
    count, step, cols = a_buf.shape
    core = lax.axis_index("section")

    def nt(left, right):
        return lax.dot_general(left, right, (((1,), (1,)), ((), ())), preferred_element_type=F32)

    def fetches(hbm, buf, sem):
        return [
            pltpu.make_async_copy(hbm.at[pl.ds(k * step, step), :], buf.at[k], sem.at[k])
            for k in range(count)
        ]

    get_a, get_b = fetches(a_hbm, a_buf, a_sem), fetches(b_hbm, b_buf, b_sem)

    def put(k):
        at = slice(k * step, (k + 1) * step)
        return pltpu.make_async_copy(out_buf.at[:, at], out_hbm.at[:, at], out_sem.at[k])

    @pl.when(core == 0)
    def _():
        for k in range(count):
            get_a[k].start()
            get_b[k].start()
        for k in range(count):
            get_a[k].wait()
            get_b[k].wait()
            block = nt(rows_ref[:, :cols], a_buf[k]) + nt(got_ref[...], b_buf[k])
            out_buf[:, k * step : (k + 1) * step] = block.astype(BF16)
            put(k).start()

    @pl.when(core != 0)
    def _():
        for k in range(count):
            get_a[k].start()
        for k in range(count):
            get_a[k].wait()
            out_buf[:, k * step : (k + 1) * step] = nt(got_ref[...], a_buf[k]).astype(BF16)
            put(k).start()

    for k in range(count):
        put(k).wait()


def dnorm_partial(rows, got, weight_a, weight_b):
    width, cols = weight_a.shape
    step = 512
    count = width // step
    return pl.pallas_call(
        dnorm_kernel,
        in_specs=[VMEM] * 2 + [HBM] * 2,
        out_specs=HBM,
        out_shape=pltpu.HBM((TOK, width), BF16),
        scratch_shapes=[pltpu.VMEM((count, step, cols), BF16)] * 2
        + [pltpu.VMEM((TOK, width), BF16)]
        + [pltpu.SemaphoreType.DMA((count,))] * 3,
        compiler_params=params(24),
        cost_estimate=cost(4 * TOK * width * cols, 4 * width * cols),
        name="dnorm",
    )(rows, got, in_hbm(weight_a), in_hbm(weight_b))


def rms_back_kernel(x_hbm, gain_ref, parts_ref, out_hbm, x_ref, row_ref, sem, sems):
    rows = row_ref.shape[0]
    mine = pl.multiple_of(lax.axis_index("mp") * rows, rows)
    get_x = pltpu.make_async_copy(x_hbm.at[pl.ds(mine, rows), :], x_ref, sem)
    get_x.start()
    dnorm = parts_ref[0].astype(F32)
    for i in range(1, RING):
        dnorm += parts_ref[i].astype(F32)
    get_x.wait()
    xf = x_ref[...].astype(F32)
    scale = lax.rsqrt(jnp.mean(xf * xf, axis=-1, keepdims=True) + EPS)
    upper = gain_ref[...] * dnorm
    inner = jnp.mean(xf * upper, axis=-1, keepdims=True)
    row_ref[...] = (scale * upper - xf * (scale * scale * scale * inner)).astype(BF16)
    puts = [pltpu.make_async_copy(row_ref, out_hbm.at[i], sems.at[i]) for i in range(RING)]
    for put in puts:
        put.start()
    for put in puts:
        put.wait()


def rms_back(x, gain, parts):
    _, rows, width = parts.shape
    return pl.pallas_call(
        rms_back_kernel,
        in_specs=[HBM] + [VMEM] * 2,
        out_specs=HBM,
        out_shape=pltpu.HBM((RING, rows, width), BF16),
        scratch_shapes=[pltpu.VMEM((rows, width), BF16)] * 2
        + [pltpu.SemaphoreType.DMA, pltpu.SemaphoreType.DMA((RING,))],
        compiler_params=params(),
        cost_estimate=cost(10 * rows * width, 12 * rows * width),
        name="rms_back",
    )(in_hbm(x), gain, parts)


def shift(value, axis, k):
    return lax.ppermute(value, axis, [(i, (i + k) % RING) for i in range(RING)])


def gathered(block, axis):
    left, right = lax.optimization_barrier((shift(block, axis, 1), shift(block, axis, 3)))
    return [block, left, right, shift(left, axis, 1)]


def moved(value, k, along, across=False):
    pairs = []
    for core in range(2):
        for z in range(RING):
            for x in range(RING):
                to = {"z": z, "x": x}
                to[along[core]] = (to[along[core]] + k) % RING
                target = (1 - core if across else core, to["z"], to["x"])
                pairs.append(
                    ((core * RING + z) * RING + x, (target[0] * RING + target[1]) * RING + target[2])
                )
    return lax.ppermute(value, ("section", "z", "x"), pairs)


GATHER, REDUCE = "xz", "zx"


def fetched(own, others):
    return [own] + [moved(others[k], k, GATHER) for k in (1, 3, 2)]


def left_loads(lefts, buf, sems, ks):
    block = buf.shape[-1]
    mine = lax.axis_index("mp")
    loads = [[[] for _ in ks] for _ in range(2)]
    for f in range(2):
        for i, k in enumerate(ks):
            for j, (left, distance) in enumerate(zip(lefts, ORDER, strict=True)):
                at = pl.multiple_of((mine + distance) % RING * QUARTER, QUARTER)
                loads[f][i].append(
                    pltpu.make_async_copy(
                        left.at[f, :, :, pl.ds(k * block, block)],
                        buf.at[f, i, :, pl.ds(at, QUARTER), :],
                        sems.at[f, i, j],
                    )
                )
                loads[f][i][-1].start()
    return loads


def left_scratch(block, count):
    return [
        pltpu.VMEM((2, count, RING, TOK, block), BF16),
        pltpu.SemaphoreType.DMA((2, count, RING)),
    ]


def flat(value):
    return value.reshape(RING * TOK, value.shape[-1])


def far_kernel(*refs):
    lefts, pieces = refs[:RING], refs[RING : 2 * RING]
    top_ref, low_ref, rows_ref, other_ref, buf, sems = refs[2 * RING :]
    loads = left_loads(lefts, buf, sems, (2, 0))
    for i, piece in enumerate(pieces):
        rows_ref[i * TOK : (i + 1) * TOK, :] = piece[...]
    half, cols = top_ref.shape[0], top_ref.shape[1] // 2
    for m in range(2):
        at = slice(m * cols, (m + 1) * cols)
        wait_all(loads[m][0])
        block = tn(flat(buf[m, 0]), rows_ref[:, at]).astype(BF16)
        top_ref[:, at] = block[:half]
        low_ref[:, at] = block[half:]
    wait_all(loads[0][1])
    wait_all(loads[1][1])
    other_ref[...] = tn(flat(buf[1, 1]), rows_ref[:, cols:]).astype(BF16)


def far_block(lefts, pieces):
    rows, cols = pieces[0].shape
    block = lefts[0].shape[-1] // RING
    half = jax.ShapeDtypeStruct((block // 2, cols), BF16)
    return pl.pallas_call(
        far_kernel,
        in_specs=[HBM] * RING + [VMEM] * RING,
        out_specs=[VMEM] * 4,
        out_shape=[
            half,
            half,
            jax.ShapeDtypeStruct((RING * rows, cols), BF16),
            jax.ShapeDtypeStruct((block, cols // 2), BF16),
        ],
        scratch_shapes=left_scratch(block, 2),
        compiler_params=params(),
        cost_estimate=cost(3 * RING * rows * block * cols, 8 * RING * rows * cols),
        name="far",
    )(*[in_hbm(left) for left in lefts], *pieces)


def side_kernel(*refs):
    lefts, (rows_ref, from_left, from_right) = refs[:RING], refs[RING : RING + 3]
    rights, to_lefts, buf, sems = refs[RING + 3 : RING + 5], refs[RING + 5 : RING + 7], *refs[RING + 7 :]
    loads = left_loads(lefts, buf, sems, (1, 3))
    half, cols = from_left.shape[0], rights[0].shape[1]
    for m in range(2):
        at = slice(m * cols, (m + 1) * cols)

        def product(i, m=m, at=at):
            wait_all(loads[m][i])
            return tn(flat(buf[m, i]), rows_ref[:, at])

        block = product(0)
        rights[m][:half, :] = (block[:half] + from_left[:, at].astype(F32)).astype(BF16)
        rights[m][half:, :] = block[half:].astype(BF16)
        block = product(1)
        to_lefts[m][:half, :] = block[:half].astype(BF16)
        to_lefts[m][half:, :] = (block[half:] + from_right[:, at].astype(F32)).astype(BF16)


def side_blocks(lefts, rows, from_left, from_right):
    depth, cols = rows.shape
    block = lefts[0].shape[-1] // RING
    shape = jax.ShapeDtypeStruct((block, cols // 2), BF16)
    return pl.pallas_call(
        side_kernel,
        in_specs=[HBM] * RING + [VMEM] * 3,
        out_specs=[VMEM] * 4,
        out_shape=[shape] * 4,
        scratch_shapes=left_scratch(block, 2),
        compiler_params=params(),
        cost_estimate=cost(4 * depth * block * cols, 4 * depth * cols),
        name="side",
    )(*[in_hbm(left) for left in lefts], rows, from_left, from_right)


def middle_kernel(*refs):
    lefts, (rows_ref, own_hbm, out_buf, buf, sems, out_sem) = refs[:RING], refs[RING:]
    loads = left_loads(lefts, buf, sems, (0,))
    wait_all(loads[0][0])
    wait_all(loads[1][0])
    out_buf[...] = tn(flat(buf[0, 0]), rows_ref[:, : out_buf.shape[1]]).astype(BF16)
    put = pltpu.make_async_copy(out_buf, own_hbm, out_sem)
    put.start()
    put.wait()


def middle_block(lefts, rows):
    depth, cols = rows.shape
    block = lefts[0].shape[-1] // RING
    return pl.pallas_call(
        middle_kernel,
        in_specs=[HBM] * RING + [VMEM],
        out_specs=HBM,
        out_shape=pltpu.HBM((block, cols // 2), BF16),
        scratch_shapes=[pltpu.VMEM((block, cols // 2), BF16)]
        + left_scratch(block, 1)
        + [pltpu.SemaphoreType.DMA],
        compiler_params=params(),
        cost_estimate=cost(depth * block * cols, 4 * depth * cols),
        name="middle",
    )(*[in_hbm(left) for left in lefts], rows)


def own_kernel(own_hbm, other_hbm, *refs):
    parts, outs, (base_ref, out_buf, base_sems, out_sems) = refs[:4], refs[4:6], refs[6:]
    gets = [
        pltpu.make_async_copy(base, base_ref.at[m], base_sems.at[m])
        for m, base in enumerate((own_hbm, other_hbm))
    ]
    for get in gets:
        get.start()
    core = lax.axis_index("section")
    chunks = out_sems.shape[1]
    size = out_buf.shape[1] // chunks

    def put(m, c, out):
        at = slice(c * size, (c + 1) * size)
        return pltpu.make_async_copy(out_buf.at[m, at], out.at[at], out_sems.at[m, c])

    def write(m, c):
        @pl.when(core == m)
        def _():
            put(m, c, outs[0]).start()

        @pl.when(core != m)
        def _():
            put(m, c, outs[1]).start()

    for m in range(2):
        gets[m].wait()
        for c in range(chunks):
            at = slice(c * size, (c + 1) * size)
            total_of = base_ref[m, at].astype(F32) + parts[2 * m][at].astype(F32)
            out_buf[m, at] = total_of + parts[2 * m + 1][at].astype(F32)
            write(m, c)
    for m in range(2):
        for c in range(chunks):
            put(m, c, outs[0]).wait()


def own_blocks(own, other, parts):
    block, cols = own.shape
    return pl.pallas_call(
        own_kernel,
        in_specs=[HBM] * 2 + [VMEM] * 4,
        out_specs=[HBM] * 2,
        out_shape=[pltpu.HBM((block, cols), F32)] * 2,
        scratch_shapes=[
            pltpu.VMEM((2, block, cols), BF16),
            pltpu.VMEM((2, block, cols), F32),
            pltpu.SemaphoreType.DMA((2,)),
            pltpu.SemaphoreType.DMA((2, 4)),
        ],
        compiler_params=params(),
        cost_estimate=cost(4 * block * cols, 20 * block * cols),
        name="own",
    )(in_hbm(own), in_hbm(other), *parts)


def per_device(states, gains, proj_a, proj_b, cotangent, src_len, tgt_len, dest):
    weight_a = proj_a[0]
    weight_b = proj_b[0]
    rows = states[0]
    keep, send, mine, other = forward(rows, gains, cotangent, weight_a, weight_b)
    swap = [(0, 1), (1, 0)]
    got = lax.ppermute(send, "section", swap)
    slots, slices = pack(keep, got, src_len, dest, mine, lax.ppermute(other, "section", swap))
    width = slots.shape[1]
    slots = slots.reshape(SEQ_DEV, MAXLEN, width)
    slots = lax.all_to_all(slots, ("z", "x"), split_axis=0, concat_axis=0, tiled=True)
    slots = slots.reshape(SLOTS, width)
    pieces = fetched(slices[0], {1: slices[1], 3: slices[2], 2: slices[3]})
    front, back, own = attend(keep, got, slots, src_len, tgt_len, dest, pieces)
    lefts = gathered(own, "mp")
    back = back.reshape(SEQ_DEV, MAXLEN, width)
    back = lax.all_to_all(back, ("z", "x"), split_axis=0, concat_axis=0, tiled=True)
    keep, send = unpack(back.reshape(SLOTS, width), front, src_len, dest)
    got = lax.ppermute(send, "section", swap)
    kind, others = join(keep, got)

    rights = fetched(kind, {k: kind for k in (1, 2, 3)})
    others = lax.ppermute(others, "section", swap)
    others, lefts[1], lefts[2] = lax.optimization_barrier((others, lefts[1], lefts[2]))
    partial = dnorm_partial(kind, others, weight_a, weight_b)
    partial, rights[1], rights[2] = lax.optimization_barrier((partial, rights[1], rights[2]))
    parts = lax.all_to_all(
        partial.reshape(RING, TOK // RING, -1), "mp", split_axis=0, concat_axis=0, tiled=True
    )
    top, low, stack, own_other = far_block(lefts, rights)
    from_left, from_right = moved(top, 1, REDUCE), moved(low, 3, REDUCE)
    own = middle_block(lefts, stack)
    crossed = lax.ppermute(own_other, "section", swap)
    stack, own, crossed = lax.optimization_barrier((stack, own, crossed))
    right, right_other, left, left_other = side_blocks(lefts, stack, from_left, from_right)
    left_other, parts = lax.optimization_barrier((left_other, parts))
    sums = [
        moved(right, 1, REDUCE),
        moved(left, 3, REDUCE),
        moved(right_other, 1, REDUCE, True),
        moved(left_other, 3, REDUCE, True),
    ]
    quarters = rms_back(rows, gains, parts)
    quarters = lax.all_to_all(quarters, "mp", split_axis=0, concat_axis=0, tiled=True)
    grad_a, grad_b = own_blocks(own, crossed, sums)
    grad_states = quarters.reshape(rows.shape)
    return (grad_states[None], grad_a[None], grad_b[None])


def solution(mesh):
    split = jax.sharding.Mesh(mesh.devices.reshape(2, RING, RING, RING), ("section", "z", "x", "mp"))
    dp = ("z", "x")
    return jax.shard_map(
        per_device,
        mesh=split,
        in_specs=(
            P("section", dp, None),
            P("section", None),
            P("section", None, "mp"),
            P("section", None, "mp"),
            P(dp, None),
            P(),
            P(),
            P(),
        ),
        out_specs=(P("section", dp, None), P("section", dp, "mp"), P("section", dp, "mp")),
        check_vma=False,
    )
```

```python
import jax
import jax.numpy as jnp
from jax import lax
from jax.experimental import pallas as pl
from jax.experimental.pallas import tpu as pltpu
from jax.sharding import PartitionSpec as P

HEAD_DIM = 64
SEQ_DEV = 16
MAXLEN = 16
TOK = 128
SLOTS = 256
RING = 4
QUARTER = TOK // RING
ORDER = (0, 3, 1, 2)
EPS = 1e-06
SHARE = 16
F32 = jnp.float32
BF16 = jnp.bfloat16
VMEM = pl.BlockSpec(memory_space=pltpu.VMEM)
ANY = pl.BlockSpec(memory_space=pl.ANY)
HBM = pl.BlockSpec(memory_space=pltpu.HBM)


def iota(shape, dim):
    return lax.broadcasted_iota(jnp.int32, shape, dim)


def total(value, axis):
    return jnp.sum(value.astype(F32), axis=axis, keepdims=True)


def tn(left, right):
    return lax.dot_general(left, right, (((0,), (0,)), ((), ())), preferred_element_type=F32)


def in_hbm(value):
    return pltpu.with_memory_space_constraint(value, pltpu.HBM)


def cost(flops, nbytes):
    return pl.CostEstimate(flops=flops // SHARE, bytes_accessed=nbytes // SHARE, transcendentals=0)


def params(mib=12, **more):
    return pltpu.CompilerParams(vmem_limit_bytes=mib << 20, **more)


def column_of(row):
    square = jnp.broadcast_to(row, (SEQ_DEV, SEQ_DEV))
    same = iota((SEQ_DEV, SEQ_DEV), 0) == iota((SEQ_DEV, SEQ_DEV), 1)
    return total(jnp.where(same, square, 0), 1)


def member_index():
    return lax.axis_index("z") * RING + lax.axis_index("x")


def slot_onehot(member, src_len, dest):
    i, j = iota((SEQ_DEV, SEQ_DEV), 0), iota((SEQ_DEV, SEQ_DEV), 1)
    lengths = src_len[pl.ds(member, 1), :]
    ends = total(jnp.where(j <= i, jnp.broadcast_to(lengths, (SEQ_DEV, SEQ_DEV)), 0), 1)
    begins = ends - column_of(lengths)
    place = column_of(dest[pl.ds(member, 1), :] >> 4) * MAXLEN
    row = iota((SEQ_DEV, TOK), 1).astype(F32)
    inside = (row >= begins) & (row < ends)
    target = total(jnp.where(inside, place + row - begins, 0.0), 0)
    hit = iota((SLOTS, TOK), 0).astype(F32) == target
    return jnp.where(hit, 1.0, 0.0).astype(BF16)


def pair_mask(member, src_len, tgt_len, dest):
    i, j = iota((SEQ_DEV, SEQ_DEV), 0), iota((SEQ_DEV, SEQ_DEV), 1)
    column = column_of(tgt_len[pl.ds(member, 1), :])
    ends = total(jnp.where(i <= j, jnp.broadcast_to(column, (SEQ_DEV, SEQ_DEV)), 0.0), 0)
    row = iota((TOK, SEQ_DEV), 0).astype(F32)
    mine = total(jnp.where(row >= ends, 1.0, 0.0), 1)
    codes = dest[...]
    to_me = (codes >> 4) == member
    target = total(jnp.where(to_me, codes & 15, 0), 1)
    length = total(jnp.where(to_me, src_len[...], 0), 1)
    lane = iota((SEQ_DEV, SLOTS), 1)
    own = (lane >> 4) == iota((SEQ_DEV, SLOTS), 0)
    target = total(jnp.where(own, target, 0.0), 0)
    length = total(jnp.where(own, length, 0.0), 0)
    step = (iota((1, SLOTS), 1) & 15).astype(F32)
    target = jnp.where(step < length, target, -1.0)
    return mine == target


def forward_kernel(
    x_hbm, gain_hbm, cot_hbm, a_hbm, b_hbm, keep_ref, send_ref, *rest
):
    mine_ref, other_ref = rest[:2]
    x_ref, gain_ref, a_buf, b_buf, normed_ref, left_ref, in_sem, a_sem, b_sem, out_sem = rest[2:]
    count, step, cols = a_buf.shape
    core = lax.axis_index("section")
    get_x = pltpu.make_async_copy(x_hbm, x_ref, in_sem.at[0])
    get_gain = pltpu.make_async_copy(gain_hbm, gain_ref, in_sem.at[1])
    get_left = pltpu.make_async_copy(cot_hbm, left_ref, in_sem.at[2])
    get_x.start()
    get_gain.start()

    def fetch(k):
        rows = pl.ds(k * step, step)
        return (
            pltpu.make_async_copy(a_hbm.at[rows, :], a_buf.at[k], a_sem.at[k]),
            pltpu.make_async_copy(b_hbm.at[rows, :], b_buf.at[k], b_sem.at[k]),
        )

    for k in range(count):
        copy_a, copy_b = fetch(k)
        copy_a.start()
        if k == 0:

            @pl.when(core != 0)
            def _():
                get_left.start()

        copy_b.start()
    get_x.wait()
    get_gain.wait()
    xf = x_ref[...].astype(F32)
    scale = lax.rsqrt(jnp.mean(xf * xf, axis=-1, keepdims=True) + EPS)
    normed_ref[...] = (xf * scale * gain_ref[...]).astype(BF16)

    def product(ref, k, buf):
        return jnp.dot(ref[:, k * step : (k + 1) * step], buf[k], preferred_element_type=F32)

    fetch(0)[0].wait()
    acc_a = product(normed_ref, 0, a_buf)

    @pl.when(core == 0)
    def _():
        left_ref[...] = normed_ref[...]

    @pl.when(core != 0)
    def _():
        get_left.wait()

    fetch(0)[1].wait()
    acc_b = product(left_ref, 0, b_buf)
    z, x = lax.axis_index("z"), lax.axis_index("x")
    quarter = pl.ds(pl.multiple_of(lax.axis_index("mp") * QUARTER, QUARTER), QUARTER)
    block = cols // RING
    copies = []
    for k in range(RING):
        for j in range(RING):
            to = slice(j * block, (j + 1) * block)
            at_x = ((z + j) % RING * RING + (x + k) % RING) * block
            at_z = ((z + k) % RING * RING + (x + j) % RING) * block
            at_mine = jnp.where(core == 0, at_x, at_z)
            at_other = jnp.where(core == 0, at_z, at_x)
            for source, at, out in ((left_ref, at_mine, mine_ref), (normed_ref, at_other, other_ref)):
                copies.append(
                    pltpu.make_async_copy(
                        source.at[quarter, pl.ds(pl.multiple_of(at, block), block)],
                        out.at[k, :, to],
                        out_sem.at[len(copies)],
                    )
                )
                copies[-1].start()

    for k in range(1, count):
        for copy in fetch(k):
            copy.wait()
        acc_a += product(normed_ref, k, a_buf)
        acc_b += product(left_ref, k, b_buf)
    half = cols // 2
    parts = [[acc[:, i * half : (i + 1) * half].astype(BF16) for acc in (acc_a, acc_b)] for i in range(2)]

    def put(ref, pieces):
        ref[:, :half] = pieces[0]
        ref[:, half:] = pieces[1]

    @pl.when(core == 0)
    def _():
        put(keep_ref, parts[0])
        put(send_ref, parts[1])

    @pl.when(core != 0)
    def _():
        put(keep_ref, parts[1])
        put(send_ref, parts[0])

    for copy in copies:
        copy.wait()


def forward(x, gain, cot, weight_a, weight_b):
    rows, width = x.shape
    cols = weight_a.shape[1]
    step = 512
    count = width // step
    half = jax.ShapeDtypeStruct((rows, cols), BF16)
    return pl.pallas_call(
        forward_kernel,
        in_specs=[HBM] * 5,
        out_specs=[VMEM] * 4,
        out_shape=[half] * 2 + [jax.ShapeDtypeStruct((RING, QUARTER, cols), BF16)] * 2,
        scratch_shapes=[pltpu.VMEM((rows, width), BF16), pltpu.VMEM((1, width), F32)]
        + [pltpu.VMEM((count, step, cols), BF16)] * 2
        + [pltpu.VMEM((rows, width), BF16)] * 2
        + [pltpu.SemaphoreType.DMA((3,))]
        + [pltpu.SemaphoreType.DMA((count,))] * 2
        + [pltpu.SemaphoreType.DMA((2 * RING * RING,))],
        compiler_params=params(32),
        cost_estimate=cost(4 * rows * width * cols, 4 * width * cols),
        name="forward",
    )(in_hbm(x), in_hbm(gain), in_hbm(cot), in_hbm(weight_a), in_hbm(weight_b))


def wait_all(copies):
    for copy in copies:
        copy.wait()


def pack_kernel(keep_ref, got_ref, src_ref, dest_ref, mine_ref, other_ref, out_ref, *rest):
    for out, k in zip(rest, (0, 1, 3, 2), strict=True):
        out[0] = mine_ref[k]
        out[1] = other_ref[k]
    spread = slot_onehot(member_index(), src_ref, dest_ref)

    @pl.when(lax.axis_index("section") == 0)
    def _():
        out_ref[...] = jnp.dot(spread, keep_ref[...], preferred_element_type=F32).astype(BF16)

    @pl.when(lax.axis_index("section") != 0)
    def _():
        out_ref[...] = jnp.dot(spread, got_ref[...], preferred_element_type=F32).astype(BF16)


def pack(keep, got, src_len, dest, mine, other):
    width = keep.shape[1]
    _, rows, cols = mine.shape
    outs = pl.pallas_call(
        pack_kernel,
        in_specs=[VMEM] * 6,
        out_specs=[VMEM] * (1 + RING),
        out_shape=[jax.ShapeDtypeStruct((SLOTS, width), BF16)]
        + [jax.ShapeDtypeStruct((2, rows, cols), BF16)] * RING,
        compiler_params=params(),
        cost_estimate=cost(2 * SLOTS * TOK * width, 2 * SLOTS * width),
        name="pack",
    )(keep, got, src_len, dest, mine, other)
    return outs[0], outs[1:]


def attend_kernel(
    keep_ref, got_ref, slots_ref, src_ref, tgt_ref, dest_ref, front_ref, back_ref, own_ref
):
    mask = pair_mask(member_index(), src_ref, tgt_ref, dest_ref)

    @pl.when(lax.axis_index("section") == 0)
    def _():
        own_ref[...] = got_ref[...]

    @pl.when(lax.axis_index("section") != 0)
    def _():
        own_ref[...] = keep_ref[...]

    half = own_ref.shape[1] // 2
    pair = 2 * HEAD_DIM
    low = iota((1, pair), 1) < HEAD_DIM
    nothing = jnp.zeros((), BF16)

    def both(value):
        return jnp.concatenate(
            [jnp.where(low, value, nothing), jnp.where(low, nothing, value)], axis=0
        )

    def nt(left, right):
        return lax.dot_general(left, right, (((1,), (1,)), ((), ())), preferred_element_type=F32)

    def one(score, dweight):
        expo = jnp.where(mask, jnp.exp(score), 0.0)
        weight = expo * (1.0 / jnp.sum(expo, axis=-1, keepdims=True))
        mean = jnp.sum(weight * dweight, axis=-1, keepdims=True)
        return weight.astype(BF16), (weight * (dweight - mean)).astype(BF16)

    def fold(value):
        return jnp.where(low, value[:SLOTS], value[SLOTS:]).astype(BF16)

    for p in range(half // pair):
        first = slice(p * pair, (p + 1) * pair)
        second = slice(half + p * pair, half + (p + 1) * pair)
        query, dout = own_ref[:, first], own_ref[:, second]
        keys, values = both(slots_ref[:, first]), both(slots_ref[:, second])
        score, dweight = nt(query, keys), nt(dout, values)
        weight_0, dscore_0 = one(score[:, :SLOTS], dweight[:, :SLOTS])
        weight_1, dscore_1 = one(score[:, SLOTS:], dweight[:, SLOTS:])
        weight = jnp.concatenate([weight_0, weight_1], axis=1)
        dscore = jnp.concatenate([dscore_0, dscore_1], axis=1)
        front_ref[:, first] = jnp.dot(dscore, keys, preferred_element_type=F32).astype(BF16)
        front_ref[:, second] = jnp.dot(weight, values, preferred_element_type=F32).astype(BF16)
        back_ref[:, first] = fold(tn(dscore, query))
        back_ref[:, second] = fold(tn(weight, dout))


def attend(keep, got, slots, src_len, tgt_len, dest):
    rows, width = keep.shape
    return pl.pallas_call(
        attend_kernel,
        in_specs=[VMEM] * 6,
        out_specs=[VMEM] * 2,
        out_shape=[
            jax.ShapeDtypeStruct((rows, width), BF16),
            jax.ShapeDtypeStruct((SLOTS, width), BF16),
        ],
        scratch_shapes=[pltpu.VMEM((rows, width), BF16)],
        compiler_params=params(),
        cost_estimate=cost(24 * rows * SLOTS * width, 8 * SLOTS * width),
        name="attend",
    )(keep, got, slots, src_len, tgt_len, dest)


def stack_kernel(*refs):
    for p in range(RING):
        for m in range(2):
            refs[RING][m, p] = refs[p][m]


def stacked(pieces):
    _, quarter, cols = pieces[0].shape
    return pl.pallas_call(
        stack_kernel,
        in_specs=[VMEM] * RING,
        out_specs=VMEM,
        out_shape=jax.ShapeDtypeStruct((2, RING, quarter, cols), BF16),
        compiler_params=params(),
        cost_estimate=cost(0, 4 * RING * pieces[0].size),
        name="stack",
    )(*pieces)


def unpack_kernel(back_ref, front_ref, src_ref, dest_ref, keep_ref, send_ref):
    spread = slot_onehot(member_index(), src_ref, dest_ref)
    rows = tn(spread, back_ref[...]).astype(BF16)
    half = rows.shape[1] // 2
    core = lax.axis_index("section")

    @pl.when(core == 0)
    def _():
        keep_ref[:, :half] = rows[:, :half]
        keep_ref[:, half:] = front_ref[:, :half]
        send_ref[:, :half] = front_ref[:, half:]
        send_ref[:, half:] = rows[:, half:]

    @pl.when(core != 0)
    def _():
        keep_ref[:, :half] = front_ref[:, half:]
        keep_ref[:, half:] = rows[:, half:]
        send_ref[:, :half] = rows[:, :half]
        send_ref[:, half:] = front_ref[:, :half]


def unpack(back, front, src_len, dest):
    width = front.shape[1]
    half = jax.ShapeDtypeStruct((TOK, width), BF16)
    return pl.pallas_call(
        unpack_kernel,
        in_specs=[VMEM] * 4,
        out_specs=[VMEM] * 2,
        out_shape=[half, half],
        compiler_params=params(),
        cost_estimate=cost(2 * SLOTS * TOK * width, 4 * SLOTS * width),
        name="unpack",
    )(back, front, src_len, dest)


def join_kernel(keep_ref, got_ref, rows_ref, other_ref):
    width = keep_ref.shape[1]
    half = width // 2
    core = lax.axis_index("section")
    mine = pl.multiple_of(core * half, half)
    theirs = pl.multiple_of((1 - core) * half, half)
    for ref, at in ((keep_ref, mine), (got_ref, theirs)):
        rows_ref[:, pl.ds(at, half)] = ref[:, :half]
        rows_ref[:, pl.ds(pl.multiple_of(width + at, half), half)] = ref[:, half:]
        other_ref[:, pl.ds(at, half)] = ref[:, half:]


def join(keep, got):
    rows, width = keep.shape
    return pl.pallas_call(
        join_kernel,
        in_specs=[VMEM, VMEM],
        out_specs=[VMEM] * 2,
        out_shape=[
            jax.ShapeDtypeStruct((rows, 2 * width), BF16),
            jax.ShapeDtypeStruct((rows, width), BF16),
        ],
        compiler_params=params(),
        cost_estimate=cost(0, 8 * keep.size),
        name="join",
    )(keep, got)


def dnorm_kernel(rows_ref, got_ref, a_hbm, b_hbm, out_hbm, a_buf, b_buf, out_buf, a_sem, b_sem, out_sem):
    count, step, cols = a_buf.shape
    core = lax.axis_index("section")

    def nt(left, right):
        return lax.dot_general(left, right, (((1,), (1,)), ((), ())), preferred_element_type=F32)

    def fetches(hbm, buf, sem):
        return [
            pltpu.make_async_copy(hbm.at[pl.ds(k * step, step), :], buf.at[k], sem.at[k])
            for k in range(count)
        ]

    get_a, get_b = fetches(a_hbm, a_buf, a_sem), fetches(b_hbm, b_buf, b_sem)

    def put(k):
        at = slice(k * step, (k + 1) * step)
        return pltpu.make_async_copy(out_buf.at[:, at], out_hbm.at[:, at], out_sem.at[k])

    @pl.when(core == 0)
    def _():
        for k in range(count):
            get_a[k].start()
            get_b[k].start()
        for k in range(count):
            get_a[k].wait()
            get_b[k].wait()
            block = nt(rows_ref[:, :cols], a_buf[k]) + nt(got_ref[...], b_buf[k])
            out_buf[:, k * step : (k + 1) * step] = block.astype(BF16)
            put(k).start()

    @pl.when(core != 0)
    def _():
        for k in range(count):
            get_a[k].start()
        for k in range(count):
            get_a[k].wait()
            out_buf[:, k * step : (k + 1) * step] = nt(got_ref[...], a_buf[k]).astype(BF16)
            put(k).start()

    for k in range(count):
        put(k).wait()


def dnorm_partial(rows, got, weight_a, weight_b):
    width, cols = weight_a.shape
    step = 512
    count = width // step
    return pl.pallas_call(
        dnorm_kernel,
        in_specs=[VMEM] * 2 + [HBM] * 2,
        out_specs=HBM,
        out_shape=pltpu.HBM((TOK, width), BF16),
        scratch_shapes=[pltpu.VMEM((count, step, cols), BF16)] * 2
        + [pltpu.VMEM((TOK, width), BF16)]
        + [pltpu.SemaphoreType.DMA((count,))] * 3,
        compiler_params=params(24),
        cost_estimate=cost(4 * TOK * width * cols, 4 * width * cols),
        name="dnorm",
    )(rows, got, in_hbm(weight_a), in_hbm(weight_b))


def rms_back_kernel(x_hbm, gain_ref, parts_ref, out_ref, x_ref, sem):
    rows = out_ref.shape[0]
    mine = pl.multiple_of(lax.axis_index("mp") * rows, rows)
    get_x = pltpu.make_async_copy(x_hbm.at[pl.ds(mine, rows), :], x_ref, sem)
    get_x.start()
    dnorm = parts_ref[0].astype(F32)
    for i in range(1, RING):
        dnorm += parts_ref[i].astype(F32)
    get_x.wait()
    xf = x_ref[...].astype(F32)
    scale = lax.rsqrt(jnp.mean(xf * xf, axis=-1, keepdims=True) + EPS)
    upper = gain_ref[...] * dnorm
    inner = jnp.mean(xf * upper, axis=-1, keepdims=True)
    out_ref[...] = (scale * upper - xf * (scale * scale * scale * inner)).astype(BF16)


def rms_back(x, gain, parts):
    rows, width = parts.shape[1:]
    return pl.pallas_call(
        rms_back_kernel,
        in_specs=[HBM] + [VMEM] * 2,
        out_specs=VMEM,
        out_shape=jax.ShapeDtypeStruct((rows, width), BF16),
        scratch_shapes=[pltpu.VMEM((rows, width), BF16), pltpu.SemaphoreType.DMA],
        compiler_params=params(),
        cost_estimate=cost(10 * rows * width, 12 * rows * width),
        name="rms_back",
    )(in_hbm(x), gain, parts)


def place_kernel(*refs):
    pieces, (out_hbm, sems) = refs[:RING], refs[RING:]
    rows = pieces[0].shape[0]
    copies = []
    for i, k in enumerate(ORDER):
        at = pl.multiple_of((lax.axis_index("mp") + k) % RING * rows, rows)
        copies.append(pltpu.make_async_copy(pieces[i], out_hbm.at[pl.ds(at, rows), :], sems.at[i]))
        copies[-1].start()
    for copy in copies:
        copy.wait()


def place(pieces):
    rows, width = pieces[0].shape
    return pl.pallas_call(
        place_kernel,
        in_specs=[ANY] * RING,
        out_specs=HBM,
        out_shape=pltpu.HBM((RING * rows, width), BF16),
        scratch_shapes=[pltpu.SemaphoreType.DMA((RING,))],
        compiler_params=params(),
        cost_estimate=cost(0, 4 * RING * rows * width),
        name="place",
    )(*pieces)


def shift(value, axis, k):
    return lax.ppermute(value, axis, [(i, (i + k) % RING) for i in range(RING)])


def gathered(block, axis):
    left, right = lax.optimization_barrier((shift(block, axis, 1), shift(block, axis, 3)))
    return [block, left, right, shift(left, axis, 1)]


def moved(value, k, along, across=False):
    pairs = []
    for core in range(2):
        for z in range(RING):
            for x in range(RING):
                to = {"z": z, "x": x}
                to[along[core]] = (to[along[core]] + k) % RING
                target = (1 - core if across else core, to["z"], to["x"])
                pairs.append(
                    ((core * RING + z) * RING + x, (target[0] * RING + target[1]) * RING + target[2])
                )
    return lax.ppermute(value, ("section", "z", "x"), pairs)


GATHER, REDUCE = "xz", "zx"


def fetched(own, others):
    return [own] + [moved(others[k], k, GATHER) for k in (1, 3, 2)]


def left_loads(lefts, buf, sems, ks):
    block = buf.shape[-1]
    mine = lax.axis_index("mp")
    loads = [[[] for _ in ks] for _ in range(2)]
    for f in range(2):
        for i, k in enumerate(ks):
            for j, (left, distance) in enumerate(zip(lefts, ORDER, strict=True)):
                at = pl.multiple_of((mine + distance) % RING * QUARTER, QUARTER)
                loads[f][i].append(
                    pltpu.make_async_copy(
                        left.at[f, :, :, pl.ds(k * block, block)],
                        buf.at[f, i, :, pl.ds(at, QUARTER), :],
                        sems.at[f, i, j],
                    )
                )
                loads[f][i][-1].start()
    return loads


def left_scratch(block, count):
    return [
        pltpu.VMEM((2, count, RING, TOK, block), BF16),
        pltpu.SemaphoreType.DMA((2, count, RING)),
    ]


def flat(value):
    return value.reshape(RING * TOK, value.shape[-1])


def far_kernel(*refs):
    lefts, pieces = refs[:RING], refs[RING : 2 * RING]
    top_ref, low_ref, rows_ref, other_ref, buf, sems = refs[2 * RING :]
    loads = left_loads(lefts, buf, sems, (2, 0))
    for i, piece in enumerate(pieces):
        rows_ref[i * TOK : (i + 1) * TOK, :] = piece[...]
    half, cols = top_ref.shape[0], top_ref.shape[1] // 2
    for m in range(2):
        at = slice(m * cols, (m + 1) * cols)
        wait_all(loads[m][0])
        block = tn(flat(buf[m, 0]), rows_ref[:, at]).astype(BF16)
        top_ref[:, at] = block[:half]
        low_ref[:, at] = block[half:]
    wait_all(loads[0][1])
    wait_all(loads[1][1])
    other_ref[...] = tn(flat(buf[1, 1]), rows_ref[:, cols:]).astype(BF16)


def far_block(lefts, pieces):
    rows, cols = pieces[0].shape
    block = lefts[0].shape[-1] // RING
    half = jax.ShapeDtypeStruct((block // 2, cols), BF16)
    return pl.pallas_call(
        far_kernel,
        in_specs=[HBM] * RING + [VMEM] * RING,
        out_specs=[VMEM] * 4,
        out_shape=[
            half,
            half,
            jax.ShapeDtypeStruct((RING * rows, cols), BF16),
            jax.ShapeDtypeStruct((block, cols // 2), BF16),
        ],
        scratch_shapes=left_scratch(block, 2),
        compiler_params=params(),
        cost_estimate=cost(3 * RING * rows * block * cols, 8 * RING * rows * cols),
        name="far",
    )(*[in_hbm(left) for left in lefts], *pieces)


def side_kernel(*refs):
    lefts, (rows_ref, from_left, from_right) = refs[:RING], refs[RING : RING + 3]
    rights, to_lefts, buf, sems = refs[RING + 3 : RING + 5], refs[RING + 5 : RING + 7], *refs[RING + 7 :]
    loads = left_loads(lefts, buf, sems, (1, 3))
    half, cols = from_left.shape[0], rights[0].shape[1]
    for m in range(2):
        at = slice(m * cols, (m + 1) * cols)

        def product(i, m=m, at=at):
            wait_all(loads[m][i])
            return tn(flat(buf[m, i]), rows_ref[:, at])

        block = product(0)
        rights[m][:half, :] = (block[:half] + from_left[:, at].astype(F32)).astype(BF16)
        rights[m][half:, :] = block[half:].astype(BF16)
        block = product(1)
        to_lefts[m][:half, :] = block[:half].astype(BF16)
        to_lefts[m][half:, :] = (block[half:] + from_right[:, at].astype(F32)).astype(BF16)


def side_blocks(lefts, rows, from_left, from_right):
    depth, cols = rows.shape
    block = lefts[0].shape[-1] // RING
    shape = jax.ShapeDtypeStruct((block, cols // 2), BF16)
    return pl.pallas_call(
        side_kernel,
        in_specs=[HBM] * RING + [VMEM] * 3,
        out_specs=[VMEM] * 4,
        out_shape=[shape] * 4,
        scratch_shapes=left_scratch(block, 2),
        compiler_params=params(),
        cost_estimate=cost(4 * depth * block * cols, 4 * depth * cols),
        name="side",
    )(*[in_hbm(left) for left in lefts], rows, from_left, from_right)


def middle_kernel(*refs):
    lefts, (rows_ref, own_hbm, out_buf, buf, sems, out_sem) = refs[:RING], refs[RING:]
    loads = left_loads(lefts, buf, sems, (0,))
    wait_all(loads[0][0])
    wait_all(loads[1][0])
    out_buf[...] = tn(flat(buf[0, 0]), rows_ref[:, : out_buf.shape[1]]).astype(BF16)
    put = pltpu.make_async_copy(out_buf, own_hbm, out_sem)
    put.start()
    put.wait()


def middle_block(lefts, rows):
    depth, cols = rows.shape
    block = lefts[0].shape[-1] // RING
    return pl.pallas_call(
        middle_kernel,
        in_specs=[HBM] * RING + [VMEM],
        out_specs=HBM,
        out_shape=pltpu.HBM((block, cols // 2), BF16),
        scratch_shapes=[pltpu.VMEM((block, cols // 2), BF16)]
        + left_scratch(block, 1)
        + [pltpu.SemaphoreType.DMA],
        compiler_params=params(),
        cost_estimate=cost(depth * block * cols, 4 * depth * cols),
        name="middle",
    )(*[in_hbm(left) for left in lefts], rows)


def own_kernel(own_hbm, other_hbm, *refs):
    parts, outs, (base_ref, out_buf, base_sems, out_sems) = refs[:4], refs[4:6], refs[6:]
    gets = [
        pltpu.make_async_copy(base, base_ref.at[m], base_sems.at[m])
        for m, base in enumerate((own_hbm, other_hbm))
    ]
    for get in gets:
        get.start()
    core = lax.axis_index("section")
    chunks = out_sems.shape[1]
    size = out_buf.shape[1] // chunks

    def put(m, c, out):
        at = slice(c * size, (c + 1) * size)
        return pltpu.make_async_copy(out_buf.at[m, at], out.at[at], out_sems.at[m, c])

    def write(m, c):
        @pl.when(core == m)
        def _():
            put(m, c, outs[0]).start()

        @pl.when(core != m)
        def _():
            put(m, c, outs[1]).start()

    for m in range(2):
        gets[m].wait()
        for c in range(chunks):
            at = slice(c * size, (c + 1) * size)
            total_of = base_ref[m, at].astype(F32) + parts[2 * m][at].astype(F32)
            out_buf[m, at] = total_of + parts[2 * m + 1][at].astype(F32)
            write(m, c)
    for m in range(2):
        for c in range(chunks):
            put(m, c, outs[0]).wait()


def own_blocks(own, other, parts):
    block, cols = own.shape
    return pl.pallas_call(
        own_kernel,
        in_specs=[HBM] * 2 + [VMEM] * 4,
        out_specs=[HBM] * 2,
        out_shape=[pltpu.HBM((block, cols), F32)] * 2,
        scratch_shapes=[
            pltpu.VMEM((2, block, cols), BF16),
            pltpu.VMEM((2, block, cols), F32),
            pltpu.SemaphoreType.DMA((2,)),
            pltpu.SemaphoreType.DMA((2, 4)),
        ],
        compiler_params=params(),
        cost_estimate=cost(4 * block * cols, 20 * block * cols),
        name="own",
    )(in_hbm(own), in_hbm(other), *parts)


def per_device(states, gains, proj_a, proj_b, cotangent, src_len, tgt_len, dest):
    weight_a = proj_a[0]
    weight_b = proj_b[0]
    rows = states[0]
    keep, send, mine, other = forward(rows, gains, cotangent, weight_a, weight_b)
    swap = [(0, 1), (1, 0)]
    got = lax.ppermute(send, "section", swap)
    slots, slices = pack(keep, got, src_len, dest, mine, lax.ppermute(other, "section", swap))
    width = slots.shape[1]
    slots = slots.reshape(SEQ_DEV, MAXLEN, width)
    slots = lax.all_to_all(slots, ("z", "x"), split_axis=0, concat_axis=0, tiled=True)
    slots = slots.reshape(SLOTS, width)
    pieces = fetched(slices[0], {1: slices[1], 3: slices[2], 2: slices[3]})
    front, back = attend(keep, got, slots, src_len, tgt_len, dest)
    back, pieces = lax.optimization_barrier((back, pieces))
    lefts = gathered(stacked(pieces), "mp")
    back = back.reshape(SEQ_DEV, MAXLEN, width)
    back = lax.all_to_all(back, ("z", "x"), split_axis=0, concat_axis=0, tiled=True)
    keep, send = unpack(back.reshape(SLOTS, width), front, src_len, dest)
    got = lax.ppermute(send, "section", swap)
    kind, others = join(keep, got)

    rights = fetched(kind, {k: kind for k in (1, 2, 3)})
    others = lax.ppermute(others, "section", swap)
    others, lefts[1], lefts[2] = lax.optimization_barrier((others, lefts[1], lefts[2]))
    partial = dnorm_partial(kind, others, weight_a, weight_b)
    partial, rights[1], rights[2] = lax.optimization_barrier((partial, rights[1], rights[2]))
    parts = lax.all_to_all(
        partial.reshape(RING, TOK // RING, -1), "mp", split_axis=0, concat_axis=0, tiled=True
    )
    top, low, stack, own_other = far_block(lefts, rights)
    from_left, from_right = moved(top, 1, REDUCE), moved(low, 3, REDUCE)
    own = middle_block(lefts, stack)
    crossed = lax.ppermute(own_other, "section", swap)
    stack, own, crossed = lax.optimization_barrier((stack, own, crossed))
    right, right_other, left, left_other = side_blocks(lefts, stack, from_left, from_right)
    left_other, parts = lax.optimization_barrier((left_other, parts))
    sums = [
        moved(right, 1, REDUCE),
        moved(left, 3, REDUCE),
        moved(right_other, 1, REDUCE, True),
        moved(left_other, 3, REDUCE, True),
    ]
    quarter = rms_back(rows, gains, parts)
    quarters = gathered(quarter, "mp")
    grad_a, grad_b = own_blocks(own, crossed, sums)
    quarters[3], grad_a = lax.optimization_barrier((quarters[3], grad_a))
    grad_states = place(quarters)
    return (grad_states[None], grad_a[None], grad_b[None])


def solution(mesh):
    split = jax.sharding.Mesh(mesh.devices.reshape(2, RING, RING, RING), ("section", "z", "x", "mp"))
    dp = ("z", "x")
    return jax.shard_map(
        per_device,
        mesh=split,
        in_specs=(
            P("section", dp, None),
            P("section", None),
            P("section", None, "mp"),
            P("section", None, "mp"),
            P(dp, None),
            P(),
            P(),
            P(),
        ),
        out_specs=(P("section", dp, None), P("section", dp, "mp"), P("section", dp, "mp")),
        check_vma=False,
    )
```

```python
import jax
import jax.numpy as jnp
from jax import lax
from jax.experimental import pallas as pl
from jax.experimental.pallas import tpu as pltpu
from jax.sharding import PartitionSpec as P

HEAD_DIM = 64
SEQ_DEV = 16
MAXLEN = 16
TOK = 128
SLOTS = 256
RING = 4
QUARTER = TOK // RING
ORDER = (0, 3, 1, 2)
EPS = 1e-06
SHARE = 16
F32 = jnp.float32
BF16 = jnp.bfloat16
VMEM = pl.BlockSpec(memory_space=pltpu.VMEM)
ANY = pl.BlockSpec(memory_space=pl.ANY)
HBM = pl.BlockSpec(memory_space=pltpu.HBM)


def iota(shape, dim):
    return lax.broadcasted_iota(jnp.int32, shape, dim)


def total(value, axis):
    return jnp.sum(value.astype(F32), axis=axis, keepdims=True)


def tn(left, right):
    return lax.dot_general(left, right, (((0,), (0,)), ((), ())), preferred_element_type=F32)


def in_hbm(value):
    return pltpu.with_memory_space_constraint(value, pltpu.HBM)


def cost(flops, nbytes):
    return pl.CostEstimate(flops=flops // SHARE, bytes_accessed=nbytes // SHARE, transcendentals=0)


def params(mib=12, **more):
    return pltpu.CompilerParams(vmem_limit_bytes=mib << 20, **more)


def column_of(row):
    square = jnp.broadcast_to(row, (SEQ_DEV, SEQ_DEV))
    same = iota((SEQ_DEV, SEQ_DEV), 0) == iota((SEQ_DEV, SEQ_DEV), 1)
    return total(jnp.where(same, square, 0), 1)


def member_index():
    return lax.axis_index("z") * RING + lax.axis_index("x")


def slot_onehot(member, src_len, dest):
    i, j = iota((SEQ_DEV, SEQ_DEV), 0), iota((SEQ_DEV, SEQ_DEV), 1)
    lengths = src_len[pl.ds(member, 1), :]
    ends = total(jnp.where(j <= i, jnp.broadcast_to(lengths, (SEQ_DEV, SEQ_DEV)), 0), 1)
    begins = ends - column_of(lengths)
    place = column_of(dest[pl.ds(member, 1), :] >> 4) * MAXLEN
    row = iota((SEQ_DEV, TOK), 1).astype(F32)
    inside = (row >= begins) & (row < ends)
    target = total(jnp.where(inside, place + row - begins, 0.0), 0)
    hit = iota((SLOTS, TOK), 0).astype(F32) == target
    return jnp.where(hit, 1.0, 0.0).astype(BF16)


def pair_mask(member, src_len, tgt_len, dest):
    i, j = iota((SEQ_DEV, SEQ_DEV), 0), iota((SEQ_DEV, SEQ_DEV), 1)
    column = column_of(tgt_len[pl.ds(member, 1), :])
    ends = total(jnp.where(i <= j, jnp.broadcast_to(column, (SEQ_DEV, SEQ_DEV)), 0.0), 0)
    row = iota((TOK, SEQ_DEV), 0).astype(F32)
    mine = total(jnp.where(row >= ends, 1.0, 0.0), 1)
    codes = dest[...]
    to_me = (codes >> 4) == member
    target = total(jnp.where(to_me, codes & 15, 0), 1)
    length = total(jnp.where(to_me, src_len[...], 0), 1)
    lane = iota((SEQ_DEV, SLOTS), 1)
    own = (lane >> 4) == iota((SEQ_DEV, SLOTS), 0)
    target = total(jnp.where(own, target, 0.0), 0)
    length = total(jnp.where(own, length, 0.0), 0)
    step = (iota((1, SLOTS), 1) & 15).astype(F32)
    target = jnp.where(step < length, target, -1.0)
    return mine == target


def forward_kernel(
    x_hbm, gain_hbm, cot_hbm, a_hbm, b_hbm, keep_ref, send_ref, *rest
):
    mine_ref, other_ref = rest[:2]
    x_ref, gain_ref, a_buf, b_buf, normed_ref, left_ref, in_sem, a_sem, b_sem, out_sem = rest[2:]
    count, step, cols = a_buf.shape
    core = lax.axis_index("section")
    get_x = pltpu.make_async_copy(x_hbm, x_ref, in_sem.at[0])
    get_gain = pltpu.make_async_copy(gain_hbm, gain_ref, in_sem.at[1])
    get_left = pltpu.make_async_copy(cot_hbm, left_ref, in_sem.at[2])
    get_x.start()
    get_gain.start()

    def fetch(k):
        rows = pl.ds(k * step, step)
        return (
            pltpu.make_async_copy(a_hbm.at[rows, :], a_buf.at[k], a_sem.at[k]),
            pltpu.make_async_copy(b_hbm.at[rows, :], b_buf.at[k], b_sem.at[k]),
        )

    for k in range(count):
        copy_a, copy_b = fetch(k)
        copy_a.start()
        if k == 0:

            @pl.when(core != 0)
            def _():
                get_left.start()

        copy_b.start()
    get_x.wait()
    get_gain.wait()
    xf = x_ref[...].astype(F32)
    scale = lax.rsqrt(jnp.mean(xf * xf, axis=-1, keepdims=True) + EPS)
    normed_ref[...] = (xf * scale * gain_ref[...]).astype(BF16)

    def product(ref, k, buf):
        return jnp.dot(ref[:, k * step : (k + 1) * step], buf[k], preferred_element_type=F32)

    fetch(0)[0].wait()
    acc_a = product(normed_ref, 0, a_buf)

    @pl.when(core == 0)
    def _():
        left_ref[...] = normed_ref[...]

    @pl.when(core != 0)
    def _():
        get_left.wait()

    fetch(0)[1].wait()
    acc_b = product(left_ref, 0, b_buf)
    z, x = lax.axis_index("z"), lax.axis_index("x")
    quarter = pl.ds(pl.multiple_of(lax.axis_index("mp") * QUARTER, QUARTER), QUARTER)
    block = cols // RING
    copies = []
    for k in range(RING):
        for j in range(RING):
            to = slice(j * block, (j + 1) * block)
            at_x = ((z + j) % RING * RING + (x + k) % RING) * block
            at_z = ((z + k) % RING * RING + (x + j) % RING) * block
            at_mine = jnp.where(core == 0, at_x, at_z)
            at_other = jnp.where(core == 0, at_z, at_x)
            for source, at, out in ((left_ref, at_mine, mine_ref), (normed_ref, at_other, other_ref)):
                copies.append(
                    pltpu.make_async_copy(
                        source.at[quarter, pl.ds(pl.multiple_of(at, block), block)],
                        out.at[k, :, to],
                        out_sem.at[len(copies)],
                    )
                )
                copies[-1].start()

    for k in range(1, count):
        for copy in fetch(k):
            copy.wait()
        acc_a += product(normed_ref, k, a_buf)
        acc_b += product(left_ref, k, b_buf)
    half = cols // 2
    parts = [[acc[:, i * half : (i + 1) * half].astype(BF16) for acc in (acc_a, acc_b)] for i in range(2)]

    def put(ref, pieces):
        ref[:, :half] = pieces[0]
        ref[:, half:] = pieces[1]

    @pl.when(core == 0)
    def _():
        put(keep_ref, parts[0])
        put(send_ref, parts[1])

    @pl.when(core != 0)
    def _():
        put(keep_ref, parts[1])
        put(send_ref, parts[0])

    for copy in copies:
        copy.wait()


def forward(x, gain, cot, weight_a, weight_b):
    rows, width = x.shape
    cols = weight_a.shape[1]
    step = 512
    count = width // step
    half = jax.ShapeDtypeStruct((rows, cols), BF16)
    return pl.pallas_call(
        forward_kernel,
        in_specs=[HBM] * 5,
        out_specs=[VMEM] * 4,
        out_shape=[half] * 2 + [jax.ShapeDtypeStruct((RING, QUARTER, cols), BF16)] * 2,
        scratch_shapes=[pltpu.VMEM((rows, width), BF16), pltpu.VMEM((1, width), F32)]
        + [pltpu.VMEM((count, step, cols), BF16)] * 2
        + [pltpu.VMEM((rows, width), BF16)] * 2
        + [pltpu.SemaphoreType.DMA((3,))]
        + [pltpu.SemaphoreType.DMA((count,))] * 2
        + [pltpu.SemaphoreType.DMA((2 * RING * RING,))],
        compiler_params=params(32),
        cost_estimate=cost(4 * rows * width * cols, 4 * width * cols),
        name="forward",
    )(in_hbm(x), in_hbm(gain), in_hbm(cot), in_hbm(weight_a), in_hbm(weight_b))


def wait_all(copies):
    for copy in copies:
        copy.wait()


def pack_kernel(keep_ref, got_ref, src_ref, dest_ref, mine_ref, other_ref, out_ref, *rest):
    for out, k in zip(rest, (0, 1, 3, 2), strict=True):
        out[0] = mine_ref[k]
        out[1] = other_ref[k]
    spread = slot_onehot(member_index(), src_ref, dest_ref)

    @pl.when(lax.axis_index("section") == 0)
    def _():
        out_ref[...] = jnp.dot(spread, keep_ref[...], preferred_element_type=F32).astype(BF16)

    @pl.when(lax.axis_index("section") != 0)
    def _():
        out_ref[...] = jnp.dot(spread, got_ref[...], preferred_element_type=F32).astype(BF16)


def pack(keep, got, src_len, dest, mine, other):
    width = keep.shape[1]
    _, rows, cols = mine.shape
    outs = pl.pallas_call(
        pack_kernel,
        in_specs=[VMEM] * 6,
        out_specs=[VMEM] * (1 + RING),
        out_shape=[jax.ShapeDtypeStruct((SLOTS, width), BF16)]
        + [jax.ShapeDtypeStruct((2, rows, cols), BF16)] * RING,
        compiler_params=params(),
        cost_estimate=cost(2 * SLOTS * TOK * width, 2 * SLOTS * width),
        name="pack",
    )(keep, got, src_len, dest, mine, other)
    return outs[0], outs[1:]


def attend_kernel(
    keep_ref, got_ref, slots_ref, src_ref, tgt_ref, dest_ref, front_ref, back_ref, own_ref
):
    mask = pair_mask(member_index(), src_ref, tgt_ref, dest_ref)

    @pl.when(lax.axis_index("section") == 0)
    def _():
        own_ref[...] = got_ref[...]

    @pl.when(lax.axis_index("section") != 0)
    def _():
        own_ref[...] = keep_ref[...]

    half = own_ref.shape[1] // 2
    pair = 2 * HEAD_DIM
    low = iota((1, pair), 1) < HEAD_DIM
    nothing = jnp.zeros((), BF16)

    def both(value):
        return jnp.concatenate(
            [jnp.where(low, value, nothing), jnp.where(low, nothing, value)], axis=0
        )

    def nt(left, right):
        return lax.dot_general(left, right, (((1,), (1,)), ((), ())), preferred_element_type=F32)

    def one(score, dweight):
        expo = jnp.where(mask, jnp.exp(score), 0.0)
        weight = expo * (1.0 / jnp.sum(expo, axis=-1, keepdims=True))
        mean = jnp.sum(weight * dweight, axis=-1, keepdims=True)
        return weight.astype(BF16), (weight * (dweight - mean)).astype(BF16)

    def fold(value):
        return jnp.where(low, value[:SLOTS], value[SLOTS:]).astype(BF16)

    for p in range(half // pair):
        first = slice(p * pair, (p + 1) * pair)
        second = slice(half + p * pair, half + (p + 1) * pair)
        query, dout = own_ref[:, first], own_ref[:, second]
        keys, values = both(slots_ref[:, first]), both(slots_ref[:, second])
        score, dweight = nt(query, keys), nt(dout, values)
        weight_0, dscore_0 = one(score[:, :SLOTS], dweight[:, :SLOTS])
        weight_1, dscore_1 = one(score[:, SLOTS:], dweight[:, SLOTS:])
        weight = jnp.concatenate([weight_0, weight_1], axis=1)
        dscore = jnp.concatenate([dscore_0, dscore_1], axis=1)
        front_ref[:, first] = jnp.dot(dscore, keys, preferred_element_type=F32).astype(BF16)
        front_ref[:, second] = jnp.dot(weight, values, preferred_element_type=F32).astype(BF16)
        back_ref[:, first] = fold(tn(dscore, query))
        back_ref[:, second] = fold(tn(weight, dout))


def attend(keep, got, slots, src_len, tgt_len, dest):
    rows, width = keep.shape
    return pl.pallas_call(
        attend_kernel,
        in_specs=[VMEM] * 6,
        out_specs=[VMEM] * 2,
        out_shape=[
            jax.ShapeDtypeStruct((rows, width), BF16),
            jax.ShapeDtypeStruct((SLOTS, width), BF16),
        ],
        scratch_shapes=[pltpu.VMEM((rows, width), BF16)],
        compiler_params=params(),
        cost_estimate=cost(24 * rows * SLOTS * width, 8 * SLOTS * width),
        name="attend",
    )(keep, got, slots, src_len, tgt_len, dest)


def stack_kernel(*refs):
    for p in range(RING):
        for m in range(2):
            refs[RING][m, p] = refs[p][m]


def stacked(pieces):
    _, quarter, cols = pieces[0].shape
    return pl.pallas_call(
        stack_kernel,
        in_specs=[VMEM] * RING,
        out_specs=VMEM,
        out_shape=jax.ShapeDtypeStruct((2, RING, quarter, cols), BF16),
        compiler_params=params(),
        cost_estimate=cost(0, 4 * RING * pieces[0].size),
        name="stack",
    )(*pieces)


def unpack_kernel(back_ref, front_ref, src_ref, dest_ref, keep_ref, send_ref):
    spread = slot_onehot(member_index(), src_ref, dest_ref)
    rows = tn(spread, back_ref[...]).astype(BF16)
    half = rows.shape[1] // 2
    core = lax.axis_index("section")

    @pl.when(core == 0)
    def _():
        keep_ref[:, :half] = rows[:, :half]
        keep_ref[:, half:] = front_ref[:, :half]
        send_ref[:, :half] = front_ref[:, half:]
        send_ref[:, half:] = rows[:, half:]

    @pl.when(core != 0)
    def _():
        keep_ref[:, :half] = front_ref[:, half:]
        keep_ref[:, half:] = rows[:, half:]
        send_ref[:, :half] = rows[:, :half]
        send_ref[:, half:] = front_ref[:, :half]


def unpack(back, front, src_len, dest):
    width = front.shape[1]
    half = jax.ShapeDtypeStruct((TOK, width), BF16)
    return pl.pallas_call(
        unpack_kernel,
        in_specs=[VMEM] * 4,
        out_specs=[VMEM] * 2,
        out_shape=[half, half],
        compiler_params=params(),
        cost_estimate=cost(2 * SLOTS * TOK * width, 4 * SLOTS * width),
        name="unpack",
    )(back, front, src_len, dest)


def join_kernel(keep_ref, got_ref, rows_ref, other_ref):
    width = keep_ref.shape[1]
    half = width // 2
    core = lax.axis_index("section")
    mine = pl.multiple_of(core * half, half)
    theirs = pl.multiple_of((1 - core) * half, half)
    for ref, at in ((keep_ref, mine), (got_ref, theirs)):
        rows_ref[:, pl.ds(at, half)] = ref[:, :half]
        rows_ref[:, pl.ds(pl.multiple_of(width + at, half), half)] = ref[:, half:]
        other_ref[:, pl.ds(at, half)] = ref[:, half:]


def join(keep, got):
    rows, width = keep.shape
    return pl.pallas_call(
        join_kernel,
        in_specs=[VMEM, VMEM],
        out_specs=[VMEM] * 2,
        out_shape=[
            jax.ShapeDtypeStruct((rows, 2 * width), BF16),
            jax.ShapeDtypeStruct((rows, width), BF16),
        ],
        compiler_params=params(),
        cost_estimate=cost(0, 8 * keep.size),
        name="join",
    )(keep, got)


def dnorm_kernel(rows_ref, got_ref, a_hbm, b_hbm, out_hbm, a_buf, b_buf, out_buf, a_sem, b_sem, out_sem):
    count, step, cols = a_buf.shape
    core = lax.axis_index("section")

    def nt(left, right):
        return lax.dot_general(left, right, (((1,), (1,)), ((), ())), preferred_element_type=F32)

    def fetches(hbm, buf, sem):
        return [
            pltpu.make_async_copy(hbm.at[pl.ds(k * step, step), :], buf.at[k], sem.at[k])
            for k in range(count)
        ]

    get_a, get_b = fetches(a_hbm, a_buf, a_sem), fetches(b_hbm, b_buf, b_sem)

    def put(k):
        at = slice(k * step, (k + 1) * step)
        return pltpu.make_async_copy(out_buf.at[:, at], out_hbm.at[:, at], out_sem.at[k])

    @pl.when(core == 0)
    def _():
        for k in range(count):
            get_a[k].start()
            get_b[k].start()
        for k in range(count):
            get_a[k].wait()
            get_b[k].wait()
            block = nt(rows_ref[:, :cols], a_buf[k]) + nt(got_ref[...], b_buf[k])
            out_buf[:, k * step : (k + 1) * step] = block.astype(BF16)
            put(k).start()

    @pl.when(core != 0)
    def _():
        for k in range(count):
            get_a[k].start()
        for k in range(count):
            get_a[k].wait()
            out_buf[:, k * step : (k + 1) * step] = nt(got_ref[...], a_buf[k]).astype(BF16)
            put(k).start()

    for k in range(count):
        put(k).wait()


def dnorm_partial(rows, got, weight_a, weight_b):
    width, cols = weight_a.shape
    step = 512
    count = width // step
    return pl.pallas_call(
        dnorm_kernel,
        in_specs=[VMEM] * 2 + [HBM] * 2,
        out_specs=HBM,
        out_shape=pltpu.HBM((TOK, width), BF16),
        scratch_shapes=[pltpu.VMEM((count, step, cols), BF16)] * 2
        + [pltpu.VMEM((TOK, width), BF16)]
        + [pltpu.SemaphoreType.DMA((count,))] * 3,
        compiler_params=params(24),
        cost_estimate=cost(4 * TOK * width * cols, 4 * width * cols),
        name="dnorm",
    )(rows, got, in_hbm(weight_a), in_hbm(weight_b))


def rms_back_kernel(x_hbm, gain_ref, parts_ref, out_ref, x_ref, sem):
    rows = out_ref.shape[0]
    mine = pl.multiple_of(lax.axis_index("mp") * rows, rows)
    get_x = pltpu.make_async_copy(x_hbm.at[pl.ds(mine, rows), :], x_ref, sem)
    get_x.start()
    dnorm = parts_ref[0].astype(F32)
    for i in range(1, RING):
        dnorm += parts_ref[i].astype(F32)
    get_x.wait()
    xf = x_ref[...].astype(F32)
    scale = lax.rsqrt(jnp.mean(xf * xf, axis=-1, keepdims=True) + EPS)
    upper = gain_ref[...] * dnorm
    inner = jnp.mean(xf * upper, axis=-1, keepdims=True)
    out_ref[...] = (scale * upper - xf * (scale * scale * scale * inner)).astype(BF16)


def rms_back(x, gain, parts):
    rows, width = parts.shape[1:]
    return pl.pallas_call(
        rms_back_kernel,
        in_specs=[HBM] + [VMEM] * 2,
        out_specs=VMEM,
        out_shape=jax.ShapeDtypeStruct((rows, width), BF16),
        scratch_shapes=[pltpu.VMEM((rows, width), BF16), pltpu.SemaphoreType.DMA],
        compiler_params=params(),
        cost_estimate=cost(10 * rows * width, 12 * rows * width),
        name="rms_back",
    )(in_hbm(x), gain, parts)


def shift(value, axis, k):
    return lax.ppermute(value, axis, [(i, (i + k) % RING) for i in range(RING)])


def gathered(block, axis):
    left, right = lax.optimization_barrier((shift(block, axis, 1), shift(block, axis, 3)))
    return [block, left, right, shift(left, axis, 1)]


def moved(value, k, along, across=False):
    pairs = []
    for core in range(2):
        for z in range(RING):
            for x in range(RING):
                to = {"z": z, "x": x}
                to[along[core]] = (to[along[core]] + k) % RING
                target = (1 - core if across else core, to["z"], to["x"])
                pairs.append(
                    ((core * RING + z) * RING + x, (target[0] * RING + target[1]) * RING + target[2])
                )
    return lax.ppermute(value, ("section", "z", "x"), pairs)


GATHER, REDUCE = "xz", "zx"


def fetched(own, others):
    return [own] + [moved(others[k], k, GATHER) for k in (1, 3, 2)]


def left_loads(lefts, buf, sems, ks):
    block = buf.shape[-1]
    mine = lax.axis_index("mp")
    loads = [[[] for _ in ks] for _ in range(2)]
    for f in range(2):
        for i, k in enumerate(ks):
            for j, (left, distance) in enumerate(zip(lefts, ORDER, strict=True)):
                at = pl.multiple_of((mine + distance) % RING * QUARTER, QUARTER)
                loads[f][i].append(
                    pltpu.make_async_copy(
                        left.at[f, :, :, pl.ds(k * block, block)],
                        buf.at[f, i, :, pl.ds(at, QUARTER), :],
                        sems.at[f, i, j],
                    )
                )
                loads[f][i][-1].start()
    return loads


def left_scratch(block, count):
    return [
        pltpu.VMEM((2, count, RING, TOK, block), BF16),
        pltpu.SemaphoreType.DMA((2, count, RING)),
    ]


def flat(value):
    return value.reshape(RING * TOK, value.shape[-1])


def far_kernel(*refs):
    lefts, pieces = refs[:RING], refs[RING : 2 * RING]
    top_ref, low_ref, rows_ref, other_ref, buf, sems = refs[2 * RING :]
    loads = left_loads(lefts, buf, sems, (2, 0))
    for i, piece in enumerate(pieces):
        rows_ref[i * TOK : (i + 1) * TOK, :] = piece[...]
    half, cols = top_ref.shape[0], top_ref.shape[1] // 2
    for m in range(2):
        at = slice(m * cols, (m + 1) * cols)
        wait_all(loads[m][0])
        block = tn(flat(buf[m, 0]), rows_ref[:, at]).astype(BF16)
        top_ref[:, at] = block[:half]
        low_ref[:, at] = block[half:]
    wait_all(loads[0][1])
    wait_all(loads[1][1])
    other_ref[...] = tn(flat(buf[1, 1]), rows_ref[:, cols:]).astype(BF16)


def far_block(lefts, pieces):
    rows, cols = pieces[0].shape
    block = lefts[0].shape[-1] // RING
    half = jax.ShapeDtypeStruct((block // 2, cols), BF16)
    return pl.pallas_call(
        far_kernel,
        in_specs=[HBM] * RING + [VMEM] * RING,
        out_specs=[VMEM] * 4,
        out_shape=[
            half,
            half,
            jax.ShapeDtypeStruct((RING * rows, cols), BF16),
            jax.ShapeDtypeStruct((block, cols // 2), BF16),
        ],
        scratch_shapes=left_scratch(block, 2),
        compiler_params=params(),
        cost_estimate=cost(3 * RING * rows * block * cols, 8 * RING * rows * cols),
        name="far",
    )(*[in_hbm(left) for left in lefts], *pieces)


def side_kernel(*refs):
    lefts, (rows_ref, from_left, from_right) = refs[:RING], refs[RING : RING + 3]
    rights, to_lefts, buf, sems = refs[RING + 3 : RING + 5], refs[RING + 5 : RING + 7], *refs[RING + 7 :]
    loads = left_loads(lefts, buf, sems, (1, 3))
    half, cols = from_left.shape[0], rights[0].shape[1]
    for m in range(2):
        at = slice(m * cols, (m + 1) * cols)

        def product(i, m=m, at=at):
            wait_all(loads[m][i])
            return tn(flat(buf[m, i]), rows_ref[:, at])

        block = product(0)
        rights[m][:half, :] = (block[:half] + from_left[:, at].astype(F32)).astype(BF16)
        rights[m][half:, :] = block[half:].astype(BF16)
        block = product(1)
        to_lefts[m][:half, :] = block[:half].astype(BF16)
        to_lefts[m][half:, :] = (block[half:] + from_right[:, at].astype(F32)).astype(BF16)


def side_blocks(lefts, rows, from_left, from_right):
    depth, cols = rows.shape
    block = lefts[0].shape[-1] // RING
    shape = jax.ShapeDtypeStruct((block, cols // 2), BF16)
    return pl.pallas_call(
        side_kernel,
        in_specs=[HBM] * RING + [VMEM] * 3,
        out_specs=[VMEM] * 4,
        out_shape=[shape] * 4,
        scratch_shapes=left_scratch(block, 2),
        compiler_params=params(),
        cost_estimate=cost(4 * depth * block * cols, 4 * depth * cols),
        name="side",
    )(*[in_hbm(left) for left in lefts], rows, from_left, from_right)


def middle_kernel(*refs):
    lefts, (rows_ref, own_hbm, out_buf, buf, sems, out_sem) = refs[:RING], refs[RING:]
    loads = left_loads(lefts, buf, sems, (0,))
    wait_all(loads[0][0])
    wait_all(loads[1][0])
    out_buf[...] = tn(flat(buf[0, 0]), rows_ref[:, : out_buf.shape[1]]).astype(BF16)
    put = pltpu.make_async_copy(out_buf, own_hbm, out_sem)
    put.start()
    put.wait()


def middle_block(lefts, rows):
    depth, cols = rows.shape
    block = lefts[0].shape[-1] // RING
    return pl.pallas_call(
        middle_kernel,
        in_specs=[HBM] * RING + [VMEM],
        out_specs=HBM,
        out_shape=pltpu.HBM((block, cols // 2), BF16),
        scratch_shapes=[pltpu.VMEM((block, cols // 2), BF16)]
        + left_scratch(block, 1)
        + [pltpu.SemaphoreType.DMA],
        compiler_params=params(),
        cost_estimate=cost(depth * block * cols, 4 * depth * cols),
        name="middle",
    )(*[in_hbm(left) for left in lefts], rows)


def own_kernel(own_hbm, other_hbm, *refs):
    parts, quarters, outs, states_hbm = refs[:4], refs[4 : 4 + RING], refs[4 + RING : 6 + RING], refs[6 + RING]
    base_ref, out_buf, base_sems, out_sems, quarter_sems = refs[7 + RING :]
    gets = [
        pltpu.make_async_copy(base, base_ref.at[m], base_sems.at[m])
        for m, base in enumerate((own_hbm, other_hbm))
    ]
    for get in gets:
        get.start()
    rows = quarters[0].shape[0]
    places = []
    for i, k in enumerate(ORDER):
        at = pl.multiple_of((lax.axis_index("mp") + k) % RING * rows, rows)
        places.append(
            pltpu.make_async_copy(quarters[i], states_hbm.at[pl.ds(at, rows), :], quarter_sems.at[i])
        )
        places[-1].start()
    core = lax.axis_index("section")
    chunks = out_sems.shape[1]
    size = out_buf.shape[1] // chunks

    def put(m, c, out):
        at = slice(c * size, (c + 1) * size)
        return pltpu.make_async_copy(out_buf.at[m, at], out.at[at], out_sems.at[m, c])

    def write(m, c):
        @pl.when(core == m)
        def _():
            put(m, c, outs[0]).start()

        @pl.when(core != m)
        def _():
            put(m, c, outs[1]).start()

    for m in range(2):
        gets[m].wait()
        for c in range(chunks):
            at = slice(c * size, (c + 1) * size)
            total_of = base_ref[m, at].astype(F32) + parts[2 * m][at].astype(F32)
            out_buf[m, at] = total_of + parts[2 * m + 1][at].astype(F32)
            write(m, c)
    wait_all(places)
    for m in range(2):
        for c in range(chunks):
            put(m, c, outs[0]).wait()


def own_blocks(own, other, parts, quarters):
    block, cols = own.shape
    rows, width = quarters[0].shape
    return pl.pallas_call(
        own_kernel,
        in_specs=[HBM] * 2 + [VMEM] * 4 + [ANY] * RING,
        out_specs=[HBM] * 3,
        out_shape=[pltpu.HBM((block, cols), F32)] * 2 + [pltpu.HBM((RING * rows, width), BF16)],
        scratch_shapes=[
            pltpu.VMEM((2, block, cols), BF16),
            pltpu.VMEM((2, block, cols), F32),
            pltpu.SemaphoreType.DMA((2,)),
            pltpu.SemaphoreType.DMA((2, 4)),
            pltpu.SemaphoreType.DMA((RING,)),
        ],
        compiler_params=params(),
        cost_estimate=cost(4 * block * cols, 28 * block * cols),
        name="own",
    )(in_hbm(own), in_hbm(other), *parts, *quarters)


def per_device(states, gains, proj_a, proj_b, cotangent, src_len, tgt_len, dest):
    weight_a = proj_a[0]
    weight_b = proj_b[0]
    rows = states[0]
    keep, send, mine, other = forward(rows, gains, cotangent, weight_a, weight_b)
    swap = [(0, 1), (1, 0)]
    got = lax.ppermute(send, "section", swap)
    slots, slices = pack(keep, got, src_len, dest, mine, lax.ppermute(other, "section", swap))
    width = slots.shape[1]
    slots = slots.reshape(SEQ_DEV, MAXLEN, width)
    slots = lax.all_to_all(slots, ("z", "x"), split_axis=0, concat_axis=0, tiled=True)
    slots = slots.reshape(SLOTS, width)
    pieces = fetched(slices[0], {1: slices[1], 3: slices[2], 2: slices[3]})
    front, back = attend(keep, got, slots, src_len, tgt_len, dest)
    back, pieces = lax.optimization_barrier((back, pieces))
    lefts = gathered(stacked(pieces), "mp")
    back = back.reshape(SEQ_DEV, MAXLEN, width)
    back = lax.all_to_all(back, ("z", "x"), split_axis=0, concat_axis=0, tiled=True)
    keep, send = unpack(back.reshape(SLOTS, width), front, src_len, dest)
    got = lax.ppermute(send, "section", swap)
    kind, others = join(keep, got)

    rights = fetched(kind, {k: kind for k in (1, 2, 3)})
    others = lax.ppermute(others, "section", swap)
    others, lefts[1], lefts[2] = lax.optimization_barrier((others, lefts[1], lefts[2]))
    partial = dnorm_partial(kind, others, weight_a, weight_b)
    partial, rights[1], rights[2] = lax.optimization_barrier((partial, rights[1], rights[2]))
    parts = lax.all_to_all(
        partial.reshape(RING, TOK // RING, -1), "mp", split_axis=0, concat_axis=0, tiled=True
    )
    top, low, stack, own_other = far_block(lefts, rights)
    from_left, from_right = moved(top, 1, REDUCE), moved(low, 3, REDUCE)
    own = middle_block(lefts, stack)
    crossed = lax.ppermute(own_other, "section", swap)
    stack, own, crossed = lax.optimization_barrier((stack, own, crossed))
    right, right_other, left, left_other = side_blocks(lefts, stack, from_left, from_right)
    left_other, parts = lax.optimization_barrier((left_other, parts))
    sums = [
        moved(right, 1, REDUCE),
        moved(left, 3, REDUCE),
        moved(right_other, 1, REDUCE, True),
        moved(left_other, 3, REDUCE, True),
    ]
    quarter = rms_back(rows, gains, parts)
    before, after = shift(quarter, "mp", 1), shift(quarter, "mp", 3)
    quarters = [quarter, before, after, shift(after, "mp", 3)]
    grad_a, grad_b, grad_states = own_blocks(own, crossed, sums, quarters)
    return (grad_states[None], grad_a[None], grad_b[None])


def solution(mesh):
    split = jax.sharding.Mesh(mesh.devices.reshape(2, RING, RING, RING), ("section", "z", "x", "mp"))
    dp = ("z", "x")
    return jax.shard_map(
        per_device,
        mesh=split,
        in_specs=(
            P("section", dp, None),
            P("section", None),
            P("section", None, "mp"),
            P("section", None, "mp"),
            P(dp, None),
            P(),
            P(),
            P(),
        ),
        out_specs=(P("section", dp, None), P("section", dp, "mp"), P("section", dp, "mp")),
        check_vma=False,
    )
```

```python
import jax
import jax.numpy as jnp
from jax import lax
from jax.experimental import pallas as pl
from jax.experimental.pallas import tpu as pltpu
from jax.sharding import PartitionSpec as P

HEAD_DIM = 64
SEQ_DEV = 16
MAXLEN = 16
TOK = 128
SLOTS = 256
RING = 4
QUARTER = TOK // RING
ORDER = (0, 3, 1, 2)
EPS = 1e-06
SHARE = 16
F32 = jnp.float32
BF16 = jnp.bfloat16
VMEM = pl.BlockSpec(memory_space=pltpu.VMEM)
ANY = pl.BlockSpec(memory_space=pl.ANY)
HBM = pl.BlockSpec(memory_space=pltpu.HBM)


def iota(shape, dim):
    return lax.broadcasted_iota(jnp.int32, shape, dim)


def total(value, axis):
    return jnp.sum(value.astype(F32), axis=axis, keepdims=True)


def tn(left, right):
    return lax.dot_general(left, right, (((0,), (0,)), ((), ())), preferred_element_type=F32)


def in_hbm(value):
    return pltpu.with_memory_space_constraint(value, pltpu.HBM)


def cost(flops, nbytes):
    return pl.CostEstimate(flops=flops // SHARE, bytes_accessed=nbytes // SHARE, transcendentals=0)


def params(mib=12, **more):
    return pltpu.CompilerParams(vmem_limit_bytes=mib << 20, **more)


def column_of(row):
    square = jnp.broadcast_to(row, (SEQ_DEV, SEQ_DEV))
    same = iota((SEQ_DEV, SEQ_DEV), 0) == iota((SEQ_DEV, SEQ_DEV), 1)
    return total(jnp.where(same, square, 0), 1)


def member_index():
    return lax.axis_index("z") * RING + lax.axis_index("x")


def slot_onehot(member, src_len, dest):
    i, j = iota((SEQ_DEV, SEQ_DEV), 0), iota((SEQ_DEV, SEQ_DEV), 1)
    lengths = src_len[pl.ds(member, 1), :]
    ends = total(jnp.where(j <= i, jnp.broadcast_to(lengths, (SEQ_DEV, SEQ_DEV)), 0), 1)
    begins = ends - column_of(lengths)
    place = column_of(dest[pl.ds(member, 1), :] >> 4) * MAXLEN
    row = iota((SEQ_DEV, TOK), 1).astype(F32)
    inside = (row >= begins) & (row < ends)
    target = total(jnp.where(inside, place + row - begins, 0.0), 0)
    hit = iota((SLOTS, TOK), 0).astype(F32) == target
    return jnp.where(hit, 1.0, 0.0).astype(BF16)


def pair_mask(member, src_len, tgt_len, dest):
    i, j = iota((SEQ_DEV, SEQ_DEV), 0), iota((SEQ_DEV, SEQ_DEV), 1)
    column = column_of(tgt_len[pl.ds(member, 1), :])
    ends = total(jnp.where(i <= j, jnp.broadcast_to(column, (SEQ_DEV, SEQ_DEV)), 0.0), 0)
    row = iota((TOK, SEQ_DEV), 0).astype(F32)
    mine = total(jnp.where(row >= ends, 1.0, 0.0), 1)
    codes = dest[...]
    to_me = (codes >> 4) == member
    target = total(jnp.where(to_me, codes & 15, 0), 1)
    length = total(jnp.where(to_me, src_len[...], 0), 1)
    lane = iota((SEQ_DEV, SLOTS), 1)
    own = (lane >> 4) == iota((SEQ_DEV, SLOTS), 0)
    target = total(jnp.where(own, target, 0.0), 0)
    length = total(jnp.where(own, length, 0.0), 0)
    step = (iota((1, SLOTS), 1) & 15).astype(F32)
    target = jnp.where(step < length, target, -1.0)
    return mine == target


def forward_kernel(
    x_hbm, gain_hbm, cot_hbm, a_hbm, b_hbm, keep_ref, send_ref, *rest
):
    mine_ref, other_ref = rest[:2]
    x_ref, gain_ref, a_buf, b_buf, normed_ref, left_ref, in_sem, a_sem, b_sem, out_sem = rest[2:]
    count, step, cols = a_buf.shape
    core = lax.axis_index("section")
    get_x = pltpu.make_async_copy(x_hbm, x_ref, in_sem.at[0])
    get_gain = pltpu.make_async_copy(gain_hbm, gain_ref, in_sem.at[1])
    get_left = pltpu.make_async_copy(cot_hbm, left_ref, in_sem.at[2])
    get_x.start()
    get_gain.start()

    def fetch(k):
        rows = pl.ds(k * step, step)
        return (
            pltpu.make_async_copy(a_hbm.at[rows, :], a_buf.at[k], a_sem.at[k]),
            pltpu.make_async_copy(b_hbm.at[rows, :], b_buf.at[k], b_sem.at[k]),
        )

    for k in range(count):
        copy_a, copy_b = fetch(k)
        copy_a.start()
        if k == 0:

            @pl.when(core != 0)
            def _():
                get_left.start()

        copy_b.start()
    get_x.wait()
    get_gain.wait()
    xf = x_ref[...].astype(F32)
    scale = lax.rsqrt(jnp.mean(xf * xf, axis=-1, keepdims=True) + EPS)
    normed_ref[...] = (xf * scale * gain_ref[...]).astype(BF16)

    def product(ref, k, buf):
        return jnp.dot(ref[:, k * step : (k + 1) * step], buf[k], preferred_element_type=F32)

    fetch(0)[0].wait()
    acc_a = product(normed_ref, 0, a_buf)

    @pl.when(core == 0)
    def _():
        left_ref[...] = normed_ref[...]

    @pl.when(core != 0)
    def _():
        get_left.wait()

    fetch(0)[1].wait()
    acc_b = product(left_ref, 0, b_buf)
    z, x = lax.axis_index("z"), lax.axis_index("x")
    quarter = pl.ds(pl.multiple_of(lax.axis_index("mp") * QUARTER, QUARTER), QUARTER)
    block = cols // RING
    copies = []
    for k in range(RING):
        for j in range(RING):
            to = slice(j * block, (j + 1) * block)
            at_x = ((z + j) % RING * RING + (x + k) % RING) * block
            at_z = ((z + k) % RING * RING + (x + j) % RING) * block
            at_mine = jnp.where(core == 0, at_x, at_z)
            at_other = jnp.where(core == 0, at_z, at_x)
            for source, at, out in ((left_ref, at_mine, mine_ref), (normed_ref, at_other, other_ref)):
                copies.append(
                    pltpu.make_async_copy(
                        source.at[quarter, pl.ds(pl.multiple_of(at, block), block)],
                        out.at[k, :, to],
                        out_sem.at[len(copies)],
                    )
                )
                copies[-1].start()

    for k in range(1, count):
        for copy in fetch(k):
            copy.wait()
        acc_a += product(normed_ref, k, a_buf)
        acc_b += product(left_ref, k, b_buf)
    half = cols // 2
    parts = [[acc[:, i * half : (i + 1) * half].astype(BF16) for acc in (acc_a, acc_b)] for i in range(2)]

    def put(ref, pieces):
        ref[:, :half] = pieces[0]
        ref[:, half:] = pieces[1]

    @pl.when(core == 0)
    def _():
        put(keep_ref, parts[0])
        put(send_ref, parts[1])

    @pl.when(core != 0)
    def _():
        put(keep_ref, parts[1])
        put(send_ref, parts[0])

    for copy in copies:
        copy.wait()


def forward(x, gain, cot, weight_a, weight_b):
    rows, width = x.shape
    cols = weight_a.shape[1]
    step = 512
    count = width // step
    half = jax.ShapeDtypeStruct((rows, cols), BF16)
    return pl.pallas_call(
        forward_kernel,
        in_specs=[HBM] * 5,
        out_specs=[VMEM] * 4,
        out_shape=[half] * 2 + [jax.ShapeDtypeStruct((RING, QUARTER, cols), BF16)] * 2,
        scratch_shapes=[pltpu.VMEM((rows, width), BF16), pltpu.VMEM((1, width), F32)]
        + [pltpu.VMEM((count, step, cols), BF16)] * 2
        + [pltpu.VMEM((rows, width), BF16)] * 2
        + [pltpu.SemaphoreType.DMA((3,))]
        + [pltpu.SemaphoreType.DMA((count,))] * 2
        + [pltpu.SemaphoreType.DMA((2 * RING * RING,))],
        compiler_params=params(32),
        cost_estimate=cost(4 * rows * width * cols, 4 * width * cols),
        name="forward",
    )(in_hbm(x), in_hbm(gain), in_hbm(cot), in_hbm(weight_a), in_hbm(weight_b))


def wait_all(copies):
    for copy in copies:
        copy.wait()


def pack_kernel(keep_ref, got_ref, src_ref, dest_ref, mine_ref, other_ref, out_ref, *rest):
    for out, k in zip(rest, (0, 1, 3, 2), strict=True):
        out[0] = mine_ref[k]
        out[1] = other_ref[k]
    spread = slot_onehot(member_index(), src_ref, dest_ref)

    @pl.when(lax.axis_index("section") == 0)
    def _():
        out_ref[...] = jnp.dot(spread, keep_ref[...], preferred_element_type=F32).astype(BF16)

    @pl.when(lax.axis_index("section") != 0)
    def _():
        out_ref[...] = jnp.dot(spread, got_ref[...], preferred_element_type=F32).astype(BF16)


def pack(keep, got, src_len, dest, mine, other):
    width = keep.shape[1]
    _, rows, cols = mine.shape
    outs = pl.pallas_call(
        pack_kernel,
        in_specs=[VMEM] * 6,
        out_specs=[VMEM] * (1 + RING),
        out_shape=[jax.ShapeDtypeStruct((SLOTS, width), BF16)]
        + [jax.ShapeDtypeStruct((2, rows, cols), BF16)] * RING,
        compiler_params=params(),
        cost_estimate=cost(2 * SLOTS * TOK * width, 2 * SLOTS * width),
        name="pack",
    )(keep, got, src_len, dest, mine, other)
    return outs[0], outs[1:]


def attend_kernel(
    keep_ref, got_ref, slots_ref, src_ref, tgt_ref, dest_ref, front_ref, back_ref, own_ref
):
    mask = pair_mask(member_index(), src_ref, tgt_ref, dest_ref)

    @pl.when(lax.axis_index("section") == 0)
    def _():
        own_ref[...] = got_ref[...]

    @pl.when(lax.axis_index("section") != 0)
    def _():
        own_ref[...] = keep_ref[...]

    half = own_ref.shape[1] // 2
    pair = 2 * HEAD_DIM
    low = iota((1, pair), 1) < HEAD_DIM
    nothing = jnp.zeros((), BF16)

    def both(value):
        return jnp.concatenate(
            [jnp.where(low, value, nothing), jnp.where(low, nothing, value)], axis=0
        )

    def nt(left, right):
        return lax.dot_general(left, right, (((1,), (1,)), ((), ())), preferred_element_type=F32)

    def one(score, dweight):
        expo = jnp.where(mask, jnp.exp(score), 0.0)
        weight = expo * (1.0 / jnp.sum(expo, axis=-1, keepdims=True))
        mean = jnp.sum(weight * dweight, axis=-1, keepdims=True)
        return weight.astype(BF16), (weight * (dweight - mean)).astype(BF16)

    def fold(value):
        return jnp.where(low, value[:SLOTS], value[SLOTS:]).astype(BF16)

    for p in range(half // pair):
        first = slice(p * pair, (p + 1) * pair)
        second = slice(half + p * pair, half + (p + 1) * pair)
        query, dout = own_ref[:, first], own_ref[:, second]
        keys, values = both(slots_ref[:, first]), both(slots_ref[:, second])
        score, dweight = nt(query, keys), nt(dout, values)
        weight_0, dscore_0 = one(score[:, :SLOTS], dweight[:, :SLOTS])
        weight_1, dscore_1 = one(score[:, SLOTS:], dweight[:, SLOTS:])
        weight = jnp.concatenate([weight_0, weight_1], axis=1)
        dscore = jnp.concatenate([dscore_0, dscore_1], axis=1)
        front_ref[:, first] = jnp.dot(dscore, keys, preferred_element_type=F32).astype(BF16)
        front_ref[:, second] = jnp.dot(weight, values, preferred_element_type=F32).astype(BF16)
        back_ref[:, first] = fold(tn(dscore, query))
        back_ref[:, second] = fold(tn(weight, dout))


def attend(keep, got, slots, src_len, tgt_len, dest):
    rows, width = keep.shape
    return pl.pallas_call(
        attend_kernel,
        in_specs=[VMEM] * 6,
        out_specs=[VMEM] * 2,
        out_shape=[
            jax.ShapeDtypeStruct((rows, width), BF16),
            jax.ShapeDtypeStruct((SLOTS, width), BF16),
        ],
        scratch_shapes=[pltpu.VMEM((rows, width), BF16)],
        compiler_params=params(),
        cost_estimate=cost(24 * rows * SLOTS * width, 8 * SLOTS * width),
        name="attend",
    )(keep, got, slots, src_len, tgt_len, dest)


def stack_kernel(*refs):
    for p in range(RING):
        for m in range(2):
            refs[RING][m, p] = refs[p][m]


def stacked(pieces):
    _, quarter, cols = pieces[0].shape
    return pl.pallas_call(
        stack_kernel,
        in_specs=[VMEM] * RING,
        out_specs=VMEM,
        out_shape=jax.ShapeDtypeStruct((2, RING, quarter, cols), BF16),
        compiler_params=params(),
        cost_estimate=cost(0, 4 * RING * pieces[0].size),
        name="stack",
    )(*pieces)


def unpack_kernel(back_ref, front_ref, src_ref, dest_ref, keep_ref, send_ref):
    spread = slot_onehot(member_index(), src_ref, dest_ref)
    rows = tn(spread, back_ref[...]).astype(BF16)
    half = rows.shape[1] // 2
    core = lax.axis_index("section")

    @pl.when(core == 0)
    def _():
        keep_ref[:, :half] = rows[:, :half]
        keep_ref[:, half:] = front_ref[:, :half]
        send_ref[:, :half] = front_ref[:, half:]
        send_ref[:, half:] = rows[:, half:]

    @pl.when(core != 0)
    def _():
        keep_ref[:, :half] = front_ref[:, half:]
        keep_ref[:, half:] = rows[:, half:]
        send_ref[:, :half] = rows[:, :half]
        send_ref[:, half:] = front_ref[:, :half]


def unpack(back, front, src_len, dest):
    width = front.shape[1]
    half = jax.ShapeDtypeStruct((TOK, width), BF16)
    return pl.pallas_call(
        unpack_kernel,
        in_specs=[VMEM] * 4,
        out_specs=[VMEM] * 2,
        out_shape=[half, half],
        compiler_params=params(),
        cost_estimate=cost(2 * SLOTS * TOK * width, 4 * SLOTS * width),
        name="unpack",
    )(back, front, src_len, dest)


def join_kernel(keep_ref, got_ref, rows_ref, other_ref):
    width = keep_ref.shape[1]
    half = width // 2
    core = lax.axis_index("section")
    mine = pl.multiple_of(core * half, half)
    theirs = pl.multiple_of((1 - core) * half, half)
    for ref, at in ((keep_ref, mine), (got_ref, theirs)):
        rows_ref[:, pl.ds(at, half)] = ref[:, :half]
        rows_ref[:, pl.ds(pl.multiple_of(width + at, half), half)] = ref[:, half:]
        other_ref[:, pl.ds(at, half)] = ref[:, half:]


def join(keep, got):
    rows, width = keep.shape
    return pl.pallas_call(
        join_kernel,
        in_specs=[VMEM, VMEM],
        out_specs=[VMEM] * 2,
        out_shape=[
            jax.ShapeDtypeStruct((rows, 2 * width), BF16),
            jax.ShapeDtypeStruct((rows, width), BF16),
        ],
        compiler_params=params(),
        cost_estimate=cost(0, 8 * keep.size),
        name="join",
    )(keep, got)


def dnorm_kernel(rows_ref, got_ref, a_hbm, b_hbm, out_hbm, a_buf, b_buf, out_buf, a_sem, b_sem, out_sem):
    count, step, cols = a_buf.shape
    core = lax.axis_index("section")

    def nt(left, right):
        return lax.dot_general(left, right, (((1,), (1,)), ((), ())), preferred_element_type=F32)

    def fetches(hbm, buf, sem):
        return [
            pltpu.make_async_copy(hbm.at[pl.ds(k * step, step), :], buf.at[k], sem.at[k])
            for k in range(count)
        ]

    get_a, get_b = fetches(a_hbm, a_buf, a_sem), fetches(b_hbm, b_buf, b_sem)

    def put(k):
        at = slice(k * step, (k + 1) * step)
        return pltpu.make_async_copy(out_buf.at[:, at], out_hbm.at[:, at], out_sem.at[k])

    @pl.when(core == 0)
    def _():
        for k in range(count):
            get_a[k].start()
            get_b[k].start()
        for k in range(count):
            get_a[k].wait()
            get_b[k].wait()
            block = nt(rows_ref[:, :cols], a_buf[k]) + nt(got_ref[...], b_buf[k])
            out_buf[:, k * step : (k + 1) * step] = block.astype(BF16)
            put(k).start()

    @pl.when(core != 0)
    def _():
        for k in range(count):
            get_a[k].start()
        for k in range(count):
            get_a[k].wait()
            out_buf[:, k * step : (k + 1) * step] = nt(got_ref[...], a_buf[k]).astype(BF16)
            put(k).start()

    for k in range(count):
        put(k).wait()


def dnorm_partial(rows, got, weight_a, weight_b):
    width, cols = weight_a.shape
    step = 512
    count = width // step
    return pl.pallas_call(
        dnorm_kernel,
        in_specs=[VMEM] * 2 + [HBM] * 2,
        out_specs=HBM,
        out_shape=pltpu.HBM((TOK, width), BF16),
        scratch_shapes=[pltpu.VMEM((count, step, cols), BF16)] * 2
        + [pltpu.VMEM((TOK, width), BF16)]
        + [pltpu.SemaphoreType.DMA((count,))] * 3,
        compiler_params=params(24),
        cost_estimate=cost(4 * TOK * width * cols, 4 * width * cols),
        name="dnorm",
    )(rows, got, in_hbm(weight_a), in_hbm(weight_b))


def rms_back_kernel(x_hbm, gain_ref, parts_ref, out_ref, x_ref, sem):
    rows = out_ref.shape[0]
    mine = pl.multiple_of(lax.axis_index("mp") * rows, rows)
    get_x = pltpu.make_async_copy(x_hbm.at[pl.ds(mine, rows), :], x_ref, sem)
    get_x.start()
    dnorm = parts_ref[0].astype(F32)
    for i in range(1, RING):
        dnorm += parts_ref[i].astype(F32)
    get_x.wait()
    xf = x_ref[...].astype(F32)
    scale = lax.rsqrt(jnp.mean(xf * xf, axis=-1, keepdims=True) + EPS)
    upper = gain_ref[...] * dnorm
    inner = jnp.mean(xf * upper, axis=-1, keepdims=True)
    out_ref[...] = (scale * upper - xf * (scale * scale * scale * inner)).astype(BF16)


def rms_back(x, gain, parts):
    rows, width = parts.shape[1:]
    return pl.pallas_call(
        rms_back_kernel,
        in_specs=[HBM] + [VMEM] * 2,
        out_specs=VMEM,
        out_shape=jax.ShapeDtypeStruct((rows, width), BF16),
        scratch_shapes=[pltpu.VMEM((rows, width), BF16), pltpu.SemaphoreType.DMA],
        compiler_params=params(),
        cost_estimate=cost(10 * rows * width, 12 * rows * width),
        name="rms_back",
    )(in_hbm(x), gain, parts)


def place_kernel(*refs):
    pieces, (out_hbm, sems) = refs[:RING], refs[RING:]
    rows = pieces[0].shape[0]
    copies = []
    for i, k in enumerate(ORDER):
        at = pl.multiple_of((lax.axis_index("mp") + k) % RING * rows, rows)
        copies.append(pltpu.make_async_copy(pieces[i], out_hbm.at[pl.ds(at, rows), :], sems.at[i]))
        copies[-1].start()
    for copy in copies:
        copy.wait()


def place(pieces):
    rows, width = pieces[0].shape
    return pl.pallas_call(
        place_kernel,
        in_specs=[ANY] * RING,
        out_specs=HBM,
        out_shape=pltpu.HBM((RING * rows, width), BF16),
        scratch_shapes=[pltpu.SemaphoreType.DMA((RING,))],
        compiler_params=params(),
        cost_estimate=cost(0, 4 * RING * rows * width),
        name="place",
    )(*pieces)


def shift(value, axis, k):
    return lax.ppermute(value, axis, [(i, (i + k) % RING) for i in range(RING)])


def gathered(block, axis):
    left, right = lax.optimization_barrier((shift(block, axis, 1), shift(block, axis, 3)))
    return [block, left, right, shift(left, axis, 1)]


def moved(value, k, along, across=False):
    pairs = []
    for core in range(2):
        for z in range(RING):
            for x in range(RING):
                to = {"z": z, "x": x}
                to[along[core]] = (to[along[core]] + k) % RING
                target = (1 - core if across else core, to["z"], to["x"])
                pairs.append(
                    ((core * RING + z) * RING + x, (target[0] * RING + target[1]) * RING + target[2])
                )
    return lax.ppermute(value, ("section", "z", "x"), pairs)


GATHER, REDUCE = "xz", "zx"


def fetched(own, others):
    return [own] + [moved(others[k], k, GATHER) for k in (1, 3, 2)]


def left_loads(lefts, buf, sems, ks):
    block = buf.shape[-1]
    mine = lax.axis_index("mp")
    loads = [[[] for _ in ks] for _ in range(2)]
    for f in range(2):
        for i, k in enumerate(ks):
            for j, (left, distance) in enumerate(zip(lefts, ORDER, strict=True)):
                at = pl.multiple_of((mine + distance) % RING * QUARTER, QUARTER)
                loads[f][i].append(
                    pltpu.make_async_copy(
                        left.at[f, :, :, pl.ds(k * block, block)],
                        buf.at[f, i, :, pl.ds(at, QUARTER), :],
                        sems.at[f, i, j],
                    )
                )
                loads[f][i][-1].start()
    return loads


def left_scratch(block, count):
    return [
        pltpu.VMEM((2, count, RING, TOK, block), BF16),
        pltpu.SemaphoreType.DMA((2, count, RING)),
    ]


def flat(value):
    return value.reshape(RING * TOK, value.shape[-1])


def far_kernel(*refs):
    lefts, pieces = refs[:RING], refs[RING : 2 * RING]
    top_ref, low_ref, rows_ref, buf, sems = refs[2 * RING :]
    loads = left_loads(lefts, buf, sems, (2,))
    for i, piece in enumerate(pieces):
        rows_ref[i * TOK : (i + 1) * TOK, :] = piece[...]
    half, cols = top_ref.shape[0], top_ref.shape[1] // 2
    for m in range(2):
        at = slice(m * cols, (m + 1) * cols)
        wait_all(loads[m][0])
        block = tn(flat(buf[m, 0]), rows_ref[:, at]).astype(BF16)
        top_ref[:, at] = block[:half]
        low_ref[:, at] = block[half:]


def far_block(lefts, pieces):
    rows, cols = pieces[0].shape
    block = lefts[0].shape[-1] // RING
    half = jax.ShapeDtypeStruct((block // 2, cols), BF16)
    return pl.pallas_call(
        far_kernel,
        in_specs=[HBM] * RING + [VMEM] * RING,
        out_specs=[VMEM] * 3,
        out_shape=[half, half, jax.ShapeDtypeStruct((RING * rows, cols), BF16)],
        scratch_shapes=left_scratch(block, 1),
        compiler_params=params(),
        cost_estimate=cost(2 * RING * rows * block * cols, 8 * RING * rows * cols),
        name="far",
    )(*[in_hbm(left) for left in lefts], *pieces)


def side_kernel(*refs):
    lefts, (rows_ref, from_left, from_right) = refs[:RING], refs[RING : RING + 3]
    rights, to_lefts, buf, sems = refs[RING + 3 : RING + 5], refs[RING + 5 : RING + 7], *refs[RING + 7 :]
    loads = left_loads(lefts, buf, sems, (1, 3))
    half, cols = from_left.shape[0], rights[0].shape[1]
    for m in range(2):
        at = slice(m * cols, (m + 1) * cols)

        def product(i, m=m, at=at):
            wait_all(loads[m][i])
            return tn(flat(buf[m, i]), rows_ref[:, at])

        block = product(0)
        rights[m][:half, :] = (block[:half] + from_left[:, at].astype(F32)).astype(BF16)
        rights[m][half:, :] = block[half:].astype(BF16)
        block = product(1)
        to_lefts[m][:half, :] = block[:half].astype(BF16)
        to_lefts[m][half:, :] = (block[half:] + from_right[:, at].astype(F32)).astype(BF16)


def side_blocks(lefts, rows, from_left, from_right):
    depth, cols = rows.shape
    block = lefts[0].shape[-1] // RING
    shape = jax.ShapeDtypeStruct((block, cols // 2), BF16)
    return pl.pallas_call(
        side_kernel,
        in_specs=[HBM] * RING + [VMEM] * 3,
        out_specs=[VMEM] * 4,
        out_shape=[shape] * 4,
        scratch_shapes=left_scratch(block, 2),
        compiler_params=params(),
        cost_estimate=cost(4 * depth * block * cols, 4 * depth * cols),
        name="side",
    )(*[in_hbm(left) for left in lefts], rows, from_left, from_right)


def middle_kernel(*refs):
    lefts, (rows_ref, own_hbm, other_hbm, out_buf, buf, sems, out_sems) = refs[:RING], refs[RING:]
    loads = left_loads(lefts, buf, sems, (0,))
    cols = out_buf.shape[2]
    puts = []
    for m, out in enumerate((own_hbm, other_hbm)):
        wait_all(loads[m][0])
        at = slice(m * cols, (m + 1) * cols)
        out_buf[m] = tn(flat(buf[m, 0]), rows_ref[:, at]).astype(BF16)
        puts.append(pltpu.make_async_copy(out_buf.at[m], out, out_sems.at[m]))
        puts[-1].start()
    wait_all(puts)


def middle_blocks(lefts, rows):
    depth, cols = rows.shape
    block = lefts[0].shape[-1] // RING
    return pl.pallas_call(
        middle_kernel,
        in_specs=[HBM] * RING + [VMEM],
        out_specs=[HBM] * 2,
        out_shape=[pltpu.HBM((block, cols // 2), BF16)] * 2,
        scratch_shapes=[pltpu.VMEM((2, block, cols // 2), BF16)]
        + left_scratch(block, 1)
        + [pltpu.SemaphoreType.DMA((2,))],
        compiler_params=params(),
        cost_estimate=cost(2 * depth * block * cols, 4 * depth * cols),
        name="middle",
    )(*[in_hbm(left) for left in lefts], rows)


def own_kernel(own_hbm, other_ref, *refs):
    parts, outs, (own_ref, out_buf, own_sem, out_sems) = refs[:4], refs[4:6], refs[6:]
    get = pltpu.make_async_copy(own_hbm, own_ref, own_sem)
    get.start()
    core = lax.axis_index("section")
    chunks = out_sems.shape[1]
    size = out_buf.shape[1] // chunks

    def put(m, c, out):
        at = slice(c * size, (c + 1) * size)
        return pltpu.make_async_copy(out_buf.at[m, at], out.at[at], out_sems.at[m, c])

    def write(m, c):
        @pl.when(core == m)
        def _():
            put(m, c, outs[0]).start()

        @pl.when(core != m)
        def _():
            put(m, c, outs[1]).start()

    for m, base in ((1, other_ref), (0, own_ref)):
        if m == 0:
            get.wait()
        for c in range(chunks):
            at = slice(c * size, (c + 1) * size)
            total_of = base[at].astype(F32) + parts[2 * m][at].astype(F32)
            out_buf[m, at] = total_of + parts[2 * m + 1][at].astype(F32)
            write(m, c)
    for m in range(2):
        for c in range(chunks):
            put(m, c, outs[0]).wait()


def own_blocks(own, other, parts):
    block, cols = own.shape
    return pl.pallas_call(
        own_kernel,
        in_specs=[HBM] + [VMEM] * 5,
        out_specs=[HBM] * 2,
        out_shape=[pltpu.HBM((block, cols), F32)] * 2,
        scratch_shapes=[
            pltpu.VMEM((block, cols), BF16),
            pltpu.VMEM((2, block, cols), F32),
            pltpu.SemaphoreType.DMA,
            pltpu.SemaphoreType.DMA((2, 4)),
        ],
        compiler_params=params(),
        cost_estimate=cost(4 * block * cols, 20 * block * cols),
        name="own",
    )(in_hbm(own), other, *parts)


def per_device(states, gains, proj_a, proj_b, cotangent, src_len, tgt_len, dest):
    weight_a = proj_a[0]
    weight_b = proj_b[0]
    rows = states[0]
    keep, send, mine, other = forward(rows, gains, cotangent, weight_a, weight_b)
    swap = [(0, 1), (1, 0)]
    got = lax.ppermute(send, "section", swap)
    slots, slices = pack(keep, got, src_len, dest, mine, lax.ppermute(other, "section", swap))
    width = slots.shape[1]
    slots = slots.reshape(SEQ_DEV, MAXLEN, width)
    slots = lax.all_to_all(slots, ("z", "x"), split_axis=0, concat_axis=0, tiled=True)
    slots = slots.reshape(SLOTS, width)
    pieces = fetched(slices[0], {1: slices[1], 3: slices[2], 2: slices[3]})
    front, back = attend(keep, got, slots, src_len, tgt_len, dest)
    back, pieces = lax.optimization_barrier((back, pieces))
    lefts = gathered(stacked(pieces), "mp")
    back = back.reshape(SEQ_DEV, MAXLEN, width)
    back = lax.all_to_all(back, ("z", "x"), split_axis=0, concat_axis=0, tiled=True)
    keep, send = unpack(back.reshape(SLOTS, width), front, src_len, dest)
    got = lax.ppermute(send, "section", swap)
    kind, others = join(keep, got)

    rights = fetched(kind, {k: kind for k in (1, 2, 3)})
    others = lax.ppermute(others, "section", swap)
    others, lefts[1], lefts[2] = lax.optimization_barrier((others, lefts[1], lefts[2]))
    partial = dnorm_partial(kind, others, weight_a, weight_b)
    partial, rights[1], rights[2] = lax.optimization_barrier((partial, rights[1], rights[2]))
    parts = lax.all_to_all(
        partial.reshape(RING, TOK // RING, -1), "mp", split_axis=0, concat_axis=0, tiled=True
    )
    top, low, stack = far_block(lefts, rights)
    from_left, from_right = moved(top, 1, REDUCE), moved(low, 3, REDUCE)
    parts, _, _ = lax.optimization_barrier((parts, from_left, from_right))
    right, right_other, left, left_other = side_blocks(lefts, stack, from_left, from_right)
    own, own_other = middle_blocks(lefts, stack)
    own_other, _ = lax.optimization_barrier((own_other, right))
    sums = [
        moved(right, 1, REDUCE),
        moved(left, 3, REDUCE),
        moved(right_other, 1, REDUCE, True),
        moved(left_other, 3, REDUCE, True),
    ]
    quarter = rms_back(rows, gains, parts)
    grad_states = place(gathered(quarter, "mp"))
    grad_a, grad_b = own_blocks(own, lax.ppermute(own_other, "section", swap), sums)
    return (grad_states[None], grad_a[None], grad_b[None])


def solution(mesh):
    split = jax.sharding.Mesh(mesh.devices.reshape(2, RING, RING, RING), ("section", "z", "x", "mp"))
    dp = ("z", "x")
    return jax.shard_map(
        per_device,
        mesh=split,
        in_specs=(
            P("section", dp, None),
            P("section", None),
            P("section", None, "mp"),
            P("section", None, "mp"),
            P(dp, None),
            P(),
            P(),
            P(),
        ),
        out_specs=(P("section", dp, None), P("section", dp, "mp"), P("section", dp, "mp")),
        check_vma=False,
    )
```
